32 devices in a mesh: dp: 8 (over y, x, core), mp: 4 (over z).
Axes of the slice: x: 2, y: 2, z: 4, core: 2. Of those that a mesh axis runs over, the one named last changes fastest.
Arguments:
- layer_input: float32 [8192, 512], P('dp'), may hold values from -6 to 6
- encoder_memory: float32 [8192, 512], P('dp', 'mp'), may hold values from -6 to 6
- output_grad: float32 [8192, 512], P('dp'), may hold values from -6 to 6
- target_lengths: int32 [8, 32], P('dp'), may hold values from 1 to 64, 1024 in all within a row
- memory_lengths: int32 [8, 32], P('dp'), may hold values from 1 to 64, 1024 in all within a row
- source_slots: int32 [8192], P('dp'), may hold values from 0 to 1407, as said below
- pair_counts: int32 [8, 8], replicated, may hold values from 112 to 176, as said below
- attend_input: float32 [6, 512, 512], P(None, 'dp', 'mp'), may hold values from -0.25 to 0.25
- attend_output: float32 [2, 512, 512], P(None, 'mp', 'dp'), may hold values from -1.5 to 1.5
- expand_weight: float32 [512, 2048], P('dp', 'mp'), may hold values from -0.25 to 0.25
- reduce_weight: float32 [2048, 512], P('mp', 'dp'), may hold values from -0.125 to 0.125
- norm_vectors: float32 [7, 512], P(None, 'dp')
- expand_bias: float32 [2048], P(('mp', 'dp')), may hold values from -1.75 to 1.75
- attend_input_first: float32 [6, 512, 512], P(None, 'dp', 'mp'), may hold values from -0.0029296875 to 0.0029296875
- attend_input_second: float32 [6, 512, 512], P(None, 'dp', 'mp'), may hold values from 2.3809886e-07 to 9.5239545e-07
- attend_output_first: float32 [2, 512, 512], P(None, 'mp', 'dp'), may hold values from -0.0029296875 to 0.0029296875
- attend_output_second: float32 [2, 512, 512], P(None, 'mp', 'dp'), may hold values from 2.3809886e-07 to 9.5239545e-07
- expand_weight_first: float32 [512, 2048], P('dp', 'mp'), may hold values from -0.0029296875 to 0.0029296875
- expand_weight_second: float32 [512, 2048], P('dp', 'mp'), may hold values from 2.3809886e-07 to 9.5239545e-07
- reduce_weight_first: float32 [2048, 512], P('mp', 'dp'), may hold values from -0.0029296875 to 0.0029296875
- reduce_weight_second: float32 [2048, 512], P('mp', 'dp'), may hold values from 2.3809886e-07 to 9.5239545e-07
- norm_vectors_first: float32 [7, 512], P(None, 'dp'), may hold values from -0.0029296875 to 0.0029296875
- norm_vectors_second: float32 [7, 512], P(None, 'dp'), may hold values from 2.3809886e-07 to 9.5239545e-07
- expand_bias_first: float32 [2048], P(('mp', 'dp')), may hold values from -0.0029296875 to 0.0029296875
- expand_bias_second: float32 [2048], P(('mp', 'dp')), may hold values from 2.3809886e-07 to 9.5239545e-07
Outputs:
- layer_output: float32 [8192, 512], P('dp')
- input_grad: float32 [8192, 512], P('dp')
- memory_grad: float32 [8192, 512], P('dp', 'mp')
- grad_norm: float32 [1], replicated
- new_attend_input: float32 [6, 512, 512], P(None, 'dp', 'mp')
- new_attend_output: float32 [2, 512, 512], P(None, 'mp', 'dp')
- new_expand_weight: float32 [512, 2048], P('dp', 'mp')
- new_reduce_weight: float32 [2048, 512], P('mp', 'dp')
- new_norm_vectors: float32 [7, 512], P(None, 'dp')
- new_expand_bias: float32 [2048], P(('mp', 'dp'))
- attend_input_copy: bfloat16 [6, 512, 512], P(None, 'dp', 'mp')
- attend_output_copy: bfloat16 [2, 512, 512], P(None, 'mp', 'dp')
- expand_weight_copy: bfloat16 [512, 2048], P('dp', 'mp')
- reduce_weight_copy: bfloat16 [2048, 512], P('mp', 'dp')
- first_attend_input: float32 [6, 512, 512], P(None, 'dp', 'mp')
- second_attend_input: float32 [6, 512, 512], P(None, 'dp', 'mp')
- first_attend_output: float32 [2, 512, 512], P(None, 'mp', 'dp')
- second_attend_output: float32 [2, 512, 512], P(None, 'mp', 'dp')
- first_expand_weight: float32 [512, 2048], P('dp', 'mp')
- second_expand_weight: float32 [512, 2048], P('dp', 'mp')
- first_reduce_weight: float32 [2048, 512], P('mp', 'dp')
- second_reduce_weight: float32 [2048, 512], P('mp', 'dp')
- first_norm_vectors: float32 [7, 512], P(None, 'dp')
- second_norm_vectors: float32 [7, 512], P(None, 'dp')
- first_expand_bias: float32 [2048], P(('mp', 'dp'))
- second_expand_bias: float32 [2048], P(('mp', 'dp'))
- matrix_norms: float32 [2, 10], replicated
The draws below stay inside these ranges and needn't reach their ends.
Inputs may be any that keep to these rules, and one draw needn't show every extreme that they name: `target_lengths`: each row's 32 lengths sum to 1024. `memory_lengths`: each row's 32 lengths sum to 1024. Every row and every column sums to 1024; device a's rows for device j are a run of its rows that starts at the sum of pair_counts[a, i] over i < j. `source_slots`: on device j each value a * 176 + s with s < pair_counts[a, j] appears exactly once.
All inputs are finite; a program needn't handle non-finite values.
Results may differ from the reference program's by a relative error of at most 0.001.
Values sent between devices are 32-bit elements; how exact they have to be, the bound alone decides.
No kernel may reach another device: no remote copies, remote signals or barrier semaphores. Data moves between devices by JAX's collectives and lax.ppermute only.
A program may use at most 192 MiB of HBM per device.

```python
import math
import jax
import jax.numpy as jnp
import numpy as np
from jax import lax

D = 512
H = 8
HD = 64
FF = 2048
TOK_DEV = 1024
SEG_MOST = 64
STEP_NUM = 6
NSEG = 32
EXTRA = 64
BASE = 112
CAP = 176
TOKENS = 8192
N_DP = 8


def route_table(key):
    shifts = jax.random.permutation(jax.random.fold_in(key, 7), N_DP)[:N_DP // 4]
    source = jnp.arange(N_DP, dtype=jnp.int32)[:, None]
    target = jnp.arange(N_DP, dtype=jnp.int32)[None, :]
    offset_gap = (target - source) % N_DP
    shift_hits = jnp.sum((offset_gap[:, :, None] == shifts[None, None, :]).astype(jnp.int32), axis=2)
    return BASE + EXTRA * shift_hits


def draw_pair_counts(key, part):
    return route_table(key).astype(jnp.int32)


def draw_source_slots(key, part):
    counts_table = route_table(key)
    column_end = jnp.cumsum(counts_table, axis=0)
    column_start = column_end - counts_table
    places = jnp.arange(TOK_DEV, dtype=jnp.int32)
    anchor = jnp.sum((column_end.T[:, :, None] <= places[None, None, :]).astype(jnp.int32), axis=1)
    start_of = jnp.take_along_axis(column_start.T, anchor, axis=1)
    slot_codes = anchor * CAP + places[None, :] - start_of
    row_keys = jax.random.split(jax.random.fold_in(key, 9), N_DP)
    orders = jax.vmap(lambda sub_key: jax.random.permutation(sub_key, TOK_DEV))(row_keys)
    shuffled = jnp.take_along_axis(slot_codes, orders, axis=1)
    return shuffled.reshape(N_DP * TOK_DEV).astype(jnp.int32)


def draw_norm_vectors(key, part):
    normal_draw = jax.random.normal(key, (7, D), jnp.float32)
    row_ids = jnp.arange(7, dtype=jnp.int32)[:, None]
    return jnp.where(row_ids < 3, 1.0 + 0.1 * normal_draw, 0.3 * normal_draw)


def levels(own_key, shape, cuts, low, high):
    gain, own = 1.0, jax.random.fold_in(own_key, 6)
    for dim, shards_of in cuts:
        draws = jnp.exp(jax.random.uniform(jax.random.fold_in(own, dim), (shards_of,), jnp.float32, low / len(cuts), high / len(cuts)))
        gain = gain * jnp.repeat(draws, shape[dim] // shards_of).reshape([-1 if axis == dim else 1 for axis in range(len(shape))])
    return gain


def split_up(count, total, bound, lean):
    loads = [(1 << 20) // math.isqrt(grade ** lean) + 1 for grade in range(2, count + 1)]
    surplus, counts = total - bound - (count - 1), [1] * (count - 1)
    while surplus > 0:
        candidates = [i for i in range(count - 1) if counts[i] < bound]
        mass, remaining = sum([loads[i] for i in candidates]), surplus
        for i in candidates:
            extra = min(bound - counts[i], max(1, remaining * loads[i] // mass), surplus)
            counts[i] = counts[i] + extra
            surplus = surplus - extra
    return np.array([bound] + counts)


def ragged_sizes(rng, count, total, reach, slope):
    if count == 2:
        one = jax.random.randint(rng, (), max(1, total - reach), min(reach, total - 1) + 1)
        return jnp.stack([one, total - one])
    tallies = jnp.asarray(split_up(count, total, reach, slope), jnp.int32)
    pairs = (count - 1) // 2
    giver, taker = tallies[1:1 + 2 * pairs:2], tallies[2:2 + 2 * pairs:2]
    slack = jnp.minimum(giver - 1, reach - taker)
    passed = jax.random.randint(jax.random.fold_in(rng, 1), (pairs,), 0, 1 << 20) % (slack + 1)
    tallies = tallies.at[1:1 + 2 * pairs:2].set(giver - passed).at[2:2 + 2 * pairs:2].set(taker + passed)
    return tallies[jax.random.permutation(jax.random.fold_in(rng, 2), count)]


def normal_values(own_key, shape, deviation, limit, shards=(), kind=jnp.bfloat16):
    loudness = levels(own_key, shape, shards, -0.22, 0.18) if shards else 1.0
    entries = jax.random.normal(own_key, shape, jnp.float32) * deviation * loudness
    return jnp.minimum(jnp.maximum(entries, -limit), limit).astype(kind)


def setup_inputs(seed: int = 0) -> dict:
    splits = jax.random.split(jax.random.key(seed), 26)
    return {
        "layer_input": normal_values(splits[0], (TOKENS, D), 1.0, 6.0, ((0, 8),), jnp.float32),
        "encoder_memory": normal_values(splits[1], (TOKENS, D), 1.0, 6.0, ((0, 8), (1, 4)), jnp.float32),
        "output_grad": normal_values(splits[2], (TOKENS, D), 1.0, 6.0, ((0, 8),), jnp.float32),
        "target_lengths": jax.vmap(lambda own: ragged_sizes(own, NSEG, TOK_DEV, SEG_MOST, 1))(jax.random.split(splits[3], N_DP)).reshape((N_DP, NSEG)).astype(jnp.int32),
        "memory_lengths": jax.vmap(lambda own: ragged_sizes(own, NSEG, TOK_DEV, SEG_MOST, 1))(jax.random.split(splits[4], N_DP)).reshape((N_DP, NSEG)).astype(jnp.int32),
        "source_slots": draw_source_slots(jax.random.fold_in(splits[25], 71), 0),
        "pair_counts": draw_pair_counts(jax.random.fold_in(splits[25], 71), 0),
        "attend_input": normal_values(splits[7], (6, D, H * HD), D ** -0.5, 0.25, ((1, 8), (2, 4)), jnp.float32),
        "attend_output": normal_values(splits[8], (2, H * HD, D), (D // 32) ** -0.5, 1.5, ((1, 4), (2, 8)), jnp.float32),
        "expand_weight": normal_values(splits[9], (D, FF), D ** -0.5, 0.25, ((0, 8), (1, 4)), jnp.float32),
        "reduce_weight": normal_values(splits[10], (FF, D), FF ** -0.5, 0.125, ((0, 4), (1, 8)), jnp.float32),
        "norm_vectors": draw_norm_vectors(jax.random.fold_in(splits[25], 71), 0),
        "expand_bias": normal_values(splits[12], (FF,), 0.3, 1.75, ((0, 32),), jnp.float32),
        "attend_input_first": normal_values(splits[13], (6, D, H * HD), ((8 * D * H * HD + 2 * D * FF + FF + 7 * D) ** -0.5), 0.0029296875, ((1, 8), (2, 4)), jnp.float32),
        "attend_input_second": jnp.clip(jnp.exp(math.log(9.523954531687195e-07) - 1.3862944 * jax.random.uniform(splits[14], (6, D, H * HD), jnp.float32) ** levels(splits[14], (6, D, H * HD), ((1, 8), (2, 4)), -0.2, 0.2)), 2.3809886329217989e-07, 9.523954531687195e-07),
        "attend_output_first": normal_values(splits[15], (2, H * HD, D), ((8 * D * H * HD + 2 * D * FF + FF + 7 * D) ** -0.5), 0.0029296875, ((1, 4), (2, 8)), jnp.float32),
        "attend_output_second": jnp.clip(jnp.exp(math.log(9.523954531687195e-07) - 1.3862944 * jax.random.uniform(splits[16], (2, H * HD, D), jnp.float32) ** levels(splits[16], (2, H * HD, D), ((1, 4), (2, 8)), -0.2, 0.2)), 2.3809886329217989e-07, 9.523954531687195e-07),
        "expand_weight_first": normal_values(splits[17], (D, FF), ((8 * D * H * HD + 2 * D * FF + FF + 7 * D) ** -0.5), 0.0029296875, ((0, 8), (1, 4)), jnp.float32),
        "expand_weight_second": jnp.clip(jnp.exp(math.log(9.523954531687195e-07) - 1.3862944 * jax.random.uniform(splits[18], (D, FF), jnp.float32) ** levels(splits[18], (D, FF), ((0, 8), (1, 4)), -0.2, 0.2)), 2.3809886329217989e-07, 9.523954531687195e-07),
        "reduce_weight_first": normal_values(splits[19], (FF, D), ((8 * D * H * HD + 2 * D * FF + FF + 7 * D) ** -0.5), 0.0029296875, ((0, 4), (1, 8)), jnp.float32),
        "reduce_weight_second": jnp.clip(jnp.exp(math.log(9.523954531687195e-07) - 1.3862944 * jax.random.uniform(splits[20], (FF, D), jnp.float32) ** levels(splits[20], (FF, D), ((0, 4), (1, 8)), -0.2, 0.2)), 2.3809886329217989e-07, 9.523954531687195e-07),
        "norm_vectors_first": normal_values(splits[21], (7, D), ((8 * D * H * HD + 2 * D * FF + FF + 7 * D) ** -0.5), 0.0029296875, ((1, 8),), jnp.float32),
        "norm_vectors_second": jnp.clip(jnp.exp(math.log(9.523954531687195e-07) - 1.3862944 * jax.random.uniform(splits[22], (7, D), jnp.float32) ** levels(splits[22], (7, D), ((1, 8),), -0.2, 0.2)), 2.3809886329217989e-07, 9.523954531687195e-07),
        "expand_bias_first": normal_values(splits[23], (FF,), ((8 * D * H * HD + 2 * D * FF + FF + 7 * D) ** -0.5), 0.0029296875, ((0, 32),), jnp.float32),
        "expand_bias_second": jnp.clip(jnp.exp(math.log(9.523954531687195e-07) - 1.3862944 * jax.random.uniform(splits[24], (FF,), jnp.float32) ** levels(splits[24], (FF,), ((0, 32),), -0.2, 0.2)), 2.3809886329217989e-07, 9.523954531687195e-07),
    }


highest = lax.Precision.HIGHEST
norm_eps = 1e-05
adam_eps = 1e-06
first_decay = 0.5
second_decay = 0.5
matrix_decay = 0.01
peak_rate = 0.6
warm_steps = 8.0
clip_norm = 1.0
neg_large = -1e+30

def matmul(left_side, right_side):
    return jnp.dot(left_side, right_side, precision=highest, preferred_element_type=jnp.float32)

def segment_ids(lengths, length_total):
    segment_ends = jnp.cumsum(lengths)
    places = jnp.arange(length_total, dtype=jnp.int32)
    return lax.optimization_barrier(jnp.sum((segment_ends[:, None] <= places[None, :]).astype(jnp.int32), axis=0))

def layer_norm(values, gain_row, shift_row):
    centre_mean = lax.optimization_barrier(jnp.mean(values, axis=-1, keepdims=True))
    centred = values - centre_mean
    variance = lax.optimization_barrier(jnp.mean(centred * centred, axis=-1, keepdims=True))
    return centred * lax.rsqrt(variance + norm_eps) * gain_row + shift_row

def apply_gelu(values):
    return 0.5 * values * (1.0 + jnp.tanh(0.7978845608028654 * (values + 0.044715 * values * values * values)))

def attention(queries, keys_in, values_in, query_seg, key_seg):
    scores = jnp.einsum('qhe,khe->hqk', queries, keys_in, precision=highest) * HD ** (-0.5)
    allowed = query_seg[:, None] == key_seg[None, :]
    scores = jnp.where(allowed[None], scores, neg_large)
    weights = jax.nn.softmax(scores, axis=-1)
    return jnp.einsum('hqk,khe->qhe', weights, values_in, precision=highest)

def row_layer(row_input, row_memory, tok_seg, mem_seg, attend_input, attend_output, expand_weight, reduce_weight, norm_vectors, expand_bias):
    tok_rows = row_input.shape[0]

    def project(source, which_part):
        return matmul(source, attend_input[which_part]).reshape(source.shape[0], H, HD)
    self_heads = attention(project(row_input, 0), project(row_input, 1), project(row_input, 2), tok_seg, tok_seg)
    self_mix = matmul(self_heads.reshape(tok_rows, H * HD), attend_output[0])
    first_norm = layer_norm(row_input + self_mix, norm_vectors[0], norm_vectors[3])
    cross_heads = attention(project(first_norm, 3), project(row_memory, 4), project(row_memory, 5), tok_seg, mem_seg)
    cross_mix = matmul(cross_heads.reshape(tok_rows, H * HD), attend_output[1])
    second_norm = layer_norm(first_norm + cross_mix, norm_vectors[1], norm_vectors[4])
    expanded = apply_gelu(matmul(second_norm, expand_weight) + expand_bias)
    reduced = matmul(expanded, reduce_weight) + norm_vectors[6]
    return layer_norm(second_norm + reduced, norm_vectors[2], norm_vectors[5])

def part_squares(arrays, divisor):
    return jnp.concatenate([lax.optimization_barrier(jnp.sum(arrays[0] * arrays[0], axis=(1, 2))), lax.optimization_barrier(jnp.sum(arrays[1] * arrays[1], axis=(1, 2))), jnp.sum(arrays[2] * arrays[2])[None], jnp.sum(arrays[3] * arrays[3])[None], lax.optimization_barrier(jnp.sum(arrays[4] * arrays[4], axis=1)) / divisor, jnp.sum(arrays[5] * arrays[5])[None]])

def spread_parts(per_part):
    return (per_part[0:6][:, None, None], per_part[6:8][:, None, None], per_part[8], per_part[9], per_part[10:17][:, None], per_part[17])

def reference(layer_input, encoder_memory, output_grad, target_lengths, memory_lengths, source_slots, pair_counts, attend_input, attend_output, expand_weight, reduce_weight, norm_vectors, expand_bias, attend_input_first, attend_input_second, attend_output_first, attend_output_second, expand_weight_first, expand_weight_second, reduce_weight_first, reduce_weight_second, norm_vectors_first, norm_vectors_second, expand_bias_first, expand_bias_second):
    tok_segs = jax.vmap(lambda lengths: segment_ids(lengths, TOK_DEV))(target_lengths)
    mem_segs = jax.vmap(lambda lengths: segment_ids(lengths, TOK_DEV))(memory_lengths)
    offsets = jnp.cumsum(pair_counts, axis=1) - pair_counts
    anchor = source_slots // CAP
    within = source_slots % CAP
    target_dev = jnp.arange(TOKENS, dtype=jnp.int32) // TOK_DEV
    source_index = (anchor * TOK_DEV + offsets[anchor, target_dev] + within).astype(jnp.int32)

    def forward(layer_in, memory_in, attend_in, attend_out, expand_in, reduce_in, vectors_in, bias_in):
        routed = memory_in[source_index]

        def one_row(pieces):
            return row_layer(pieces[0], pieces[1], pieces[2], pieces[3], attend_in, attend_out, expand_in, reduce_in, vectors_in, bias_in)
        outputs = lax.map(jax.checkpoint(one_row), (layer_in.reshape(N_DP, TOK_DEV, D), routed.reshape(N_DP, TOK_DEV, D), tok_segs, mem_segs))
        return outputs.reshape(TOKENS, D)
    primals = (layer_input, encoder_memory, attend_input, attend_output, expand_weight, reduce_weight, norm_vectors, expand_bias)
    layer_output, pullback = jax.vjp(forward, *primals)
    grads = pullback(output_grad)
    input_grad = grads[0]
    memory_grad = grads[1]
    weight_grads = grads[2:]
    weights = primals[2:]
    firsts = (attend_input_first, attend_output_first, expand_weight_first, reduce_weight_first, norm_vectors_first, expand_bias_first)
    seconds = (attend_input_second, attend_output_second, expand_weight_second, reduce_weight_second, norm_vectors_second, expand_bias_second)
    grad_norm = jnp.sqrt(jnp.sum(part_squares(weight_grads, 1.0)))
    clip_factor = jnp.minimum(1.0, clip_norm / grad_norm)
    steps_done = jnp.float32(STEP_NUM)
    step_rate = peak_rate * jnp.minimum(steps_done / warm_steps, jnp.sqrt(warm_steps / steps_done))
    first_fix = 1.0 - first_decay ** steps_done
    second_fix = 1.0 - second_decay ** steps_done
    new_firsts = []
    new_seconds = []
    updates = []
    for number in range(6):
        clipped = weight_grads[number] * clip_factor
        moment_one = first_decay * firsts[number] + (1.0 - first_decay) * clipped
        moment_two = second_decay * seconds[number] + (1.0 - second_decay) * clipped * clipped
        decay_rate = matrix_decay if number < 4 else 0.0
        updates.append(moment_one / first_fix / (jnp.sqrt(moment_two / second_fix) + adam_eps) + decay_rate * weights[number])
        new_firsts.append(moment_one)
        new_seconds.append(moment_two)
    weight_square = part_squares(weights, 1.0)
    update_square = part_squares(updates, 1.0)
    ratios = spread_parts(jnp.sqrt(weight_square) / jnp.sqrt(update_square))
    new_weights = [weights[number] - step_rate * ratios[number] * updates[number] for number in range(6)]
    matrix_norms = jnp.stack([jnp.sqrt(weight_square[:10]), jnp.sqrt(update_square[:10])])
    return (layer_output, input_grad, memory_grad, grad_norm[None], new_weights[0], new_weights[1], new_weights[2], new_weights[3], new_weights[4], new_weights[5], new_weights[0].astype(jnp.bfloat16), new_weights[1].astype(jnp.bfloat16), new_weights[2].astype(jnp.bfloat16), new_weights[3].astype(jnp.bfloat16), new_firsts[0], new_seconds[0], new_firsts[1], new_seconds[1], new_firsts[2], new_seconds[2], new_firsts[3], new_seconds[3], new_firsts[4], new_seconds[4], new_firsts[5], new_seconds[5], matrix_norms)
```

```python
import functools

import jax
import jax.numpy as jnp
from jax import lax
from jax.experimental import pallas as pl
from jax.experimental.pallas import tpu as pltpu
from jax.sharding import PartitionSpec as P

HD = 64
STEP_NUM = 6

norm_eps = 1e-05
adam_eps = 1e-06
first_decay = 0.5
second_decay = 0.5
matrix_decay = 0.01
peak_rate = 0.6
warm_steps = 8.0
clip_norm = 1.0

bf16 = jnp.bfloat16
f32 = jnp.float32
neg_large = -1e30
q_rows = 128
key_rows = 256
pair_lanes = 128


def split_two(values):
    high = values.astype(bf16)
    return high, (values - high.astype(f32)).astype(bf16)


def dot_nn(left_side, right_side):
    return lax.dot_general(left_side, right_side, (((1,), (0,)), ((), ())), preferred_element_type=f32)


def dot_nt(left_side, right_side):
    return lax.dot_general(left_side, right_side, (((1,), (1,)), ((), ())), preferred_element_type=f32)


def dot_tn(left_side, right_side):
    return lax.dot_general(left_side, right_side, (((0,), (0,)), ((), ())), preferred_element_type=f32)


def three(dot, left_pair, right_pair):
    return (
        dot(left_pair[0], right_pair[0])
        + dot(left_pair[1], right_pair[0])
        + dot(left_pair[0], right_pair[1])
    )


def stack_heads(tile, low_half):
    return jnp.concatenate([jnp.where(low_half, tile, 0.0), jnp.where(low_half, 0.0, tile)], axis=0)


def merge_heads(stacked, low_half):
    return jnp.where(low_half, stacked[:q_rows], stacked[q_rows:])


def split_rows(source_ref, high_ref, low_ref):
    rows = source_ref.shape[0]

    def one(step, carry):
        at = pl.ds(pl.multiple_of(step * q_rows, q_rows), q_rows)
        high, low = split_two(source_ref[at, :])
        high_ref[at, :] = high
        low_ref[at, :] = low
        return carry

    lax.fori_loop(0, rows // q_rows, one, 0)
    if high_ref.shape[0] > rows:
        pad = jnp.zeros((high_ref.shape[0] - rows, high_ref.shape[1]), bf16)
        high_ref[rows:, :] = pad
        low_ref[rows:, :] = pad


def attend_kernel(
    unroll, scale, block_low, block_count,
    q_ref, k_ref, v_ref, low_ref, high_ref,
    o_ref, total_ref,
    kh_ref, kl_ref, vh_ref, vl_ref,
):
    rows, width = q_ref.shape
    split_rows(k_ref, kh_ref, kl_ref)
    split_rows(v_ref, vh_ref, vl_ref)
    groups = width // pair_lanes // unroll
    lanes = lax.broadcasted_iota(jnp.int32, (q_rows, pair_lanes), 1)
    low_half = lanes < pair_lanes // 2
    key_iota = lax.broadcasted_iota(jnp.int32, (2 * q_rows, key_rows), 1)

    def block(index, carry):
        at = pl.ds(pl.multiple_of(index * q_rows, q_rows), q_rows)
        first = low_ref[at, :]
        last = high_ref[at, :]
        first = jnp.concatenate([first, first], axis=0)
        last = jnp.concatenate([last, last], axis=0)
        total_tile = jnp.zeros((q_rows, pair_lanes), f32)
        for group in range(groups):
            columns = [
                pl.ds((group * unroll + u) * pair_lanes, pair_lanes) for u in range(unroll)
            ]
            queries = [
                split_two(stack_heads(q_ref[at, c] * scale, low_half)) for c in columns
            ]

            def chunk(step, state):
                start = pl.multiple_of(block_low[index] + step * key_rows, 16)
                here = pl.ds(start, key_rows)
                places = key_iota + start
                allowed = jnp.logical_and(places >= first, places < last)
                out = []
                for u in range(unroll):
                    top, total, held = state[u]
                    scores = three(
                        dot_nt, queries[u], (kh_ref[here, columns[u]], kl_ref[here, columns[u]])
                    )
                    scores = jnp.where(allowed, scores, neg_large)
                    new_top = jnp.maximum(top, jnp.max(scores, axis=1, keepdims=True))
                    weights = jnp.exp(scores - new_top)
                    shrink = jnp.exp(top - new_top)
                    total = total * shrink + jnp.sum(weights, axis=1, keepdims=True)
                    held = held * shrink + three(
                        dot_nn, split_two(weights), (vh_ref[here, columns[u]], vl_ref[here, columns[u]])
                    )
                    out.append((new_top, total, held))
                return tuple(out)

            start_state = tuple(
                (
                    jnp.full((2 * q_rows, 1), neg_large, f32),
                    jnp.zeros((2 * q_rows, 1), f32),
                    jnp.zeros((2 * q_rows, pair_lanes), f32),
                )
                for _ in range(unroll)
            )
            state = lax.fori_loop(0, block_count[index], chunk, start_state)
            for u in range(unroll):
                top, total, held = state[u]
                pair = group * unroll + u
                o_ref[at, columns[u]] = merge_heads(held / total, low_half)
                logs = top + jnp.log(total)
                total_tile = jnp.where(lanes == 2 * pair, logs[:q_rows], total_tile)
                total_tile = jnp.where(lanes == 2 * pair + 1, logs[q_rows:], total_tile)
        total_ref[at, :] = total_tile
        return carry

    lax.fori_loop(0, rows // q_rows, block, 0)


def attend_back_kernel(
    unroll, scale, block_low, block_count,
    q_ref, k_ref, v_ref, o_ref, g_ref, total_ref, low_ref, high_ref,
    dq_ref, dk_ref, dv_ref,
    kh_ref, kl_ref, vh_ref, vl_ref, dk_sum, dv_sum,
):
    rows, width = q_ref.shape
    split_rows(k_ref, kh_ref, kl_ref)
    split_rows(v_ref, vh_ref, vl_ref)
    dk_sum[...] = jnp.zeros_like(dk_sum)
    dv_sum[...] = jnp.zeros_like(dv_sum)
    groups = width // pair_lanes // unroll
    lanes = lax.broadcasted_iota(jnp.int32, (q_rows, pair_lanes), 1)
    low_half = lanes < pair_lanes // 2
    key_iota = lax.broadcasted_iota(jnp.int32, (2 * q_rows, key_rows), 1)

    def block(index, carry):
        at = pl.ds(pl.multiple_of(index * q_rows, q_rows), q_rows)
        first = low_ref[at, :]
        last = high_ref[at, :]
        first = jnp.concatenate([first, first], axis=0)
        last = jnp.concatenate([last, last], axis=0)
        total_tile = total_ref[at, :]
        for group in range(groups):
            columns = [
                pl.ds((group * unroll + u) * pair_lanes, pair_lanes) for u in range(unroll)
            ]
            queries, grads, logs, dots = [], [], [], []
            for u in range(unroll):
                pair = group * unroll + u
                queries.append(split_two(stack_heads(q_ref[at, columns[u]] * scale, low_half)))
                grad = stack_heads(g_ref[at, columns[u]], low_half)
                grads.append(split_two(grad))
                out = o_ref[at, columns[u]]
                dots.append(
                    jnp.sum(grad * jnp.concatenate([out, out], axis=0), axis=1, keepdims=True)
                )
                logs.append(
                    jnp.concatenate(
                        [
                            jnp.sum(jnp.where(lanes == 2 * pair, total_tile, 0.0), axis=1, keepdims=True),
                            jnp.sum(jnp.where(lanes == 2 * pair + 1, total_tile, 0.0), axis=1, keepdims=True),
                        ],
                        axis=0,
                    )
                )

            def chunk(step, state):
                start = pl.multiple_of(block_low[index] + step * key_rows, 16)
                here = pl.ds(start, key_rows)
                places = key_iota + start
                allowed = jnp.logical_and(places >= first, places < last)
                out = []
                for u in range(unroll):
                    keys = (kh_ref[here, columns[u]], kl_ref[here, columns[u]])
                    values = (vh_ref[here, columns[u]], vl_ref[here, columns[u]])
                    scores = three(dot_nt, queries[u], keys)
                    weights = jnp.where(allowed, jnp.exp(scores - logs[u]), 0.0)
                    grad_weights = three(dot_nt, grads[u], values)
                    grad_scores = split_two(weights * (grad_weights - dots[u]))
                    out.append(state[u] + three(dot_nn, grad_scores, keys))
                    dk_sum[here, columns[u]] += three(dot_tn, grad_scores, queries[u])
                    dv_sum[here, columns[u]] += three(dot_tn, split_two(weights), grads[u])
                return tuple(out)

            state = lax.fori_loop(
                0,
                block_count[index],
                chunk,
                tuple(jnp.zeros((2 * q_rows, pair_lanes), f32) for _ in range(unroll)),
            )
            for u in range(unroll):
                dq_ref[at, columns[u]] = merge_heads(state[u], low_half) * scale
        return carry

    lax.fori_loop(0, rows // q_rows, block, 0)
    dk_ref[...] = dk_sum[:rows, :]
    dv_ref[...] = dv_sum[:rows, :]


VM = functools.partial(pl.BlockSpec, memory_space=pltpu.VMEM)
SM = functools.partial(pl.BlockSpec, memory_space=pltpu.SMEM)


def attend(queries, keys_in, values_in, ranges, head_size, unroll=4):
    block_low, block_count, low, high = ranges
    rows, width = queries.shape
    pad_rows = keys_in.shape[0] + key_rows
    return pl.pallas_call(
        functools.partial(attend_kernel, unroll, head_size ** -0.5),
        out_shape=(
            jax.ShapeDtypeStruct((rows, width), f32),
            jax.ShapeDtypeStruct((rows, pair_lanes), f32),
        ),
        in_specs=[SM(), SM()] + [VM()] * 5,
        out_specs=(VM(), VM()),
        scratch_shapes=[pltpu.VMEM((pad_rows, width), bf16)] * 4,
        compiler_params=pltpu.CompilerParams(vmem_limit_bytes=48 << 20),
        cost_estimate=pl.CostEstimate(flops=12 * rows * key_rows * width, bytes_accessed=16 * rows * width, transcendentals=rows * key_rows * 8),
        name="attend",
    )(block_low, block_count, queries, keys_in, values_in, low, high)


def attend_back(queries, keys_in, values_in, outputs, totals, grad_out, ranges, head_size, unroll=4):
    block_low, block_count, low, high = ranges
    rows, width = queries.shape
    pad_rows = keys_in.shape[0] + key_rows
    return pl.pallas_call(
        functools.partial(attend_back_kernel, unroll, head_size ** -0.5),
        out_shape=tuple(jax.ShapeDtypeStruct((rows, width), f32) for _ in range(3)),
        in_specs=[SM(), SM()] + [VM()] * 8,
        out_specs=(VM(), VM(), VM()),
        scratch_shapes=[pltpu.VMEM((pad_rows, width), bf16)] * 4
        + [pltpu.VMEM((pad_rows, width), f32)] * 2,
        compiler_params=pltpu.CompilerParams(vmem_limit_bytes=56 << 20),
        cost_estimate=pl.CostEstimate(flops=30 * rows * key_rows * width, bytes_accessed=32 * rows * width, transcendentals=rows * key_rows * 8),
        name="attend_back",
    )(block_low, block_count, queries, keys_in, values_in, outputs, grad_out, totals, low, high)


def key_ranges(query_lengths, key_lengths, rows):
    query_ends = jnp.cumsum(query_lengths)
    query_starts = query_ends - query_lengths
    places = jnp.arange(rows, dtype=jnp.int32)
    low = jnp.sum(jnp.where(query_ends[None, :] <= places[:, None], key_lengths[None, :], 0), axis=1)
    high = jnp.sum(jnp.where(query_starts[None, :] <= places[:, None], key_lengths[None, :], 0), axis=1)
    block_low = low[::q_rows] // 16 * 16
    block_high = high[q_rows - 1 :: q_rows]
    block_count = (block_high - block_low + key_rows - 1) // key_rows
    return block_low, block_count, low[:, None], high[:, None]


def matmul(left_side, right_side):
    return jnp.dot(left_side, right_side, precision=lax.Precision.HIGH, preferred_element_type=f32)


def layer_norm(values, gain_row, shift_row):
    centre_mean = jnp.mean(values, axis=-1, keepdims=True)
    centred = values - centre_mean
    variance = jnp.mean(centred * centred, axis=-1, keepdims=True)
    return centred * lax.rsqrt(variance + norm_eps) * gain_row + shift_row


def apply_gelu(values):
    return (
        0.5
        * values
        * (1.0 + jnp.tanh(0.7978845608028654 * (values + 0.044715 * values * values * values)))
    )


def flip(value, axis, distance):
    pairs = [(i, i ^ distance) for i in range(lax.axis_size(axis))]
    return lax.ppermute(value, axis, pairs)


def tree_total(pieces):
    while len(pieces) > 1:
        pieces = [pieces[i] + pieces[i + 1] for i in range(0, len(pieces), 2)]
    return pieces[0]


def small_total(value):
    value = value + flip(value, "dp", 1)
    others = lax.axis_size("dp") // 2
    value = tree_total([value] + [flip(value, "dp", 2 * r) for r in range(1, others)])
    models = lax.axis_size("mp")
    return tree_total([value] + [flip(value, "mp", r) for r in range(1, models)])


def line_gather(own):
    count = lax.axis_size("mp")
    me = lax.axis_index("mp")
    left, right = [own], [own]
    for step in range(1, count):
        left.append(lax.ppermute(left[-1], "mp", [(i, i + 1) for i in range(step - 1, count - 1)]))
        right.append(lax.ppermute(right[-1], "mp", [(i, i - 1) for i in range(count - step, 0, -1)]))
    found = []
    for place in range(count):
        value = None
        for here in range(count):
            piece = left[here - place] if here >= place else right[place - here]
            value = piece if value is None else jnp.where(me == here, piece, value)
        found.append(value)
    return found


def cube_gather(own):
    count = lax.axis_size("dp")
    pieces = {0: own}
    step = 2
    while step < count:
        for at in list(pieces):
            pieces[at ^ step] = flip(pieces[at], "dp", step)
        step *= 2
    for at in list(pieces):
        pieces[at ^ 1] = flip(pieces[at], "dp", 1)
    return [pieces[r] for r in range(count)]


def place_kernel(parts, rows, columns, index_ref, *refs):
    pieces, (full_ref, rest_ref) = refs[:-2], refs[-2:]
    me = index_ref[0]
    for r, piece in enumerate(pieces):
        whose = me ^ r
        at = pl.ds(pl.multiple_of(whose * rows, rows), rows)
        for model in range(piece.shape[0]):
            for part in range(parts):
                full_ref[part, at, model * columns : (model + 1) * columns] = piece[
                    model, part * rows : (part + 1) * rows, :
                ]
            rest_ref[pl.ds(whose, 1), model] = piece[model, parts * rows :, :][None]


def place(pieces, me, parts, rows, columns):
    models, extra = pieces[0].shape[0], pieces[0].shape[1] - parts * rows
    count = len(pieces)
    return pl.pallas_call(
        functools.partial(place_kernel, parts, rows, columns),
        out_shape=(
            jax.ShapeDtypeStruct((parts, rows * count, columns * models), f32),
            jax.ShapeDtypeStruct((count, models, extra, columns), f32),
        ),
        in_specs=[SM()] + [VM()] * count,
        out_specs=(VM(), VM()),
        compiler_params=pltpu.CompilerParams(vmem_limit_bytes=40 << 20),
        name="place",
    )(me[None], *pieces)


def gather_matrices(own, me, parts, rows, columns):
    return place(cube_gather(jnp.stack(line_gather(own))), me, parts, rows, columns)


def pack_kernel(cap, starts_ref, source_ref, packed_ref, padded_ref):
    rows = source_ref.shape[0]
    padded_ref[:rows, :] = source_ref[...]
    padded_ref[rows:, :] = jnp.zeros((padded_ref.shape[0] - rows, source_ref.shape[1]), f32)

    def one(target, carry):
        packed_ref[pl.ds(target, 1)] = padded_ref[pl.ds(starts_ref[target], cap), :][None]
        return carry

    lax.fori_loop(0, packed_ref.shape[0], one, 0)


def pack_rows(source, starts, cap):
    rows, width = source.shape
    return pl.pallas_call(
        functools.partial(pack_kernel, cap),
        out_shape=jax.ShapeDtypeStruct((starts.shape[0], cap, width), f32),
        in_specs=[SM(), VM()],
        out_specs=VM(),
        scratch_shapes=[pltpu.VMEM((rows + cap, width), f32)],
        name="pack_rows",
    )(starts, source)


def unpack_kernel(slots_ref, arrived_ref, out_ref):
    def one(step, carry):
        for k in range(8):
            row = step * 8 + k
            out_ref[pl.ds(row, 1), :] = arrived_ref[pl.ds(slots_ref[row], 1), :]
        return carry

    lax.fori_loop(0, out_ref.shape[0] // 8, one, 0)


def unpack_rows(arrived, slots):
    return pl.pallas_call(
        unpack_kernel,
        out_shape=jax.ShapeDtypeStruct((slots.shape[0], arrived.shape[1]), f32),
        in_specs=[SM(), VM()],
        out_specs=VM(),
        name="unpack_rows",
    )(slots, arrived)


def place_back_kernel(slots_ref, grads_ref, out_ref):
    out_ref[...] = jnp.zeros_like(out_ref)

    def one(step, carry):
        for k in range(8):
            row = step * 8 + k
            out_ref[pl.ds(slots_ref[row], 1), :] = grads_ref[pl.ds(row, 1), :]
        return carry

    lax.fori_loop(0, grads_ref.shape[0] // 8, one, 0)


def place_back(grads_in, slots, total):
    return pl.pallas_call(
        place_back_kernel,
        out_shape=jax.ShapeDtypeStruct((total, grads_in.shape[1]), f32),
        in_specs=[SM(), VM()],
        out_specs=VM(),
        name="place_back",
    )(slots, grads_in)


def return_kernel(starts_ref, returned_ref, out_ref, padded_ref):
    cap = returned_ref.shape[1]

    def one(target, carry):
        padded_ref[pl.ds(starts_ref[target], cap), :] = returned_ref[pl.ds(target, 1)][0]
        return carry

    lax.fori_loop(0, returned_ref.shape[0], one, 0)
    out_ref[...] = padded_ref[: out_ref.shape[0], :]


def return_rows(returned, starts, rows):
    _, cap, width = returned.shape
    return pl.pallas_call(
        return_kernel,
        out_shape=jax.ShapeDtypeStruct((rows, width), f32),
        in_specs=[SM(), VM()],
        out_specs=VM(),
        scratch_shapes=[pltpu.VMEM((rows + cap, width), f32)],
        name="return_rows",
    )(starts, returned)


def cube_scatter(value):
    count = value.shape[0]
    others = count // 2
    me = lax.axis_index("dp")
    odd = me % 2 == 1
    view = value.reshape((others, 2) + value.shape[1:])
    send = jnp.where(odd, view[:, 0], view[:, 1])
    keep = jnp.where(odd, view[:, 1], view[:, 0])
    both = keep + flip(send, "dp", 1)
    block = lambda r: lax.dynamic_index_in_dim(both, (me // 2) ^ r, 0, keepdims=False)
    return tree_total([block(0)] + [flip(block(r), "dp", 2 * r) for r in range(1, others)])


def part_squares(arrays, divisor):
    return jnp.concatenate(
        [
            jnp.sum(arrays[0] * arrays[0], axis=(1, 2)),
            jnp.sum(arrays[1] * arrays[1], axis=(1, 2)),
            jnp.sum(arrays[2] * arrays[2])[None],
            jnp.sum(arrays[3] * arrays[3])[None],
            jnp.sum(arrays[4] * arrays[4], axis=1) / divisor,
            jnp.sum(arrays[5] * arrays[5])[None],
        ]
    )


def spread_parts(per_part):
    return (
        per_part[0:6][:, None, None],
        per_part[6:8][:, None, None],
        per_part[8],
        per_part[9],
        per_part[10:17][:, None],
        per_part[17],
    )


def shards(
    layer_input,
    encoder_memory,
    output_grad,
    target_lengths,
    memory_lengths,
    source_slots,
    pair_counts,
    attend_input,
    attend_output,
    expand_weight,
    reduce_weight,
    norm_vectors,
    expand_bias,
    attend_input_first,
    attend_input_second,
    attend_output_first,
    attend_output_second,
    expand_weight_first,
    expand_weight_second,
    reduce_weight_first,
    reduce_weight_second,
    norm_vectors_first,
    norm_vectors_second,
    expand_bias_first,
    expand_bias_second,
):
    data_count = lax.axis_size("dp")
    model_count = lax.axis_size("mp")
    me = lax.axis_index("dp")
    model = lax.axis_index("mp")
    tok_rows, width = layer_input.shape
    rows, columns = attend_input.shape[1:]
    units = expand_weight.shape[1]
    weights = (attend_input, attend_output, expand_weight, reduce_weight, norm_vectors, expand_bias)

    bias_rows = expand_bias.shape[0]
    vectors = jnp.concatenate(
        [
            jnp.pad(norm_vectors, ((0, 0), (0, columns - rows))),
            jnp.pad(expand_bias[None], ((0, 0), (0, columns - bias_rows))),
        ],
        axis=0,
    )
    own_self = jnp.concatenate(
        [attend_input[:3].reshape(3 * rows, columns), attend_output[0].T, vectors], axis=0
    )
    own_cross = jnp.concatenate(
        [attend_input[3:].reshape(3 * rows, columns), attend_output[1].T, vectors], axis=0
    )
    own_wide = jnp.concatenate([expand_weight, reduce_weight.T], axis=0)
    all_wide = lax.all_gather(own_wide, ("dp", "mp"))
    self_full, all_vectors = gather_matrices(own_self, me, 4, rows, columns)
    cross_full, _ = gather_matrices(own_cross, me, 4, rows, columns)
    all_wide = all_wide.reshape(data_count, model_count, 2, rows, units)
    all_wide = all_wide.transpose(2, 0, 3, 1, 4).reshape(2, rows * data_count, units * model_count)
    expand_full, reduce_turned = all_wide[0], all_wide[1]
    full_vectors = all_vectors[:, 0, :7, :rows].transpose(1, 0, 2).reshape(7, width)
    full_bias = all_vectors[:, :, 7, :bias_rows].transpose(1, 0, 2).reshape(units * model_count)

    extra_slots = tok_rows // 16
    slot_cap = (tok_rows - data_count // 4 * extra_slots) // data_count + extra_slots
    my_counts = lax.dynamic_index_in_dim(pair_counts, me, 0, keepdims=False)
    my_starts = jnp.cumsum(my_counts) - my_counts
    arrived = lax.all_to_all(
        pack_rows(encoder_memory, my_starts, slot_cap), "dp", split_axis=0, concat_axis=0, tiled=True
    )
    memory_own = unpack_rows(arrived.reshape(data_count * slot_cap, columns), source_slots)
    memory_target = jnp.concatenate(line_gather(memory_own), axis=1)

    self_ranges = key_ranges(target_lengths[0], target_lengths[0], tok_rows)
    cross_ranges = key_ranges(target_lengths[0], memory_lengths[0], tok_rows)

    self_query = matmul(layer_input, self_full[0])
    self_key = matmul(layer_input, self_full[1])
    self_value = matmul(layer_input, self_full[2])
    self_out, self_totals = attend(self_query, self_key, self_value, self_ranges, HD)
    self_mix = matmul(self_out, self_full[3].T)
    first_norm, first_back = jax.vjp(layer_norm, layer_input + self_mix, full_vectors[0], full_vectors[3])
    cross_query = matmul(first_norm, cross_full[0])
    cross_key = matmul(memory_target, cross_full[1])
    cross_value = matmul(memory_target, cross_full[2])
    cross_out, cross_totals = attend(cross_query, cross_key, cross_value, cross_ranges, HD)
    cross_mix = matmul(cross_out, cross_full[3].T)
    second_norm, second_back = jax.vjp(layer_norm, first_norm + cross_mix, full_vectors[1], full_vectors[4])
    expand_pre = matmul(second_norm, expand_full) + full_bias
    expanded, gelu_back = jax.vjp(apply_gelu, expand_pre)
    reduced = matmul(expanded, reduce_turned.T)
    layer_output, third_back = jax.vjp(
        layer_norm, second_norm + reduced + full_vectors[6], full_vectors[2], full_vectors[5]
    )

    def mine(value, size):
        return lax.dynamic_slice_in_dim(value, model * size, size, axis=1)

    def blocks(value):
        return value.reshape(data_count, rows, value.shape[1])

    resid_three_grad, gain_three, shift_three = third_back(output_grad)
    reduce_bias_grad = jnp.sum(resid_three_grad, axis=0)
    (pre_grad,) = gelu_back(matmul(resid_three_grad, reduce_turned))
    second_grad = resid_three_grad + matmul(pre_grad, expand_full.T)
    grad_reduce = matmul(resid_three_grad.T, mine(expanded, units))
    grad_expand = matmul(second_norm.T, mine(pre_grad, units))
    grad_bias = jnp.sum(mine(pre_grad, units), axis=0)
    grad_wide = lax.psum_scatter(
        blocks(jnp.concatenate([grad_expand, grad_reduce], axis=1)), "dp", scatter_dimension=0, tiled=False
    )
    resid_two_grad, gain_two, shift_two = second_back(second_grad)
    cross_out_grad = matmul(resid_two_grad, cross_full[3])
    cross_query_grad, cross_key_grad, cross_value_grad = attend_back(
        cross_query, cross_key, cross_value, cross_out, cross_totals, cross_out_grad, cross_ranges, HD
    )
    memory_columns = lambda matrix: lax.dynamic_slice_in_dim(matrix, model * columns, columns, axis=0)
    first_grad = resid_two_grad + matmul(cross_query_grad, cross_full[0].T)
    memory_grad_own = matmul(cross_key_grad, memory_columns(cross_full[1]).T) + matmul(
        cross_value_grad, memory_columns(cross_full[2]).T
    )
    returned = lax.all_to_all(
        place_back(memory_grad_own, source_slots, data_count * slot_cap).reshape(
            data_count, slot_cap, columns
        ),
        "dp",
        split_axis=0,
        concat_axis=0,
        tiled=True,
    )
    memory_grad = return_rows(returned, my_starts, tok_rows)
    grad_cross = jnp.concatenate(
        [
            matmul(first_norm.T, mine(cross_query_grad, columns)),
            matmul(memory_target.T, mine(cross_key_grad, columns)),
            matmul(memory_target.T, mine(cross_value_grad, columns)),
            matmul(resid_two_grad.T, mine(cross_out, columns)),
        ],
        axis=1,
    )
    grad_cross = lax.psum_scatter(blocks(grad_cross), "dp", scatter_dimension=0, tiled=False)
    resid_one_grad, gain_one, shift_one = first_back(first_grad)
    self_out_grad = matmul(resid_one_grad, self_full[3])
    self_query_grad, self_key_grad, self_value_grad = attend_back(
        self_query, self_key, self_value, self_out, self_totals, self_out_grad, self_ranges, HD
    )
    grad_self = jnp.concatenate(
        [
            matmul(layer_input.T, mine(self_query_grad, columns)),
            matmul(layer_input.T, mine(self_key_grad, columns)),
            matmul(layer_input.T, mine(self_value_grad, columns)),
            matmul(resid_one_grad.T, mine(self_out, columns)),
        ],
        axis=1,
    )
    grad_self = cube_scatter(blocks(grad_self))
    input_grad = (
        resid_one_grad
        + matmul(self_query_grad, self_full[0].T)
        + matmul(self_key_grad, self_full[1].T)
        + matmul(self_value_grad, self_full[2].T)
    )
    grad_vectors = jnp.stack(
        [gain_one, gain_two, gain_three, shift_one, shift_two, shift_three, reduce_bias_grad]
    )
    grad_vectors = jnp.concatenate(
        [
            grad_vectors.reshape(7, data_count, rows).transpose(1, 0, 2),
            jnp.pad(grad_bias.reshape(data_count, 1, bias_rows), ((0, 0), (0, 0), (0, rows - bias_rows))),
        ],
        axis=1,
    )
    grad_vectors = cube_scatter(grad_vectors)

    def third(value, which):
        return value[:, which * columns : (which + 1) * columns]

    grad_shards = (
        jnp.stack([third(grad_self, i) for i in range(3)] + [third(grad_cross, i) for i in range(3)]),
        jnp.stack([third(grad_self, 3).T, third(grad_cross, 3).T]),
        grad_wide[:, :units],
        grad_wide[:, units:].T,
        grad_vectors[:7],
        grad_vectors[7, :bias_rows],
    )
    firsts = (
        attend_input_first,
        attend_output_first,
        expand_weight_first,
        reduce_weight_first,
        norm_vectors_first,
        expand_bias_first,
    )
    seconds = (
        attend_input_second,
        attend_output_second,
        expand_weight_second,
        reduce_weight_second,
        norm_vectors_second,
        expand_bias_second,
    )
    weight_square = small_total(part_squares(weights, model_count))
    total_square = small_total(jnp.sum(part_squares(grad_shards, model_count))[None])[0]
    grad_norm = jnp.sqrt(total_square)
    clip_factor = jnp.minimum(1.0, clip_norm / grad_norm)
    steps_done = jnp.float32(STEP_NUM)
    step_rate = peak_rate * jnp.minimum(steps_done / warm_steps, jnp.sqrt(warm_steps / steps_done))
    first_fix = 1.0 - first_decay**steps_done
    second_fix = 1.0 - second_decay**steps_done
    new_firsts = []
    new_seconds = []
    updates = []
    for number in range(6):
        clipped = grad_shards[number] * clip_factor
        moment_one = first_decay * firsts[number] + (1.0 - first_decay) * clipped
        moment_two = second_decay * seconds[number] + (1.0 - second_decay) * clipped * clipped
        decay_rate = matrix_decay if number < 4 else 0.0
        updates.append(
            moment_one / first_fix / (jnp.sqrt(moment_two / second_fix) + adam_eps)
            + decay_rate * weights[number]
        )
        new_firsts.append(moment_one)
        new_seconds.append(moment_two)
    update_square = small_total(part_squares(updates, model_count))
    ratios = spread_parts(jnp.sqrt(weight_square) / jnp.sqrt(update_square))
    new_weights = [
        weights[number] - step_rate * ratios[number] * updates[number] for number in range(6)
    ]
    matrix_norms = jnp.stack([jnp.sqrt(weight_square[:10]), jnp.sqrt(update_square[:10])])
    return (
        layer_output,
        input_grad,
        memory_grad,
        grad_norm[None],
        *new_weights,
        *[value.astype(bf16) for value in new_weights[:4]],
        new_firsts[0],
        new_seconds[0],
        new_firsts[1],
        new_seconds[1],
        new_firsts[2],
        new_seconds[2],
        new_firsts[3],
        new_seconds[3],
        new_firsts[4],
        new_seconds[4],
        new_firsts[5],
        new_seconds[5],
        matrix_norms,
    )


def solution(mesh):
    in_specs = (
        P("dp", None),
        P("dp", "mp"),
        P("dp", None),
        P("dp", None),
        P("dp", None),
        P("dp"),
        P(),
        P(None, "dp", "mp"),
        P(None, "mp", "dp"),
        P("dp", "mp"),
        P("mp", "dp"),
        P(None, "dp"),
        P(("mp", "dp")),
        P(None, "dp", "mp"),
        P(None, "dp", "mp"),
        P(None, "mp", "dp"),
        P(None, "mp", "dp"),
        P("dp", "mp"),
        P("dp", "mp"),
        P("mp", "dp"),
        P("mp", "dp"),
        P(None, "dp"),
        P(None, "dp"),
        P(("mp", "dp")),
        P(("mp", "dp")),
    )
    out_specs = (
        P("dp", None),
        P("dp", None),
        P("dp", "mp"),
        P(),
        P(None, "dp", "mp"),
        P(None, "mp", "dp"),
        P("dp", "mp"),
        P("mp", "dp"),
        P(None, "dp"),
        P(("mp", "dp")),
        P(None, "dp", "mp"),
        P(None, "mp", "dp"),
        P("dp", "mp"),
        P("mp", "dp"),
        P(None, "dp", "mp"),
        P(None, "dp", "mp"),
        P(None, "mp", "dp"),
        P(None, "mp", "dp"),
        P("dp", "mp"),
        P("dp", "mp"),
        P("mp", "dp"),
        P("mp", "dp"),
        P(None, "dp"),
        P(None, "dp"),
        P(("mp", "dp")),
        P(("mp", "dp")),
        P(),
    )
    return jax.shard_map(shards, mesh=mesh, in_specs=in_specs, out_specs=out_specs, check_vma=False)
```

```python
import functools

import jax
import jax.numpy as jnp
from jax import lax
from jax.experimental import pallas as pl
from jax.experimental.pallas import tpu as pltpu
from jax.sharding import PartitionSpec as P

HD = 64
STEP_NUM = 6

norm_eps = 1e-05
adam_eps = 1e-06
first_decay = 0.5
second_decay = 0.5
matrix_decay = 0.01
peak_rate = 0.6
warm_steps = 8.0
clip_norm = 1.0

bf16 = jnp.bfloat16
f32 = jnp.float32
neg_large = -1e30
q_rows = 128
key_rows = 256
pair_lanes = 128


def split_two(values):
    high = values.astype(bf16)
    return high, (values - high.astype(f32)).astype(bf16)


def dot_nn(left_side, right_side):
    return lax.dot_general(left_side, right_side, (((1,), (0,)), ((), ())), preferred_element_type=f32)


def dot_nt(left_side, right_side):
    return lax.dot_general(left_side, right_side, (((1,), (1,)), ((), ())), preferred_element_type=f32)


def dot_tn(left_side, right_side):
    return lax.dot_general(left_side, right_side, (((0,), (0,)), ((), ())), preferred_element_type=f32)


def three(dot, left_pair, right_pair):
    return (
        dot(left_pair[0], right_pair[0])
        + dot(left_pair[1], right_pair[0])
        + dot(left_pair[0], right_pair[1])
    )


def swap_halves(tile):
    return pltpu.roll(tile, pair_lanes // 2, 1)


def parts_of(tile):
    high = tile.astype(bf16).astype(f32)
    return high, tile - high


def query_packs(tile, low_half):
    high, low = parts_of(tile)
    high_swap, low_swap = swap_halves(high), swap_halves(low)
    zero = jnp.zeros_like(tile)
    first = jnp.concatenate(
        [jnp.where(low_half, high, high_swap), jnp.where(low_half, low, zero)], axis=1
    )
    second = jnp.concatenate(
        [jnp.where(low_half, high_swap, high), jnp.where(low_half, low_swap, zero)], axis=1
    )
    return first.astype(bf16), second.astype(bf16)


def key_packs(tile, low_half):
    high, low = parts_of(tile)
    high_swap, low_swap = swap_halves(high), swap_halves(low)
    zero = jnp.zeros_like(tile)
    first = jnp.concatenate(
        [jnp.where(low_half, high, low_swap), jnp.where(low_half, high, zero)], axis=1
    )
    second = jnp.concatenate(
        [jnp.where(low_half, high_swap, low), jnp.where(low_half, high_swap, zero)], axis=1
    )
    return first.astype(bf16), second.astype(bf16)


def both_parts(tile):
    high, low = split_two(tile)
    return jnp.concatenate([high, low], axis=1)


def stack_heads(tile, low_half):
    return jnp.concatenate([jnp.where(low_half, tile, 0.0), jnp.where(low_half, 0.0, tile)], axis=0)


def merge_heads(stacked, low_half):
    return jnp.where(low_half, stacked[:q_rows], stacked[q_rows:])


def folded(dot, left_pair, right_both):
    wide = dot(left_pair[0], right_both)
    return wide[:, :pair_lanes] + wide[:, pair_lanes:] + dot(left_pair[1], right_both[:, :pair_lanes])


def prepare(source_ref, low_half, pack_ref, both_ref):
    rows, width = source_ref.shape

    def one(step, carry):
        at = pl.ds(pl.multiple_of(step * q_rows, q_rows), q_rows)
        for pair in range(width // pair_lanes):
            tile = source_ref[at, pair * pair_lanes : (pair + 1) * pair_lanes]
            if pack_ref is not None:
                first, second = key_packs(tile, low_half)
                pack_ref[2 * pair, at, :] = first
                pack_ref[2 * pair + 1, at, :] = second
            if both_ref is not None:
                both_ref[pair, at, :] = both_parts(tile)
        return carry

    lax.fori_loop(0, rows // q_rows, one, 0)
    for ref in (pack_ref, both_ref):
        if ref is not None:
            ref[:, rows:, :] = jnp.zeros((ref.shape[0], ref.shape[1] - rows, ref.shape[2]), bf16)


def attend_kernel(
    unroll, scale, block_low, block_count,
    q_ref, k_ref, v_ref, low_ref, high_ref,
    o_ref, total_ref,
    kp_ref, vb_ref,
):
    rows, width = q_ref.shape
    lanes = lax.broadcasted_iota(jnp.int32, (q_rows, pair_lanes), 1)
    low_half = lanes < pair_lanes // 2
    prepare(k_ref, low_half, kp_ref, None)
    prepare(v_ref, low_half, None, vb_ref)
    groups = width // pair_lanes // unroll
    key_iota = lax.broadcasted_iota(jnp.int32, (q_rows, key_rows), 1)

    def block(index, carry):
        at = pl.ds(pl.multiple_of(index * q_rows, q_rows), q_rows)
        first = low_ref[at, :]
        last = high_ref[at, :]
        for group in range(groups):
            pairs = [group * unroll + u for u in range(unroll)]
            queries = [
                query_packs(q_ref[at, p * pair_lanes : (p + 1) * pair_lanes] * scale, low_half)
                for p in pairs
            ]

            def chunk(step, state):
                start = pl.multiple_of(block_low[index] + step * key_rows, 16)
                here = pl.ds(start, key_rows)
                places = key_iota + start
                bias = jnp.where(jnp.logical_and(places >= first, places < last), 0.0, neg_large)
                bias = jnp.concatenate([bias, bias], axis=0)
                out = []
                found = [
                    jnp.concatenate(
                        [dot_nt(queries[u][h], kp_ref[2 * p + h, here, :]) for h in range(2)], axis=0
                    )
                    for u, p in enumerate(pairs)
                ]
                for u, p in enumerate(pairs):
                    scores = bias + found[u]
                    new_top = jnp.max(scores, axis=1, keepdims=True)
                    if state is not None:
                        top, total, held = state[u]
                        new_top = jnp.maximum(top, new_top)
                        shrink = jnp.exp(top - new_top)
                    weights = jnp.exp(scores - new_top)
                    new_total = jnp.sum(weights, axis=1, keepdims=True)
                    new_held = folded(dot_nn, split_two(weights), vb_ref[p, here, :])
                    if state is not None:
                        new_total = total * shrink + new_total
                        new_held = held * shrink + new_held
                    out.append((new_top, new_total, new_held))
                return tuple(out)

            def finish(state):
                tile = total_ref[at, :] if group else jnp.zeros((q_rows, pair_lanes), f32)
                for u, p in enumerate(pairs):
                    top, total, held = state[u]
                    o_ref[at, p * pair_lanes : (p + 1) * pair_lanes] = merge_heads(held / total, low_half)
                    logs = top + jnp.log(total)
                    tile = jnp.where(lanes == 2 * p, logs[:q_rows], tile)
                    tile = jnp.where(lanes == 2 * p + 1, logs[q_rows:], tile)
                total_ref[at, :] = tile

            @pl.when(block_count[index] == 1)
            def _():
                finish(chunk(0, None))

            @pl.when(block_count[index] > 1)
            def _():
                start_state = tuple(
                    (
                        jnp.full((2 * q_rows, 1), neg_large, f32),
                        jnp.zeros((2 * q_rows, 1), f32),
                        jnp.zeros((2 * q_rows, pair_lanes), f32),
                    )
                    for _ in range(unroll)
                )
                finish(lax.fori_loop(0, block_count[index], chunk, start_state))

        return carry

    lax.fori_loop(0, rows // q_rows, block, 0)


def attend_back_blocks(
    unroll, scale, block_low, block_count,
    q_ref, o_ref, g_ref, total_ref, low_ref, high_ref,
    dq_ref, kp_ref, vp_ref, kb_ref, dk_sum, dv_sum,
):
    rows, width = q_ref.shape
    lanes = lax.broadcasted_iota(jnp.int32, (q_rows, pair_lanes), 1)
    low_half = lanes < pair_lanes // 2
    groups = width // pair_lanes // unroll
    key_iota = lax.broadcasted_iota(jnp.int32, (q_rows, key_rows), 1)

    def block(index, carry):
        at = pl.ds(pl.multiple_of(index * q_rows, q_rows), q_rows)
        first = low_ref[at, :]
        last = high_ref[at, :]
        total_tile = total_ref[at, :]
        for group in range(groups):
            pairs = [group * unroll + u for u in range(unroll)]
            queries, query_both, grads, grad_both, logs, dots = [], [], [], [], [], []
            for p in pairs:
                lanes_of = slice(p * pair_lanes, (p + 1) * pair_lanes)
                tile = q_ref[at, lanes_of] * scale
                queries.append(query_packs(tile, low_half))
                query_both.append(both_parts(stack_heads(tile, low_half)))
                tile = g_ref[at, lanes_of]
                grads.append(query_packs(tile, low_half))
                grad_both.append(both_parts(stack_heads(tile, low_half)))
                product = tile * o_ref[at, lanes_of]
                column = lambda mask, value: jnp.sum(jnp.where(mask, value, 0.0), axis=1, keepdims=True)
                dots.append(
                    jnp.concatenate(
                        [column(low_half, product), column(jnp.logical_not(low_half), product)], axis=0
                    )
                )
                logs.append(
                    jnp.concatenate(
                        [column(lanes == 2 * p, total_tile), column(lanes == 2 * p + 1, total_tile)], axis=0
                    )
                )

            def chunk(step, state):
                start = pl.multiple_of(block_low[index] + step * key_rows, 16)
                here = pl.ds(start, key_rows)
                places = key_iota + start
                bias = jnp.where(jnp.logical_and(places >= first, places < last), 0.0, neg_large)
                bias = jnp.concatenate([bias, bias], axis=0)
                out = []
                found = [
                    jnp.concatenate(
                        [dot_nt(queries[u][h], kp_ref[2 * p + h, here, :]) for h in range(2)], axis=0
                    )
                    for u, p in enumerate(pairs)
                ]
                found_grad = [
                    jnp.concatenate(
                        [dot_nt(grads[u][h], vp_ref[2 * p + h, here, :]) for h in range(2)], axis=0
                    )
                    for u, p in enumerate(pairs)
                ]
                for u, p in enumerate(pairs):
                    lanes_of = slice(p * pair_lanes, (p + 1) * pair_lanes)
                    scores = bias + found[u]
                    weights = jnp.exp(scores - logs[u])
                    grad_weights = found_grad[u]
                    grad_scores = split_two(weights * (grad_weights - dots[u]))
                    new_state = folded(dot_nn, grad_scores, kb_ref[p, here, :])
                    out.append(new_state if state is None else state[u] + new_state)
                    dk_sum[here, lanes_of] += folded(dot_tn, grad_scores, query_both[u])
                    dv_sum[here, lanes_of] += folded(dot_tn, split_two(weights), grad_both[u])
                return tuple(out)

            def finish(state):
                for u, p in enumerate(pairs):
                    dq_ref[at, p * pair_lanes : (p + 1) * pair_lanes] = merge_heads(state[u], low_half) * scale

            @pl.when(block_count[index] == 1)
            def _():
                finish(chunk(0, None))

            @pl.when(block_count[index] > 1)
            def _():
                start_state = tuple(jnp.zeros((2 * q_rows, pair_lanes), f32) for _ in range(unroll))
                finish(lax.fori_loop(0, block_count[index], chunk, start_state))

        return carry

    lax.fori_loop(0, rows // q_rows, block, 0)


def own_lanes(ref, at, model, columns):
    if columns % pair_lanes == 0:
        return ref[at, pl.ds(pl.multiple_of(model * columns, pair_lanes), columns)]
    start = model * columns
    base = pl.multiple_of(start // pair_lanes * pair_lanes, pair_lanes)
    tile = ref[at, pl.ds(base, pair_lanes)]
    return pltpu.roll(tile, lax.rem(pair_lanes - lax.rem(start, pair_lanes), pair_lanes), 1)[:, :columns]


def norm_parts(values):
    centred = values - jnp.mean(values, axis=1, keepdims=True)
    scale = lax.rsqrt(jnp.mean(centred * centred, axis=1, keepdims=True) + norm_eps)
    return centred * scale, scale


def norm_back(grad, normal, scale, gain):
    inner = grad * gain
    return (
        inner
        - jnp.mean(inner, axis=1, keepdims=True)
        - normal * jnp.mean(inner * normal, axis=1, keepdims=True)
    ) * scale


def column_sum(value):
    return jnp.sum(value, axis=0, keepdims=True)


def chunks(rows, size, body):
    lax.fori_loop(0, rows // size, lambda step, carry: (body(pl.ds(pl.multiple_of(step * size, size), size)), carry)[1], 0)


def hand_out(index_ref, grads_ref, keep_ref, send_ref, rows, extra_ref=None):
    me = index_ref[0]
    odd = lax.rem(me, 2)
    for r in range(keep_ref.shape[0]):
        pair = 2 * ((me // 2) ^ r)
        for ref, which in ((keep_ref, pair + odd), (send_ref, pair + 1 - odd)):
            ref[r, :rows, :] = grads_ref[pl.ds(pl.multiple_of(which * rows, rows), rows), :]
            if extra_ref is not None:
                ref[r, rows:, :] = extra_ref[pl.ds(which, 1)][0]


def cross_back_kernel(
    unroll, scale, columns, rows_of, bias_rows, index_ref, block_low, block_count,
    g_ref, two_ref, one_ref, mem_ref, q_ref, k_ref, v_ref, o_ref, total_ref, low_ref, high_ref,
    w_ref, vec_ref, sums_ref, bias_ref,
    keep_ref, send_ref, resid_ref, mem_grad_ref,
    kp_ref, vp_ref, kb_ref, dk_sum, dv_sum, dq_ref, go_ref, two_grad_ref, woh, wol, wqh, wql, grads, totals, parts,
):
    rows, width = q_ref.shape
    model = index_ref[1]
    lanes = lax.broadcasted_iota(jnp.int32, (q_rows, pair_lanes), 1)
    low_half = lanes < pair_lanes // 2
    prepare(k_ref, low_half, kp_ref, kb_ref)
    prepare(v_ref, low_half, vp_ref, None)
    dk_sum[...] = jnp.zeros_like(dk_sum)
    dv_sum[...] = jnp.zeros_like(dv_sum)
    woh[...], wol[...] = split_two(w_ref[3])
    wqh[...], wql[...] = split_two(w_ref[0])
    totals[...] = sums_ref[...]
    grads[...] = jnp.zeros_like(grads)

    def before(at):
        normal, spread = norm_parts(two_ref[at, :])
        grad = g_ref[at, :]
        resid = norm_back(grad, normal, spread, vec_ref[0, 1:2, :])
        totals[1:2, :] += column_sum(grad * normal)
        totals[4:5, :] += column_sum(grad)
        two_grad_ref[at, :] = resid
        go_ref[at, :] = three(dot_nn, split_two(resid), (woh[...], wol[...]))

    chunks(rows, 256, before)
    attend_back_blocks(
        unroll, scale, block_low, block_count,
        q_ref, o_ref, go_ref, total_ref, low_ref, high_ref,
        dq_ref, kp_ref, vp_ref, kb_ref, dk_sum, dv_sum,
    )

    def after(at):
        resid = two_grad_ref[at, :]
        grad = resid + three(dot_nt, split_two(dq_ref[at, :]), (wqh[...], wql[...]))
        normal, spread = norm_parts(one_ref[at, :])
        gain = vec_ref[0, 0:1, :]
        resid_ref[at, :] = norm_back(grad, normal, spread, gain)
        totals[0:1, :] += column_sum(grad * normal)
        totals[3:4, :] += column_sum(grad)
        source = split_two(normal * gain + vec_ref[0, 3:4, :])
        memory = split_two(mem_ref[at, :])
        dk = dk_sum[at, :]
        dv = dv_sum[at, :]
        grads[:, :columns] += three(dot_tn, source, split_two(own_lanes(dq_ref, at, model, columns)))
        grads[:, columns : 2 * columns] += three(
            dot_tn, memory, split_two(own_lanes(dk_sum, at, model, columns))
        )
        grads[:, 2 * columns : 3 * columns] += three(
            dot_tn, memory, split_two(own_lanes(dv_sum, at, model, columns))
        )
        grads[:, 3 * columns :] += three(
            dot_tn, split_two(resid), split_two(own_lanes(o_ref, at, model, columns))
        )
        slice_of = pl.ds(pl.multiple_of(model * columns, columns), columns)
        mem_grad_ref[at, :] = three(dot_nt, split_two(dk), split_two(w_ref[1, slice_of, :])) + three(
            dot_nt, split_two(dv), split_two(w_ref[2, slice_of, :])
        )

    chunks(rows, 256, after)
    parts[...] = jnp.zeros_like(parts)
    for j in range(parts.shape[0]):
        parts[j, :, :rows_of] = totals[:, j * rows_of : (j + 1) * rows_of]
        parts[j, 7:8, :bias_rows] = bias_ref[:, j * bias_rows : (j + 1) * bias_rows]
    hand_out(index_ref, grads, keep_ref, send_ref, rows_of, parts)


def self_back_kernel(
    unroll, scale, columns, rows_of, index_ref, block_low, block_count,
    g_ref, x_ref, q_ref, k_ref, v_ref, o_ref, total_ref, low_ref, high_ref, w_ref,
    keep_ref, send_ref, dq_ref, dk_ref, dv_ref,
    kp_ref, vp_ref, kb_ref, dk_sum, dv_sum, go_ref, woh, wol, grads,
):
    rows, width = q_ref.shape
    model = index_ref[1]
    lanes = lax.broadcasted_iota(jnp.int32, (q_rows, pair_lanes), 1)
    low_half = lanes < pair_lanes // 2
    prepare(k_ref, low_half, kp_ref, kb_ref)
    prepare(v_ref, low_half, vp_ref, None)
    dk_sum[...] = jnp.zeros_like(dk_sum)
    dv_sum[...] = jnp.zeros_like(dv_sum)
    woh[...], wol[...] = split_two(w_ref[3])
    grads[...] = jnp.zeros_like(grads)

    def before(at):
        go_ref[at, :] = three(dot_nn, split_two(g_ref[at, :]), (woh[...], wol[...]))

    chunks(rows, 256, before)
    attend_back_blocks(
        unroll, scale, block_low, block_count,
        q_ref, o_ref, go_ref, total_ref, low_ref, high_ref,
        dq_ref, kp_ref, vp_ref, kb_ref, dk_sum, dv_sum,
    )

    def after(at):
        source = split_two(x_ref[at, :])
        dk_ref[at, :] = dk_sum[at, :]
        dv_ref[at, :] = dv_sum[at, :]
        for number, ref in enumerate((dq_ref, dk_sum, dv_sum)):
            grads[:, number * columns : (number + 1) * columns] += three(
                dot_tn, source, split_two(own_lanes(ref, at, model, columns))
            )
        grads[:, 3 * columns :] += three(
            dot_tn, split_two(g_ref[at, :]), split_two(own_lanes(o_ref, at, model, columns))
        )

    chunks(rows, 256, after)
    hand_out(index_ref, grads, keep_ref, send_ref, rows_of)


VM = functools.partial(pl.BlockSpec, memory_space=pltpu.VMEM)
SM = functools.partial(pl.BlockSpec, memory_space=pltpu.SMEM)


def attend(queries, keys_in, values_in, ranges, head_size, unroll=4):
    block_low, block_count, low, high = ranges
    rows, width = queries.shape
    pad_rows = keys_in.shape[0] + key_rows
    return pl.pallas_call(
        functools.partial(attend_kernel, unroll, head_size ** -0.5),
        out_shape=(
            jax.ShapeDtypeStruct((rows, width), f32),
            jax.ShapeDtypeStruct((rows, pair_lanes), f32),
        ),
        in_specs=[SM(), SM()] + [VM()] * 5,
        out_specs=(VM(), VM()),
        scratch_shapes=[
            pltpu.VMEM((width // 64, pad_rows, 2 * pair_lanes), bf16),
            pltpu.VMEM((width // pair_lanes, pad_rows, 2 * pair_lanes), bf16),
        ],
        compiler_params=pltpu.CompilerParams(vmem_limit_bytes=48 << 20),
        cost_estimate=pl.CostEstimate(flops=12 * rows * key_rows * width, bytes_accessed=16 * rows * width, transcendentals=rows * key_rows * 8),
        name="attend",
    )(block_low, block_count, queries, keys_in, values_in, low, high)


def back_scratch(rows, width):
    pad_rows = rows + key_rows
    return [
        pltpu.VMEM((width // 64, pad_rows, 2 * pair_lanes), bf16),
        pltpu.VMEM((width // 64, pad_rows, 2 * pair_lanes), bf16),
        pltpu.VMEM((width // pair_lanes, pad_rows, 2 * pair_lanes), bf16),
        pltpu.VMEM((pad_rows, width), f32),
        pltpu.VMEM((pad_rows, width), f32),
    ]


def cross_back(
    index, ranges, grad, two, one, memory, queries, keys_in, values_in, outputs, totals,
    matrices, vectors, sums, bias, head_size, columns, rows_of, bias_rows, unroll=4,
):
    block_low, block_count, low, high = ranges
    rows, width = queries.shape
    data = width // rows_of
    block = jax.ShapeDtypeStruct((data // 2, rows_of + 8, 4 * columns), f32)
    return pl.pallas_call(
        functools.partial(cross_back_kernel, unroll, head_size ** -0.5, columns, rows_of, bias_rows),
        out_shape=(
            block,
            block,
            jax.ShapeDtypeStruct((rows, width), f32),
            jax.ShapeDtypeStruct((rows, columns), f32),
        ),
        in_specs=[SM()] * 3 + [VM()] * 15,
        out_specs=(VM(),) * 4,
        scratch_shapes=back_scratch(rows, width)
        + [pltpu.VMEM((rows, width), f32)] * 3
        + [pltpu.VMEM((width, width), bf16)] * 4
        + [
            pltpu.VMEM((width, 4 * columns), f32),
            pltpu.VMEM((8, width), f32),
            pltpu.VMEM((data, 8, 4 * columns), f32),
        ],
        compiler_params=pltpu.CompilerParams(vmem_limit_bytes=60 << 20),
        cost_estimate=pl.CostEstimate(flops=30 << 30, bytes_accessed=30 << 20, transcendentals=rows * key_rows * 8),
        name="cross_back",
    )(
        index, block_low, block_count, grad, two, one, memory, queries, keys_in, values_in, outputs, totals,
        low, high, matrices, vectors, sums, bias,
    )


def self_back(
    index, ranges, grad, source, queries, keys_in, values_in, outputs, totals, matrices,
    head_size, columns, rows_of, unroll=4,
):
    block_low, block_count, low, high = ranges
    rows, width = queries.shape
    data = width // rows_of
    block = jax.ShapeDtypeStruct((data // 2, rows_of, 4 * columns), f32)
    return pl.pallas_call(
        functools.partial(self_back_kernel, unroll, head_size ** -0.5, columns, rows_of),
        out_shape=(block, block) + (jax.ShapeDtypeStruct((rows, width), f32),) * 3,
        in_specs=[SM()] * 3 + [VM()] * 10,
        out_specs=(VM(),) * 5,
        scratch_shapes=back_scratch(rows, width)
        + [pltpu.VMEM((rows, width), f32)]
        + [pltpu.VMEM((width, width), bf16)] * 2
        + [pltpu.VMEM((width, 4 * columns), f32)],
        compiler_params=pltpu.CompilerParams(vmem_limit_bytes=60 << 20),
        cost_estimate=pl.CostEstimate(flops=30 << 30, bytes_accessed=30 << 20, transcendentals=rows * key_rows * 8),
        name="self_back",
    )(
        index, block_low, block_count, grad, source, queries, keys_in, values_in, outputs, totals,
        low, high, matrices,
    )


def key_ranges(query_lengths, key_lengths, rows):
    query_ends = jnp.cumsum(query_lengths)
    query_starts = query_ends - query_lengths
    places = jnp.arange(rows, dtype=jnp.int32)
    low = jnp.sum(jnp.where(query_ends[None, :] <= places[:, None], key_lengths[None, :], 0), axis=1)
    high = jnp.sum(jnp.where(query_starts[None, :] <= places[:, None], key_lengths[None, :], 0), axis=1)
    block_low = low[::q_rows] // 16 * 16
    block_high = high[q_rows - 1 :: q_rows]
    block_count = (block_high - block_low + key_rows - 1) // key_rows
    return block_low, block_count, low[:, None], high[:, None]


def matmul(left_side, right_side):
    return jnp.dot(left_side, right_side, precision=lax.Precision.HIGH, preferred_element_type=f32)


def layer_norm(values, gain_row, shift_row):
    centre_mean = jnp.mean(values, axis=-1, keepdims=True)
    centred = values - centre_mean
    variance = jnp.mean(centred * centred, axis=-1, keepdims=True)
    return centred * lax.rsqrt(variance + norm_eps) * gain_row + shift_row


def flip(value, axis, distance):
    pairs = [(i, i ^ distance) for i in range(lax.axis_size(axis))]
    return lax.ppermute(value, axis, pairs)


def tree_total(pieces):
    while len(pieces) > 1:
        pieces = [pieces[i] + pieces[i + 1] for i in range(0, len(pieces), 2)]
    return pieces[0]


def small_total(value):
    value = value + flip(value, "dp", 1)
    others = lax.axis_size("dp") // 2
    value = tree_total([value] + [flip(value, "dp", 2 * r) for r in range(1, others)])
    models = lax.axis_size("mp")
    return tree_total([value] + [flip(value, "mp", r) for r in range(1, models)])


def ring_gather(own):
    count = lax.axis_size("mp")
    return [own] + [
        lax.ppermute(own, "mp", [(i, (i + step) % count) for i in range(count)])
        for step in range(1, count)
    ]


def ring_order(ring):
    count = len(ring)
    me = lax.axis_index("mp")
    found = []
    for place in range(count):
        value = ring[0]
        for step in range(1, count):
            value = jnp.where(me == (place + step) % count, ring[step], value)
        found.append(value)
    return found


def even_gather(own):
    return [own] + [flip(own, "dp", r) for r in range(2, lax.axis_size("dp"), 2)]


def odd_gather(even):
    odd = [flip(value, "dp", 1) for value in even]
    return [value for pair in zip(even, odd) for value in pair]


def place_kernel(parts, rows, columns, bias_rows, index_ref, *refs):
    pieces, (full_ref, vec_ref) = refs[:-2], refs[-2:]
    me, model = index_ref[0], index_ref[1]
    models = pieces[0].shape[0]
    width = vec_ref.shape[2]
    pad = jnp.zeros((8, width - columns), f32)
    bias_row = lax.broadcasted_iota(jnp.int32, (8, width), 0) == 7
    vec_ref[...] = jnp.zeros_like(vec_ref)
    for r, piece in enumerate(pieces):
        whose = me ^ r
        at = pl.ds(pl.multiple_of(whose * rows, rows), rows)
        for place in range(models):
            slot = lax.rem(model - place + models, models)
            for part in range(parts):
                full_ref[part, at, place * columns : (place + 1) * columns] = piece[
                    slot, part * rows : (part + 1) * rows, :
                ]
            values = jnp.concatenate([piece[slot, parts * rows :, :], pad], axis=1)
            moved = pltpu.roll(values, whose * rows, 1)
            if rows != bias_rows:
                moved = jnp.where(bias_row, pltpu.roll(values, whose * bias_rows, 1), moved)
            vec_ref[place] += moved


def place(pieces, index, parts, rows, columns, bias_rows):
    models, count = pieces[0].shape[0], len(pieces)
    return pl.pallas_call(
        functools.partial(place_kernel, parts, rows, columns, bias_rows),
        out_shape=(
            jax.ShapeDtypeStruct((parts, rows * count, columns * models), f32),
            jax.ShapeDtypeStruct((models, 8, columns * models), f32),
        ),
        in_specs=[SM()] + [VM()] * count,
        out_specs=(VM(), VM()),
        compiler_params=pltpu.CompilerParams(vmem_limit_bytes=40 << 20),
        name="place",
    )(index, *pieces)


def gelu_both(values):
    inner = 0.7978845608028654 * (values + 0.044715 * values * values * values)
    bent = jnp.tanh(inner)
    half = 0.5 * (1.0 + bent)
    slope = half + 0.5 * values * (1.0 - bent * bent) * (
        0.7978845608028654 * (1.0 + 3.0 * 0.044715 * values * values)
    )
    return values * half, slope


def wide_kernel(
    rows, model_ref, z_ref, g_ref, wide_ref, all_vec_ref,
    out_ref, second_ref, grads_ref, sums_ref, bias_grad_ref,
    eh_ref, el_ref, rh_ref, rl_ref, slope_ref, xh_ref, xl_ref,
):
    tokens, width = z_ref.shape
    data, models, _, units = wide_ref.shape
    model = model_ref[0]
    vec_ref = all_vec_ref.at[0]
    block = xh_ref.shape[0]

    def load(step, carry):
        which, part = step // models, step % models
        at = pl.ds(pl.multiple_of(which * rows, rows), rows)
        to = pl.ds(pl.multiple_of(part * units, units), units)
        eh_ref[at, to], el_ref[at, to] = split_two(wide_ref[which, part, :rows, :])
        rh_ref[at, to], rl_ref[at, to] = split_two(wide_ref[which, part, rows:, :])
        return carry

    lax.fori_loop(0, data * models, load, 0)
    sums_ref[...] = jnp.zeros_like(sums_ref)
    bias_grad_ref[...] = jnp.zeros_like(bias_grad_ref)
    grads_ref[...] = jnp.zeros_like(grads_ref)

    def chunk(step, carry):
        at = pl.ds(pl.multiple_of(step * block, block), block)
        source = z_ref[at, :]
        source_pair = split_two(source)

        def forward(part, reduced):
            to = pl.ds(pl.multiple_of(part * units, units), units)
            before = three(dot_nn, source_pair, (eh_ref[:, to], el_ref[:, to])) + all_vec_ref[part, 7:8, :units]
            value, slope = gelu_both(before)
            slope_ref[:, to] = slope
            high, low = split_two(value)
            xh_ref[:, to] = high
            xl_ref[:, to] = low
            return reduced + three(dot_nt, (high, low), (rh_ref[:, to], rl_ref[:, to]))

        reduced = lax.fori_loop(0, models, forward, source + vec_ref[6:7, :])
        normal, scale = norm_parts(reduced)
        gain = vec_ref[2:3, :]
        out_ref[at, :] = normal * gain + vec_ref[5:6, :]
        grad = g_ref[at, :]
        resid = norm_back(grad, normal, scale, gain)
        sums_ref[2:3, :] += column_sum(grad * normal)
        sums_ref[5:6, :] += column_sum(grad)
        sums_ref[6:7, :] += column_sum(resid)
        resid_pair = split_two(resid)

        def backward(part, second):
            to = pl.ds(pl.multiple_of(part * units, units), units)
            back = three(dot_nn, resid_pair, (rh_ref[:, to], rl_ref[:, to])) * slope_ref[:, to]
            back_pair = split_two(back)

            @pl.when(part == model)
            def _():
                bias_grad_ref[...] += jnp.sum(back, axis=0, keepdims=True)
                grads_ref[:, :units] += three(dot_tn, source_pair, back_pair)
                grads_ref[:, units:] += three(dot_tn, resid_pair, (xh_ref[:, to], xl_ref[:, to]))

            return second + three(dot_nt, back_pair, (eh_ref[:, to], el_ref[:, to]))

        second_ref[at, :] = lax.fori_loop(0, models, backward, resid)
        return carry

    lax.fori_loop(0, tokens // block, chunk, 0)


def feed_forward(model, source, grad, wide, vectors, rows):
    tokens, width = source.shape
    data, models, _, units = wide.shape
    block = min(512, tokens)
    return pl.pallas_call(
        functools.partial(wide_kernel, rows),
        out_shape=(
            jax.ShapeDtypeStruct((tokens, width), f32),
            jax.ShapeDtypeStruct((tokens, width), f32),
            jax.ShapeDtypeStruct((width, 2 * units), f32),
            jax.ShapeDtypeStruct((8, width), f32),
            jax.ShapeDtypeStruct((1, units), f32),
        ),
        in_specs=[SM()] + [VM()] * 4,
        out_specs=(VM(),) * 5,
        scratch_shapes=[pltpu.VMEM((width, models * units), bf16)] * 4
        + [
            pltpu.VMEM((block, models * units), f32),
            pltpu.VMEM((block, models * units), bf16),
            pltpu.VMEM((block, models * units), bf16),
        ],
        compiler_params=pltpu.CompilerParams(vmem_limit_bytes=60 << 20),
        cost_estimate=pl.CostEstimate(
            flops=27 * tokens * width * models * units, bytes_accessed=24 << 20, transcendentals=tokens * models * units
        ),
        name="feed_forward",
    )(model[None], source, grad, wide, vectors)


def cell(row, lane):
    return jnp.sum(
        jnp.where(lax.broadcasted_iota(jnp.int32, row.shape, 1) == lane, row, 0.0), axis=1, keepdims=True
    )


def total_of(value):
    return jnp.sum(jnp.sum(value, axis=1, keepdims=True), axis=0, keepdims=True)


def put(row, lane, value):
    return jnp.where(lax.broadcasted_iota(jnp.int32, row.shape, 1) == lane, value, row)


def part_row(pieces, divisor):
    row = jnp.zeros((1, 128), f32)
    for number, value in enumerate(pieces):
        total = total_of(value * value)
        row = put(row, number, total / divisor if 10 <= number < 17 else total)
    return row


def part_list(arrays):
    return (
        [arrays[0][i] for i in range(arrays[0].shape[0])]
        + [arrays[1][i] for i in range(arrays[1].shape[0])]
        + [arrays[2][...], arrays[3][...]]
        + [arrays[4][i : i + 1, :] for i in range(arrays[4].shape[0])]
        + [arrays[5][...]]
    )


def squares_kernel(divisor, count, *refs):
    self_pieces, cross_pieces, rest = refs[:count], refs[count : 2 * count], refs[2 * count :]
    wide, weights, (self_ref, cross_ref, vector_ref, row_ref) = rest[0][...], rest[1:-4], rest[-4:]
    rows = self_ref.shape[0]
    value = tree_total([piece[...] for piece in self_pieces])
    both = tree_total([piece[...] for piece in cross_pieces])
    cross, vectors = both[:rows], both[rows:, :rows]
    self_ref[...] = value
    cross_ref[...] = cross
    vector_ref[...] = vectors
    total = total_of(value * value) + total_of(cross * cross) + total_of(wide * wide)
    norms = vectors[:7]
    last = vectors[7:8]
    total = total + total_of(norms * norms) / divisor + total_of(last * last)
    row_ref[...] = put(part_row(part_list(weights), divisor), 18, total)


def moments_kernel(divisor, columns, row_ref, *refs):
    grads, rest = refs[:4], refs[4:]
    weights, firsts, seconds = rest[:6], rest[6:12], rest[12:18]
    new_firsts, new_seconds, updates, out_row = rest[18:24], rest[24:30], rest[30:36], rest[36]
    units = rest[2].shape[1]
    bias_rows = rest[5].shape[1]
    norm = jnp.sqrt(cell(row_ref[...], 18))
    clip = jnp.minimum(1.0, clip_norm / norm)
    first_fix = 1.0 - first_decay**STEP_NUM
    second_fix = 1.0 - second_decay**STEP_NUM

    def step(grad, weight, first, second, decay):
        clipped = grad * clip
        one = first_decay * first + (1.0 - first_decay) * clipped
        two = second_decay * second + (1.0 - second_decay) * clipped * clipped
        return one, two, one / first_fix / (jnp.sqrt(two / second_fix) + adam_eps) + decay * weight

    squares = []

    def store(number, at, grad, decay):
        one, two, update = step(
            grad, weights[number][at], firsts[number][at], seconds[number][at], decay
        )
        new_firsts[number][at] = one
        new_seconds[number][at] = two
        updates[number][at] = update
        return update

    for number in range(2):
        for which in range(3):
            store(0, 3 * number + which, grads[number][:, which * columns : (which + 1) * columns], matrix_decay)
    for number in range(2):
        store(1, number, grads[number][:, 3 * columns : 4 * columns], matrix_decay)
    store(2, slice(None), grads[2][:, :units], matrix_decay)
    store(3, slice(None), grads[2][:, units:], matrix_decay)
    store(4, slice(None), grads[3][:7, :], 0.0)
    store(5, slice(None), grads[3][7:8, :bias_rows], 0.0)
    out_row[...] = part_row(part_list(updates), divisor)


def apply_kernel(weight_row_ref, update_row_ref, *refs):
    weights, updates, new, copies = refs[:6], refs[6:12], refs[12:18], refs[18:22]
    norms_ref, grad_norm_ref = refs[22:]
    rate = peak_rate * min(STEP_NUM / warm_steps, (warm_steps / STEP_NUM) ** 0.5)
    weight_row, update_row = jnp.sqrt(weight_row_ref[...]), jnp.sqrt(update_row_ref[...])
    lanes = lax.broadcasted_iota(jnp.int32, weight_row.shape, 1)
    ratios = rate * (weight_row / jnp.where(lanes < 18, update_row, 1.0))

    def store(number, at, part):
        value = weights[number][at] - cell(ratios, part) * updates[number][at]
        new[number][at] = value
        if number < 4:
            copies[number][at] = value.astype(bf16)

    for which in range(6):
        store(0, which, which)
    for which in range(2):
        store(1, which, 6 + which)
    store(2, slice(None), 8)
    store(3, slice(None), 9)
    for which in range(7):
        store(4, slice(which, which + 1), 10 + which)
    store(5, slice(None), 17)
    norms_ref[0:1, :] = weight_row
    norms_ref[1:2, :] = update_row
    grad_norm_ref[...] = cell(weight_row, 18)


def same(arrays, dtype=f32):
    return tuple(jax.ShapeDtypeStruct(value.shape, dtype) for value in arrays)


def whole_call(kernel, name, out_shape, *arrays):
    return pl.pallas_call(
        kernel,
        out_shape=out_shape,
        in_specs=[VM()] * len(arrays),
        out_specs=jax.tree.map(lambda _: VM(), out_shape),
        compiler_params=pltpu.CompilerParams(vmem_limit_bytes=40 << 20),
        name=name,
    )(*arrays)


def pack_kernel(cap, starts_ref, source_ref, packed_ref, padded_ref):
    rows = source_ref.shape[0]
    padded_ref[:rows, :] = source_ref[...]
    padded_ref[rows:, :] = jnp.zeros((padded_ref.shape[0] - rows, source_ref.shape[1]), f32)

    def one(target, carry):
        packed_ref[pl.ds(target, 1)] = padded_ref[pl.ds(starts_ref[target], cap), :][None]
        return carry

    lax.fori_loop(0, packed_ref.shape[0], one, 0)


def pack_rows(source, starts, cap):
    rows, width = source.shape
    return pl.pallas_call(
        functools.partial(pack_kernel, cap),
        out_shape=jax.ShapeDtypeStruct((starts.shape[0], cap, width), f32),
        in_specs=[SM(), VM()],
        out_specs=VM(),
        scratch_shapes=[pltpu.VMEM((rows + cap, width), f32)],
        name="pack_rows",
    )(starts, source)


def unpack_kernel(slots_ref, arrived_ref, out_ref):
    def one(step, carry):
        for k in range(8):
            row = step * 8 + k
            out_ref[pl.ds(row, 1), :] = arrived_ref[pl.ds(slots_ref[row], 1), :]
        return carry

    lax.fori_loop(0, out_ref.shape[0] // 8, one, 0)


def unpack_rows(arrived, slots):
    return pl.pallas_call(
        unpack_kernel,
        out_shape=jax.ShapeDtypeStruct((slots.shape[0], arrived.shape[1]), f32),
        in_specs=[SM(), VM()],
        out_specs=VM(),
        name="unpack_rows",
    )(slots, arrived)


def place_back_kernel(slots_ref, grads_ref, out_ref):
    out_ref[...] = jnp.zeros_like(out_ref)

    def one(step, carry):
        for k in range(8):
            row = step * 8 + k
            out_ref[pl.ds(slots_ref[row], 1), :] = grads_ref[pl.ds(row, 1), :]
        return carry

    lax.fori_loop(0, grads_ref.shape[0] // 8, one, 0)


def place_back(grads_in, slots, total):
    return pl.pallas_call(
        place_back_kernel,
        out_shape=jax.ShapeDtypeStruct((total, grads_in.shape[1]), f32),
        in_specs=[SM(), VM()],
        out_specs=VM(),
        name="place_back",
    )(slots, grads_in)


def return_kernel(starts_ref, returned_ref, out_ref, padded_ref):
    cap = returned_ref.shape[1]

    def one(target, carry):
        padded_ref[pl.ds(starts_ref[target], cap), :] = returned_ref[pl.ds(target, 1)][0]
        return carry

    lax.fori_loop(0, returned_ref.shape[0], one, 0)
    out_ref[...] = padded_ref[: out_ref.shape[0], :]


def return_rows(returned, starts, rows):
    _, cap, width = returned.shape
    return pl.pallas_call(
        return_kernel,
        out_shape=jax.ShapeDtypeStruct((rows, width), f32),
        in_specs=[SM(), VM()],
        out_specs=VM(),
        scratch_shapes=[pltpu.VMEM((rows + cap, width), f32)],
        name="return_rows",
    )(starts, returned)


def cube_scatter(keep, send):
    both = keep + flip(send, "dp", 1)
    return [both[0]] + [flip(both[r], "dp", 2 * r) for r in range(1, both.shape[0])]


def shards(
    layer_input,
    encoder_memory,
    output_grad,
    target_lengths,
    memory_lengths,
    source_slots,
    pair_counts,
    attend_input,
    attend_output,
    expand_weight,
    reduce_weight,
    norm_vectors,
    expand_bias,
    attend_input_first,
    attend_input_second,
    attend_output_first,
    attend_output_second,
    expand_weight_first,
    expand_weight_second,
    reduce_weight_first,
    reduce_weight_second,
    norm_vectors_first,
    norm_vectors_second,
    expand_bias_first,
    expand_bias_second,
):
    data_count = lax.axis_size("dp")
    model_count = lax.axis_size("mp")
    me = lax.axis_index("dp")
    model = lax.axis_index("mp")
    tok_rows, width = layer_input.shape
    rows, columns = attend_input.shape[1:]
    units = expand_weight.shape[1]
    attend_output, attend_output_first, attend_output_second = [
        value.transpose(0, 2, 1) for value in (attend_output, attend_output_first, attend_output_second)
    ]
    reduce_weight, reduce_weight_first, reduce_weight_second = [
        value.T for value in (reduce_weight, reduce_weight_first, reduce_weight_second)
    ]
    weights = (attend_input, attend_output, expand_weight, reduce_weight, norm_vectors, expand_bias)

    extra_slots = tok_rows // 16
    slot_cap = (tok_rows - data_count // 4 * extra_slots) // data_count + extra_slots
    my_counts = lax.dynamic_index_in_dim(pair_counts, me, 0, keepdims=False)
    my_starts = jnp.cumsum(my_counts) - my_counts
    arrived = lax.all_to_all(
        pack_rows(encoder_memory, my_starts, slot_cap), "dp", split_axis=0, concat_axis=0, tiled=True
    )

    bias_rows = expand_bias.shape[0]
    vectors = jnp.concatenate(
        [
            jnp.pad(norm_vectors, ((0, 0), (0, columns - rows))),
            jnp.pad(expand_bias[None], ((0, 0), (0, columns - bias_rows))),
        ],
        axis=0,
    )
    own_self = jnp.concatenate(
        [attend_input[:3].reshape(3 * rows, columns), attend_output[0], vectors], axis=0
    )
    own_cross = jnp.concatenate(
        [attend_input[3:].reshape(3 * rows, columns), attend_output[1], vectors], axis=0
    )
    own_wide = jnp.concatenate([expand_weight, reduce_weight], axis=0)
    index = jnp.stack([me, model])
    together = lax.optimization_barrier
    memory_own = unpack_rows(arrived.reshape(data_count * slot_cap, columns), source_slots)
    self_ring, own_cross, memory_own = together((ring_gather(own_self), own_cross, memory_own))
    self_even, cross_ring = together((even_gather(jnp.stack(self_ring)), ring_gather(own_cross)))
    memory_ring = ring_gather(memory_own)
    memory_ring[1], own_wide = together((memory_ring[1], own_wide))
    all_wide = lax.all_gather(own_wide, ("dp", "mp"))
    self_pieces = odd_gather(self_even)
    cross_even = even_gather(jnp.stack(cross_ring))
    self_full, all_vectors = place(self_pieces, index, 4, rows, columns, bias_rows)
    all_wide = all_wide.reshape(data_count, model_count, 2 * rows, units)
    full_vectors = all_vectors[0]

    self_ranges = key_ranges(target_lengths[0], target_lengths[0], tok_rows)
    cross_ranges = key_ranges(target_lengths[0], memory_lengths[0], tok_rows)

    self_query = matmul(layer_input, self_full[0])
    self_key = matmul(layer_input, self_full[1])
    self_value = matmul(layer_input, self_full[2])
    self_out, self_totals = attend(self_query, self_key, self_value, self_ranges, HD)
    self_out, memory_ring, cross_even = together((self_out, memory_ring, cross_even))
    cross_full, _ = place(odd_gather(cross_even), index, 4, rows, columns, bias_rows)
    memory_target = jnp.concatenate(ring_order(memory_ring), axis=1)
    self_mix = matmul(self_out, self_full[3].T)
    first_sum = layer_input + self_mix
    first_norm = layer_norm(first_sum, full_vectors[0], full_vectors[3])
    cross_query = matmul(first_norm, cross_full[0])
    cross_key = matmul(memory_target, cross_full[1])
    cross_value = matmul(memory_target, cross_full[2])
    cross_out, cross_totals = attend(cross_query, cross_key, cross_value, cross_ranges, HD)
    cross_mix = matmul(cross_out, cross_full[3].T)
    second_sum = first_norm + cross_mix
    second_norm = layer_norm(second_sum, full_vectors[1], full_vectors[4])
    layer_output, second_grad, grad_wide, wide_sums, grad_bias = feed_forward(
        model,
        second_norm,
        output_grad,
        all_wide,
        all_vectors,
        rows,
    )

    grad_wide = lax.psum_scatter(
        grad_wide.reshape(data_count, rows, 2 * units), "dp", scatter_dimension=0, tiled=False
    )
    keep, send, resid_one_grad, memory_grad_own = cross_back(
        index,
        cross_ranges,
        second_grad,
        second_sum,
        first_sum,
        memory_target,
        cross_query,
        cross_key,
        cross_value,
        cross_out,
        cross_totals,
        cross_full,
        all_vectors,
        wide_sums,
        grad_bias,
        HD,
        columns,
        rows,
        bias_rows,
    )
    placed = place_back(memory_grad_own, source_slots, data_count * slot_cap)
    resid_one_grad, placed = together((resid_one_grad, placed))
    returned = lax.all_to_all(
        placed.reshape(data_count, slot_cap, columns), "dp", split_axis=0, concat_axis=0, tiled=True
    )
    grad_cross = cube_scatter(keep, send)
    keep, send, self_query_grad, self_key_grad, self_value_grad = self_back(
        index,
        self_ranges,
        resid_one_grad,
        layer_input,
        self_query,
        self_key,
        self_value,
        self_out,
        self_totals,
        self_full,
        HD,
        columns,
        rows,
    )
    grad_self = cube_scatter(keep, send)
    memory_grad = return_rows(returned, my_starts, tok_rows)
    input_grad = (
        resid_one_grad
        + matmul(self_query_grad, self_full[0].T)
        + matmul(self_key_grad, self_full[1].T)
        + matmul(self_value_grad, self_full[2].T)
    )

    weights = weights[:5] + (expand_bias[None],)
    firsts = (
        attend_input_first,
        attend_output_first,
        expand_weight_first,
        reduce_weight_first,
        norm_vectors_first,
        expand_bias_first[None],
    )
    seconds = (
        attend_input_second,
        attend_output_second,
        expand_weight_second,
        reduce_weight_second,
        norm_vectors_second,
        expand_bias_second[None],
    )
    row_shape = jax.ShapeDtypeStruct((1, 128), f32)
    grad_self, grad_cross, grad_vectors, row = whole_call(
        functools.partial(squares_kernel, model_count, len(grad_self)),
        "squares",
        same(grad_self[:1] * 2) + (jax.ShapeDtypeStruct((8, rows), f32), row_shape),
        *grad_self,
        *grad_cross,
        grad_wide,
        *weights,
    )
    row = small_total(row)
    moved = whole_call(
        functools.partial(moments_kernel, model_count, columns),
        "moments",
        same(weights) * 3 + (row_shape,),
        row,
        grad_self,
        grad_cross,
        grad_wide,
        grad_vectors,
        *weights,
        *firsts,
        *seconds,
    )
    new_firsts, new_seconds, updates = moved[:6], moved[6:12], moved[12:18]
    applied = whole_call(
        apply_kernel,
        "apply",
        same(weights)
        + same(weights[:4], bf16)
        + (jax.ShapeDtypeStruct((2, 128), f32), jax.ShapeDtypeStruct((1, 1), f32)),
        row,
        small_total(moved[18]),
        *weights,
        *updates,
    )
    new_weights = applied[:5] + (applied[5][0],)
    matrix_norms = applied[10][:, :10]

    def turned(values):
        return (values[0], values[1].transpose(0, 2, 1), values[2], values[3].T) + tuple(values[4:])

    new_weights, copies = turned(new_weights), turned(applied[6:10])
    new_firsts, new_seconds = turned(new_firsts), turned(new_seconds)
    return (
        layer_output,
        input_grad,
        memory_grad,
        applied[11][0],
        *new_weights,
        *copies,
        new_firsts[0],
        new_seconds[0],
        new_firsts[1],
        new_seconds[1],
        new_firsts[2],
        new_seconds[2],
        new_firsts[3],
        new_seconds[3],
        new_firsts[4],
        new_seconds[4],
        new_firsts[5][0],
        new_seconds[5][0],
        matrix_norms,
    )


def solution(mesh):
    in_specs = (
        P("dp", None),
        P("dp", "mp"),
        P("dp", None),
        P("dp", None),
        P("dp", None),
        P("dp"),
        P(),
        P(None, "dp", "mp"),
        P(None, "mp", "dp"),
        P("dp", "mp"),
        P("mp", "dp"),
        P(None, "dp"),
        P(("mp", "dp")),
        P(None, "dp", "mp"),
        P(None, "dp", "mp"),
        P(None, "mp", "dp"),
        P(None, "mp", "dp"),
        P("dp", "mp"),
        P("dp", "mp"),
        P("mp", "dp"),
        P("mp", "dp"),
        P(None, "dp"),
        P(None, "dp"),
        P(("mp", "dp")),
        P(("mp", "dp")),
    )
    out_specs = (
        P("dp", None),
        P("dp", None),
        P("dp", "mp"),
        P(),
        P(None, "dp", "mp"),
        P(None, "mp", "dp"),
        P("dp", "mp"),
        P("mp", "dp"),
        P(None, "dp"),
        P(("mp", "dp")),
        P(None, "dp", "mp"),
        P(None, "mp", "dp"),
        P("dp", "mp"),
        P("mp", "dp"),
        P(None, "dp", "mp"),
        P(None, "dp", "mp"),
        P(None, "mp", "dp"),
        P(None, "mp", "dp"),
        P("dp", "mp"),
        P("dp", "mp"),
        P("mp", "dp"),
        P("mp", "dp"),
        P(None, "dp"),
        P(None, "dp"),
        P(("mp", "dp")),
        P(("mp", "dp")),
        P(),
    )
    return jax.shard_map(shards, mesh=mesh, in_specs=in_specs, out_specs=out_specs, check_vma=False)
```

```python
import functools

import jax
import jax.numpy as jnp
from jax import lax
from jax.experimental import pallas as pl
from jax.experimental.pallas import tpu as pltpu
from jax.sharding import PartitionSpec as P

HD = 64
STEP_NUM = 6

norm_eps = 1e-05
adam_eps = 1e-06
first_decay = 0.5
second_decay = 0.5
matrix_decay = 0.01
peak_rate = 0.6
warm_steps = 8.0
clip_norm = 1.0

bf16 = jnp.bfloat16
f32 = jnp.float32
neg_large = -1e30
q_rows = 128
key_rows = 256
pair_lanes = 128


def split_two(values):
    high = values.astype(bf16)
    return high, (values - high.astype(f32)).astype(bf16)


def dot_nn(left_side, right_side):
    return lax.dot_general(left_side, right_side, (((1,), (0,)), ((), ())), preferred_element_type=f32)


def dot_nt(left_side, right_side):
    return lax.dot_general(left_side, right_side, (((1,), (1,)), ((), ())), preferred_element_type=f32)


def dot_tn(left_side, right_side):
    return lax.dot_general(left_side, right_side, (((0,), (0,)), ((), ())), preferred_element_type=f32)


def three(dot, left_pair, right_pair):
    return (
        dot(left_pair[0], right_pair[0])
        + dot(left_pair[1], right_pair[0])
        + dot(left_pair[0], right_pair[1])
    )


def swap_halves(tile):
    return pltpu.roll(tile, pair_lanes // 2, 1)


def parts_of(tile):
    high = tile.astype(bf16).astype(f32)
    return high, tile - high


def query_packs(tile, low_half):
    high, low = parts_of(tile)
    high_swap, low_swap = swap_halves(high), swap_halves(low)
    zero = jnp.zeros_like(tile)
    first = jnp.concatenate(
        [jnp.where(low_half, high, high_swap), jnp.where(low_half, low, zero)], axis=1
    )
    second = jnp.concatenate(
        [jnp.where(low_half, high_swap, high), jnp.where(low_half, low_swap, zero)], axis=1
    )
    return first.astype(bf16), second.astype(bf16)


def key_packs(tile, low_half):
    high, low = parts_of(tile)
    high_swap, low_swap = swap_halves(high), swap_halves(low)
    zero = jnp.zeros_like(tile)
    first = jnp.concatenate(
        [jnp.where(low_half, high, low_swap), jnp.where(low_half, high, zero)], axis=1
    )
    second = jnp.concatenate(
        [jnp.where(low_half, high_swap, low), jnp.where(low_half, high_swap, zero)], axis=1
    )
    return first.astype(bf16), second.astype(bf16)


def both_parts(tile):
    high, low = split_two(tile)
    return jnp.concatenate([high, low], axis=1)


def stack_heads(tile, low_half):
    return jnp.concatenate([jnp.where(low_half, tile, 0.0), jnp.where(low_half, 0.0, tile)], axis=0)


def merge_heads(stacked, low_half):
    return jnp.where(low_half, stacked[:q_rows], stacked[q_rows:])


def folded(dot, left_pair, right_both):
    wide = dot(left_pair[0], right_both)
    return wide[:, :pair_lanes] + wide[:, pair_lanes:] + dot(left_pair[1], right_both[:, :pair_lanes])


def prepare_rows(at, source_ref, low_half, pack_ref, both_ref):
    for pair in range(source_ref.shape[1] // pair_lanes):
        tile = source_ref[at, pair * pair_lanes : (pair + 1) * pair_lanes]
        if pack_ref is not None:
            first, second = key_packs(tile, low_half)
            pack_ref[2 * pair, at, :] = first
            pack_ref[2 * pair + 1, at, :] = second
        if both_ref is not None:
            both_ref[pair, at, :] = both_parts(tile)


def clear_pad(rows, *refs):
    for ref in refs:
        ref[:, rows:, :] = jnp.zeros((ref.shape[0], ref.shape[1] - rows, ref.shape[2]), bf16)


def half_mask(rows):
    return lax.broadcasted_iota(jnp.int32, (rows, pair_lanes), 1) < pair_lanes // 2


def chunks(rows, size, body):
    def one(step, carry):
        body(pl.ds(pl.multiple_of(step * size, size), size))
        return carry

    lax.fori_loop(0, rows // size, one, 0)


def attend_kernel(
    unroll, scale, block_low, block_count,
    q_ref, k_ref, v_ref, low_ref, high_ref,
    o_ref, total_ref,
    kp_ref, vb_ref,
):
    rows, width = q_ref.shape
    lanes = lax.broadcasted_iota(jnp.int32, (q_rows, pair_lanes), 1)
    low_half = lanes < pair_lanes // 2
    clear_pad(rows, kp_ref, vb_ref)

    def before(at):
        prepare_rows(at, k_ref, low_half, kp_ref, None)
        prepare_rows(at, v_ref, low_half, None, vb_ref)

    chunks(rows, q_rows, before)
    groups = width // pair_lanes // unroll
    key_iota = lax.broadcasted_iota(jnp.int32, (q_rows, key_rows), 1)

    def block(index, carry):
        at = pl.ds(pl.multiple_of(index * q_rows, q_rows), q_rows)
        first = low_ref[at, :]
        last = high_ref[at, :]
        for group in range(groups):
            pairs = [group * unroll + u for u in range(unroll)]

            def load(u):
                lanes_of = slice(pairs[u] * pair_lanes, (pairs[u] + 1) * pair_lanes)
                return query_packs(q_ref[at, lanes_of] * scale, low_half)

            def chunk(step, state, held_packs=None):
                start = pl.multiple_of(block_low[index] + step * key_rows, 16)
                here = pl.ds(start, key_rows)
                places = key_iota + start
                bias = jnp.where(jnp.logical_and(places >= first, places < last), 0.0, neg_large)
                bias = jnp.concatenate([bias, bias], axis=0)
                out, found = [], []
                for u, p in enumerate(pairs):
                    query = load(u) if held_packs is None else held_packs[u]
                    found.append(
                        jnp.concatenate(
                            [dot_nt(query[h], kp_ref[2 * p + h, here, :]) for h in range(2)], axis=0
                        )
                    )
                for u, p in enumerate(pairs):
                    scores = bias + found[u]
                    new_top = jnp.max(scores, axis=1, keepdims=True)
                    if state is not None:
                        top, total, held = state[u]
                        new_top = jnp.maximum(top, new_top)
                        shrink = jnp.exp(top - new_top)
                    weights = jnp.exp(scores - new_top)
                    new_total = jnp.sum(weights, axis=1, keepdims=True)
                    new_held = folded(dot_nn, split_two(weights), vb_ref[p, here, :])
                    if state is not None:
                        new_total = total * shrink + new_total
                        new_held = held * shrink + new_held
                    out.append((new_top, new_total, new_held))
                return tuple(out)

            def finish(state):
                tile = total_ref[at, :] if group else jnp.zeros((q_rows, pair_lanes), f32)
                for u, p in enumerate(pairs):
                    top, total, held = state[u]
                    o_ref[at, p * pair_lanes : (p + 1) * pair_lanes] = merge_heads(held / total, low_half)
                    logs = top + jnp.log(total)
                    tile = jnp.where(lanes == 2 * p, logs[:q_rows], tile)
                    tile = jnp.where(lanes == 2 * p + 1, logs[q_rows:], tile)
                total_ref[at, :] = tile

            @pl.when(block_count[index] == 1)
            def _():
                finish(chunk(0, None))

            @pl.when(block_count[index] > 1)
            def _():
                start_state = tuple(
                    (
                        jnp.full((2 * q_rows, 1), neg_large, f32),
                        jnp.zeros((2 * q_rows, 1), f32),
                        jnp.zeros((2 * q_rows, pair_lanes), f32),
                    )
                    for _ in range(unroll)
                )
                packs = [load(u) for u in range(unroll)]
                step = lambda number, state: chunk(number, state, packs)
                finish(lax.fori_loop(0, block_count[index], step, start_state))

        return carry

    lax.fori_loop(0, rows // q_rows, block, 0)


def attend_back_blocks(
    unroll, scale, block_low, block_count,
    q_ref, o_ref, g_ref, total_ref, low_ref, high_ref,
    dq_ref, kp_ref, vp_ref, kb_ref, dk_sum, dv_sum,
):
    rows, width = q_ref.shape
    lanes = lax.broadcasted_iota(jnp.int32, (q_rows, pair_lanes), 1)
    low_half = lanes < pair_lanes // 2
    groups = width // pair_lanes // unroll
    key_iota = lax.broadcasted_iota(jnp.int32, (q_rows, key_rows), 1)

    def block(index, carry):
        at = pl.ds(pl.multiple_of(index * q_rows, q_rows), q_rows)
        first = low_ref[at, :]
        last = high_ref[at, :]
        total_tile = total_ref[at, :]
        for group in range(groups):
            pairs = [group * unroll + u for u in range(unroll)]

            def column(mask, value):
                return jnp.sum(jnp.where(mask, value, 0.0), axis=1, keepdims=True)

            def load(u):
                p = pairs[u]
                lanes_of = slice(p * pair_lanes, (p + 1) * pair_lanes)
                query = q_ref[at, lanes_of] * scale
                grad = g_ref[at, lanes_of]
                product = grad * o_ref[at, lanes_of]
                dots = [column(low_half, product), column(jnp.logical_not(low_half), product)]
                logs = [column(lanes == 2 * p, total_tile), column(lanes == 2 * p + 1, total_tile)]
                return (
                    query_packs(query, low_half),
                    query_packs(grad, low_half),
                    both_parts(stack_heads(query, low_half)),
                    both_parts(stack_heads(grad, low_half)),
                    jnp.concatenate(logs, axis=0),
                    jnp.concatenate(dots, axis=0),
                )

            def chunk(step, state, held_packs=None):
                start = pl.multiple_of(block_low[index] + step * key_rows, 16)
                here = pl.ds(start, key_rows)
                places = key_iota + start
                bias = jnp.where(jnp.logical_and(places >= first, places < last), 0.0, neg_large)
                bias = jnp.concatenate([bias, bias], axis=0)
                out, packs, found = [], [], []
                for u, p in enumerate(pairs):
                    packs.append(load(u) if held_packs is None else held_packs[u])
                    found.append(
                        [
                            jnp.concatenate(
                                [dot_nt(packs[u][k][h], ref[2 * p + h, here, :]) for h in range(2)], axis=0
                            )
                            for k, ref in enumerate((kp_ref, vp_ref))
                        ]
                    )
                for u, p in enumerate(pairs):
                    lanes_of = slice(p * pair_lanes, (p + 1) * pair_lanes)
                    _, _, query_both, grad_both, logs, dots = packs[u]
                    weights = jnp.exp(bias + found[u][0] - logs)
                    grad_scores = split_two(weights * (found[u][1] - dots))
                    new_state = folded(dot_nn, grad_scores, kb_ref[p, here, :])
                    out.append(new_state if state is None else state[u] + new_state)
                    dk_sum[here, lanes_of] += folded(dot_tn, grad_scores, query_both)
                    dv_sum[here, lanes_of] += folded(dot_tn, split_two(weights), grad_both)
                return tuple(out)

            def finish(state):
                for u, p in enumerate(pairs):
                    dq_ref[at, p * pair_lanes : (p + 1) * pair_lanes] = merge_heads(state[u], low_half) * scale

            @pl.when(block_count[index] == 1)
            def _():
                finish(chunk(0, None))

            @pl.when(block_count[index] > 1)
            def _():
                start_state = tuple(jnp.zeros((2 * q_rows, pair_lanes), f32) for _ in range(unroll))
                packs = [load(u) for u in range(unroll)]
                step = lambda number, state: chunk(number, state, packs)
                finish(lax.fori_loop(0, block_count[index], step, start_state))

        return carry

    lax.fori_loop(0, rows // q_rows, block, 0)


def own_lanes(ref, at, model, columns):
    if columns % pair_lanes == 0:
        return ref[at, pl.ds(pl.multiple_of(model * columns, pair_lanes), columns)]
    start = model * columns
    base = pl.multiple_of(start // pair_lanes * pair_lanes, pair_lanes)
    tile = ref[at, pl.ds(base, pair_lanes)]
    return pltpu.roll(tile, lax.rem(pair_lanes - lax.rem(start, pair_lanes), pair_lanes), 1)[:, :columns]


def norm_parts(values):
    centred = values - jnp.mean(values, axis=1, keepdims=True)
    scale = lax.rsqrt(jnp.mean(centred * centred, axis=1, keepdims=True) + norm_eps)
    return centred * scale, scale


def norm_back(grad, normal, scale, gain):
    inner = grad * gain
    return (
        inner
        - jnp.mean(inner, axis=1, keepdims=True)
        - normal * jnp.mean(inner * normal, axis=1, keepdims=True)
    ) * scale


def column_sum(value):
    return jnp.sum(value, axis=0, keepdims=True)


def hand_out(index_ref, grads_ref, keep_ref, send_ref, rows, extra_ref=None):
    me = index_ref[0]
    odd = lax.rem(me, 2)
    for r in range(keep_ref.shape[0]):
        pair = 2 * ((me // 2) ^ r)
        for ref, which in ((keep_ref, pair + odd), (send_ref, pair + 1 - odd)):
            ref[r, :rows, :] = grads_ref[pl.ds(pl.multiple_of(which * rows, rows), rows), :]
            if extra_ref is not None:
                ref[r, rows:, :] = extra_ref[pl.ds(which, 1)][0]


def cross_back_kernel(
    unroll, scale, columns, rows_of, bias_rows, index_ref, block_low, block_count,
    g_ref, two_ref, one_ref, mem_ref, q_ref, k_ref, v_ref, o_ref, total_ref, low_ref, high_ref,
    w_ref, vec_ref, sums_ref, bias_ref,
    keep_ref, send_ref, resid_ref, mem_grad_ref,
    kp_ref, vp_ref, kb_ref, dk_sum, dv_sum, dq_ref, go_ref, two_grad_ref, woh, wol, wqh, wql, grads, totals, parts,
):
    rows, width = q_ref.shape
    model = index_ref[1]
    mask = half_mask(256)
    clear_pad(rows, kp_ref, vp_ref, kb_ref)
    dk_sum[...] = jnp.zeros_like(dk_sum)
    dv_sum[...] = jnp.zeros_like(dv_sum)
    woh[...], wol[...] = split_two(w_ref[3])
    wqh[...], wql[...] = split_two(w_ref[0])
    totals[...] = sums_ref[...]
    grads[...] = jnp.zeros_like(grads)

    def before(at):
        normal, spread = norm_parts(two_ref[at, :])
        grad = g_ref[at, :]
        resid = norm_back(grad, normal, spread, vec_ref[0, 1:2, :])
        totals[1:2, :] += column_sum(grad * normal)
        totals[4:5, :] += column_sum(grad)
        two_grad_ref[at, :] = resid
        go_ref[at, :] = three(dot_nn, split_two(resid), (woh[...], wol[...]))
        prepare_rows(at, k_ref, mask, kp_ref, kb_ref)
        prepare_rows(at, v_ref, mask, vp_ref, None)

    chunks(rows, 256, before)
    attend_back_blocks(
        unroll, scale, block_low, block_count,
        q_ref, o_ref, go_ref, total_ref, low_ref, high_ref,
        dq_ref, kp_ref, vp_ref, kb_ref, dk_sum, dv_sum,
    )

    def after(at):
        resid = two_grad_ref[at, :]
        grad = resid + three(dot_nt, split_two(dq_ref[at, :]), (wqh[...], wql[...]))
        normal, spread = norm_parts(one_ref[at, :])
        gain = vec_ref[0, 0:1, :]
        resid_ref[at, :] = norm_back(grad, normal, spread, gain)
        totals[0:1, :] += column_sum(grad * normal)
        totals[3:4, :] += column_sum(grad)
        source = split_two(normal * gain + vec_ref[0, 3:4, :])
        memory = split_two(mem_ref[at, :])
        dk = dk_sum[at, :]
        dv = dv_sum[at, :]
        grads[:, :columns] += three(dot_tn, source, split_two(own_lanes(dq_ref, at, model, columns)))
        both = jnp.concatenate([own_lanes(ref, at, model, columns) for ref in (dk_sum, dv_sum)], axis=1)
        grads[:, columns : 3 * columns] += three(dot_tn, memory, split_two(both))
        grads[:, 3 * columns :] += three(
            dot_tn, split_two(resid), split_two(own_lanes(o_ref, at, model, columns))
        )
        slice_of = pl.ds(pl.multiple_of(model * columns, columns), columns)
        mem_grad_ref[at, :] = three(dot_nt, split_two(dk), split_two(w_ref[1, slice_of, :])) + three(
            dot_nt, split_two(dv), split_two(w_ref[2, slice_of, :])
        )

    chunks(rows, 256, after)
    parts[...] = jnp.zeros_like(parts)
    for j in range(parts.shape[0]):
        parts[j, :, :rows_of] = totals[:, j * rows_of : (j + 1) * rows_of]
        parts[j, 7:8, :bias_rows] = bias_ref[:, j * bias_rows : (j + 1) * bias_rows]
    hand_out(index_ref, grads, keep_ref, send_ref, rows_of, parts)


def self_back_kernel(
    unroll, scale, columns, rows_of, index_ref, block_low, block_count,
    g_ref, x_ref, q_ref, k_ref, v_ref, o_ref, total_ref, low_ref, high_ref, w_ref,
    keep_ref, send_ref, dq_ref, dk_ref, dv_ref,
    kp_ref, vp_ref, kb_ref, dk_sum, dv_sum, go_ref, woh, wol, grads,
):
    rows, width = q_ref.shape
    model = index_ref[1]
    mask = half_mask(256)
    clear_pad(rows, kp_ref, vp_ref, kb_ref)
    dk_sum[...] = jnp.zeros_like(dk_sum)
    dv_sum[...] = jnp.zeros_like(dv_sum)
    woh[...], wol[...] = split_two(w_ref[3])
    grads[...] = jnp.zeros_like(grads)

    def before(at):
        go_ref[at, :] = three(dot_nn, split_two(g_ref[at, :]), (woh[...], wol[...]))
        prepare_rows(at, k_ref, mask, kp_ref, kb_ref)
        prepare_rows(at, v_ref, mask, vp_ref, None)

    chunks(rows, 256, before)
    attend_back_blocks(
        unroll, scale, block_low, block_count,
        q_ref, o_ref, go_ref, total_ref, low_ref, high_ref,
        dq_ref, kp_ref, vp_ref, kb_ref, dk_sum, dv_sum,
    )

    def after(at):
        source = split_two(x_ref[at, :])
        dk_ref[at, :] = dk_sum[at, :]
        dv_ref[at, :] = dv_sum[at, :]
        every = [own_lanes(ref, at, model, columns) for ref in (dq_ref, dk_sum, dv_sum)]
        grads[:, : 3 * columns] += three(dot_tn, source, split_two(jnp.concatenate(every, axis=1)))
        grads[:, 3 * columns :] += three(
            dot_tn, split_two(g_ref[at, :]), split_two(own_lanes(o_ref, at, model, columns))
        )

    chunks(rows, 256, after)
    hand_out(index_ref, grads, keep_ref, send_ref, rows_of)


VM = functools.partial(pl.BlockSpec, memory_space=pltpu.VMEM)
SM = functools.partial(pl.BlockSpec, memory_space=pltpu.SMEM)


def attend(queries, keys_in, values_in, ranges, head_size, unroll=4):
    block_low, block_count, low, high = ranges
    rows, width = queries.shape
    pad_rows = keys_in.shape[0] + key_rows
    return pl.pallas_call(
        functools.partial(attend_kernel, unroll, head_size ** -0.5),
        out_shape=(
            jax.ShapeDtypeStruct((rows, width), f32),
            jax.ShapeDtypeStruct((rows, pair_lanes), f32),
        ),
        in_specs=[SM(), SM()] + [VM()] * 5,
        out_specs=(VM(), VM()),
        scratch_shapes=[
            pltpu.VMEM((width // 64, pad_rows, 2 * pair_lanes), bf16),
            pltpu.VMEM((width // pair_lanes, pad_rows, 2 * pair_lanes), bf16),
        ],
        compiler_params=pltpu.CompilerParams(vmem_limit_bytes=48 << 20),
        cost_estimate=pl.CostEstimate(flops=12 * rows * key_rows * width, bytes_accessed=16 * rows * width, transcendentals=rows * key_rows * 8),
        name="attend",
    )(block_low, block_count, queries, keys_in, values_in, low, high)


def back_scratch(rows, width):
    pad_rows = rows + key_rows
    return [
        pltpu.VMEM((width // 64, pad_rows, 2 * pair_lanes), bf16),
        pltpu.VMEM((width // 64, pad_rows, 2 * pair_lanes), bf16),
        pltpu.VMEM((width // pair_lanes, pad_rows, 2 * pair_lanes), bf16),
        pltpu.VMEM((pad_rows, width), f32),
        pltpu.VMEM((pad_rows, width), f32),
    ]


def cross_back(
    index, ranges, grad, two, one, memory, queries, keys_in, values_in, outputs, totals,
    matrices, vectors, sums, bias, head_size, columns, rows_of, bias_rows, unroll=4,
):
    block_low, block_count, low, high = ranges
    rows, width = queries.shape
    data = width // rows_of
    block = jax.ShapeDtypeStruct((data // 2, rows_of + 8, 4 * columns), f32)
    return pl.pallas_call(
        functools.partial(cross_back_kernel, unroll, head_size ** -0.5, columns, rows_of, bias_rows),
        out_shape=(
            block,
            block,
            jax.ShapeDtypeStruct((rows, width), f32),
            jax.ShapeDtypeStruct((rows, columns), f32),
        ),
        in_specs=[SM()] * 3 + [VM()] * 15,
        out_specs=(VM(),) * 4,
        scratch_shapes=back_scratch(rows, width)
        + [pltpu.VMEM((rows, width), f32)] * 3
        + [pltpu.VMEM((width, width), bf16)] * 4
        + [
            pltpu.VMEM((width, 4 * columns), f32),
            pltpu.VMEM((8, width), f32),
            pltpu.VMEM((data, 8, 4 * columns), f32),
        ],
        compiler_params=pltpu.CompilerParams(vmem_limit_bytes=60 << 20),
        cost_estimate=pl.CostEstimate(flops=30 << 30, bytes_accessed=30 << 20, transcendentals=rows * key_rows * 8),
        name="cross_back",
    )(
        index, block_low, block_count, grad, two, one, memory, queries, keys_in, values_in, outputs, totals,
        low, high, matrices, vectors, sums, bias,
    )


def self_back(
    index, ranges, grad, source, queries, keys_in, values_in, outputs, totals, matrices,
    head_size, columns, rows_of, unroll=4,
):
    block_low, block_count, low, high = ranges
    rows, width = queries.shape
    data = width // rows_of
    block = jax.ShapeDtypeStruct((data // 2, rows_of, 4 * columns), f32)
    return pl.pallas_call(
        functools.partial(self_back_kernel, unroll, head_size ** -0.5, columns, rows_of),
        out_shape=(block, block) + (jax.ShapeDtypeStruct((rows, width), f32),) * 3,
        in_specs=[SM()] * 3 + [VM()] * 10,
        out_specs=(VM(),) * 5,
        scratch_shapes=back_scratch(rows, width)
        + [pltpu.VMEM((rows, width), f32)]
        + [pltpu.VMEM((width, width), bf16)] * 2
        + [pltpu.VMEM((width, 4 * columns), f32)],
        compiler_params=pltpu.CompilerParams(vmem_limit_bytes=60 << 20),
        cost_estimate=pl.CostEstimate(flops=30 << 30, bytes_accessed=30 << 20, transcendentals=rows * key_rows * 8),
        name="self_back",
    )(
        index, block_low, block_count, grad, source, queries, keys_in, values_in, outputs, totals,
        low, high, matrices,
    )


def key_ranges(query_lengths, key_lengths, rows):
    query_ends = jnp.cumsum(query_lengths)
    query_starts = query_ends - query_lengths
    places = jnp.arange(rows, dtype=jnp.int32)
    low = jnp.sum(jnp.where(query_ends[None, :] <= places[:, None], key_lengths[None, :], 0), axis=1)
    high = jnp.sum(jnp.where(query_starts[None, :] <= places[:, None], key_lengths[None, :], 0), axis=1)
    block_low = low[::q_rows] // 16 * 16
    block_high = high[q_rows - 1 :: q_rows]
    block_count = (block_high - block_low + key_rows - 1) // key_rows
    return block_low, block_count, low[:, None], high[:, None]


def matmul(left_side, right_side):
    return jnp.dot(left_side, right_side, precision=lax.Precision.HIGH, preferred_element_type=f32)


def layer_norm(values, gain_row, shift_row):
    centre_mean = jnp.mean(values, axis=-1, keepdims=True)
    centred = values - centre_mean
    variance = jnp.mean(centred * centred, axis=-1, keepdims=True)
    return centred * lax.rsqrt(variance + norm_eps) * gain_row + shift_row


def flip(value, axis, distance):
    pairs = [(i, i ^ distance) for i in range(lax.axis_size(axis))]
    return lax.ppermute(value, axis, pairs)


def tree_total(pieces):
    while len(pieces) > 1:
        pieces = [pieces[i] + pieces[i + 1] for i in range(0, len(pieces), 2)]
    return pieces[0]


def small_total(value):
    value = value + flip(value, "dp", 1)
    others = lax.axis_size("dp") // 2
    value = tree_total([value] + [flip(value, "dp", 2 * r) for r in range(1, others)])
    models = lax.axis_size("mp")
    return tree_total([value] + [flip(value, "mp", r) for r in range(1, models)])


def ring_gather(own):
    count = lax.axis_size("mp")
    return [own] + [
        lax.ppermute(own, "mp", [(i, (i + step) % count) for i in range(count)])
        for step in range(1, count)
    ]


def ring_order(ring):
    count = len(ring)
    me = lax.axis_index("mp")
    found = []
    for place in range(count):
        value = ring[0]
        for step in range(1, count):
            value = jnp.where(me == (place + step) % count, ring[step], value)
        found.append(value)
    return found


def even_gather(own):
    return [own] + [flip(own, "dp", r) for r in range(2, lax.axis_size("dp"), 2)]


def odd_gather(even):
    odd = [flip(value, "dp", 1) for value in even]
    return [value for pair in zip(even, odd) for value in pair]


def place_kernel(parts, rows, columns, bias_rows, index_ref, *refs):
    pieces, (full_ref, vec_ref) = refs[:-2], refs[-2:]
    me, model = index_ref[0], index_ref[1]
    models = pieces[0].shape[0]
    width = vec_ref.shape[2]
    pad = jnp.zeros((8, width - columns), f32)
    bias_row = lax.broadcasted_iota(jnp.int32, (8, width), 0) == 7
    vec_ref[...] = jnp.zeros_like(vec_ref)
    for r, piece in enumerate(pieces):
        whose = me ^ r
        at = pl.ds(pl.multiple_of(whose * rows, rows), rows)
        for place in range(models):
            slot = lax.rem(model - place + models, models)
            for part in range(parts):
                full_ref[part, at, place * columns : (place + 1) * columns] = piece[
                    slot, part * rows : (part + 1) * rows, :
                ]
            values = jnp.concatenate([piece[slot, parts * rows :, :], pad], axis=1)
            moved = pltpu.roll(values, whose * rows, 1)
            if rows != bias_rows:
                moved = jnp.where(bias_row, pltpu.roll(values, whose * bias_rows, 1), moved)
            vec_ref[place] += moved


def place(pieces, index, parts, rows, columns, bias_rows):
    models, count = pieces[0].shape[0], len(pieces)
    return pl.pallas_call(
        functools.partial(place_kernel, parts, rows, columns, bias_rows),
        out_shape=(
            jax.ShapeDtypeStruct((parts, rows * count, columns * models), f32),
            jax.ShapeDtypeStruct((models, 8, columns * models), f32),
        ),
        in_specs=[SM()] + [VM()] * count,
        out_specs=(VM(), VM()),
        compiler_params=pltpu.CompilerParams(vmem_limit_bytes=40 << 20),
        name="place",
    )(index, *pieces)


def gelu_both(values):
    inner = 0.7978845608028654 * (values + 0.044715 * values * values * values)
    bent = jnp.tanh(inner)
    half = 0.5 * (1.0 + bent)
    slope = half + 0.5 * values * (1.0 - bent * bent) * (
        0.7978845608028654 * (1.0 + 3.0 * 0.044715 * values * values)
    )
    return values * half, slope


def wide_kernel(
    rows, model_ref, z_ref, g_ref, wide_ref, all_vec_ref,
    out_ref, second_ref, grads_ref, sums_ref, bias_grad_ref,
    eh_ref, el_ref, rh_ref, rl_ref, slope_ref, xh_ref, xl_ref, bh_ref, bl_ref,
):
    tokens, width = z_ref.shape
    data, models, _, units = wide_ref.shape
    model = model_ref[0]
    vec_ref = all_vec_ref.at[0]
    block = xh_ref.shape[0]

    def load(step, carry):
        which, part = step // models, step % models
        at = pl.ds(pl.multiple_of(which * rows, rows), rows)
        to = pl.ds(pl.multiple_of(part * units, units), units)
        eh_ref[at, to], el_ref[at, to] = split_two(wide_ref[which, part, :rows, :])
        rh_ref[at, to], rl_ref[at, to] = split_two(wide_ref[which, part, rows:, :])
        return carry

    lax.fori_loop(0, data * models, load, 0)
    sums_ref[...] = jnp.zeros_like(sums_ref)
    bias_grad_ref[...] = jnp.zeros_like(bias_grad_ref)
    grads_ref[...] = jnp.zeros_like(grads_ref)

    gain = vec_ref[2:3, :]
    half = block // 2
    halves = [slice(0, half), slice(half, block)]

    def chunk(step, carry):
        whole = pl.ds(pl.multiple_of(step * block, block), block)
        ats = [pl.ds(pl.multiple_of(step * block + h * half, half), half) for h in range(2)]
        products, resids, reduced = [None] * 2, [None] * 2, [None] * 2

        def enter(h):
            products[h] = three(dot_nn, split_two(z_ref[ats[h], :]), (eh_ref[...], el_ref[...]))

        def bend(h):
            for part in range(models):
                to = slice(part * units, (part + 1) * units)
                value, slope = gelu_both(products[h][:, to] + all_vec_ref[part, 7:8, :units])
                slope_ref[halves[h], to] = slope
                xh_ref[halves[h], to], xl_ref[halves[h], to] = split_two(value)

        def leave(h):
            reduced[h] = three(
                dot_nt, (xh_ref[halves[h], :], xl_ref[halves[h], :]), (rh_ref[...], rl_ref[...])
            )

        def turn(h):
            at = ats[h]
            normal, scale = norm_parts(z_ref[at, :] + vec_ref[6:7, :] + reduced[h])
            out_ref[at, :] = normal * gain + vec_ref[5:6, :]
            grad = g_ref[at, :]
            resids[h] = norm_back(grad, normal, scale, gain)
            sums_ref[2:3, :] += column_sum(grad * normal)
            sums_ref[5:6, :] += column_sum(grad)
            sums_ref[6:7, :] += column_sum(resids[h])

        def reenter(h):
            products[h] = three(dot_nn, split_two(resids[h]), (rh_ref[...], rl_ref[...]))

        def unbend(h):
            for part in range(models):
                to = slice(part * units, (part + 1) * units)
                back = products[h][:, to] * slope_ref[halves[h], to]
                slope_ref[halves[h], to] = back
                bh_ref[halves[h], to], bl_ref[halves[h], to] = split_two(back)

        def finish(h):
            return three(dot_nt, (bh_ref[halves[h], :], bl_ref[halves[h], :]), (eh_ref[...], el_ref[...]))

        enter(0)
        enter(1)
        bend(0)
        leave(0)
        bend(1)
        leave(1)
        turn(0)
        reenter(0)
        turn(1)
        reenter(1)
        unbend(0)
        more = finish(0)
        unbend(1)
        last = finish(1)
        second_ref[ats[0], :] = resids[0] + more
        second_ref[ats[1], :] = resids[1] + last
        to = pl.ds(pl.multiple_of(model * units, units), units)
        bias_grad_ref[...] += column_sum(slope_ref[:, to])
        grads_ref[:, :units] += three(dot_tn, split_two(z_ref[whole, :]), (bh_ref[:, to], bl_ref[:, to]))
        grads_ref[:, units:] += three(
            dot_tn, split_two(jnp.concatenate(resids, axis=0)), (xh_ref[:, to], xl_ref[:, to])
        )
        return carry

    lax.fori_loop(0, tokens // block, chunk, 0)


def feed_forward(model, source, grad, wide, vectors, rows):
    tokens, width = source.shape
    data, models, _, units = wide.shape
    block = min(512, tokens)
    return pl.pallas_call(
        functools.partial(wide_kernel, rows),
        out_shape=(
            jax.ShapeDtypeStruct((tokens, width), f32),
            jax.ShapeDtypeStruct((tokens, width), f32),
            jax.ShapeDtypeStruct((width, 2 * units), f32),
            jax.ShapeDtypeStruct((8, width), f32),
            jax.ShapeDtypeStruct((1, units), f32),
        ),
        in_specs=[SM()] + [VM()] * 4,
        out_specs=(VM(),) * 5,
        scratch_shapes=[pltpu.VMEM((width, models * units), bf16)] * 4
        + [
            pltpu.VMEM((block, models * units), f32),
        ]
        + [pltpu.VMEM((block, models * units), bf16)] * 4,
        compiler_params=pltpu.CompilerParams(vmem_limit_bytes=60 << 20),
        cost_estimate=pl.CostEstimate(
            flops=27 * tokens * width * models * units, bytes_accessed=24 << 20, transcendentals=tokens * models * units
        ),
        name="feed_forward",
    )(model[None], source, grad, wide, vectors)


def cell(row, lane):
    return jnp.sum(
        jnp.where(lax.broadcasted_iota(jnp.int32, row.shape, 1) == lane, row, 0.0), axis=1, keepdims=True
    )


def total_of(value):
    return jnp.sum(jnp.sum(value, axis=1, keepdims=True), axis=0, keepdims=True)


def put(row, lane, value):
    return jnp.where(lax.broadcasted_iota(jnp.int32, row.shape, 1) == lane, value, row)


def part_row(pieces, divisor):
    row = jnp.zeros((1, 128), f32)
    for number, value in enumerate(pieces):
        total = total_of(value * value)
        row = put(row, number, total / divisor if 10 <= number < 17 else total)
    return row


def part_list(arrays):
    return (
        [arrays[0][i] for i in range(arrays[0].shape[0])]
        + [arrays[1][i] for i in range(arrays[1].shape[0])]
        + [arrays[2][...], arrays[3][...]]
        + [arrays[4][i : i + 1, :] for i in range(arrays[4].shape[0])]
        + [arrays[5][...]]
    )


def squares_kernel(divisor, count, *refs):
    self_pieces, cross_pieces, rest = refs[:count], refs[count : 2 * count], refs[2 * count :]
    wide, weights, (self_ref, cross_ref, vector_ref, row_ref) = rest[0][...], rest[1:-4], rest[-4:]
    rows = self_ref.shape[0]
    value = tree_total([piece[...] for piece in self_pieces])
    both = tree_total([piece[...] for piece in cross_pieces])
    cross, vectors = both[:rows], both[rows:, :rows]
    self_ref[...] = value
    cross_ref[...] = cross
    vector_ref[...] = vectors
    total = total_of(value * value) + total_of(cross * cross) + total_of(wide * wide)
    norms = vectors[:7]
    last = vectors[7:8]
    total = total + total_of(norms * norms) / divisor + total_of(last * last)
    row_ref[...] = put(part_row(part_list(weights), divisor), 18, total)


def moments_kernel(divisor, columns, row_ref, *refs):
    grads, rest = refs[:4], refs[4:]
    weights, firsts, seconds = rest[:6], rest[6:12], rest[12:18]
    new_firsts, new_seconds, updates, out_row = rest[18:24], rest[24:30], rest[30:36], rest[36]
    units = rest[2].shape[1]
    bias_rows = rest[5].shape[1]
    norm = jnp.sqrt(cell(row_ref[...], 18))
    clip = jnp.minimum(1.0, clip_norm / norm)
    first_fix = 1.0 - first_decay**STEP_NUM
    second_fix = 1.0 - second_decay**STEP_NUM

    def step(grad, weight, first, second, decay):
        clipped = grad * clip
        one = first_decay * first + (1.0 - first_decay) * clipped
        two = second_decay * second + (1.0 - second_decay) * clipped * clipped
        return one, two, one / first_fix / (jnp.sqrt(two / second_fix) + adam_eps) + decay * weight

    squares = []

    def store(number, at, grad, decay):
        one, two, update = step(
            grad, weights[number][at], firsts[number][at], seconds[number][at], decay
        )
        new_firsts[number][at] = one
        new_seconds[number][at] = two
        updates[number][at] = update
        return update

    for number in range(2):
        for which in range(3):
            store(0, 3 * number + which, grads[number][:, which * columns : (which + 1) * columns], matrix_decay)
    for number in range(2):
        store(1, number, grads[number][:, 3 * columns : 4 * columns], matrix_decay)
    store(2, slice(None), grads[2][:, :units], matrix_decay)
    store(3, slice(None), grads[2][:, units:], matrix_decay)
    store(4, slice(None), grads[3][:7, :], 0.0)
    store(5, slice(None), grads[3][7:8, :bias_rows], 0.0)
    out_row[...] = part_row(part_list(updates), divisor)


def apply_kernel(weight_row_ref, update_row_ref, *refs):
    weights, updates, new, copies = refs[:6], refs[6:12], refs[12:18], refs[18:22]
    norms_ref, grad_norm_ref = refs[22:]
    rate = peak_rate * min(STEP_NUM / warm_steps, (warm_steps / STEP_NUM) ** 0.5)
    weight_row, update_row = jnp.sqrt(weight_row_ref[...]), jnp.sqrt(update_row_ref[...])
    lanes = lax.broadcasted_iota(jnp.int32, weight_row.shape, 1)
    ratios = rate * (weight_row / jnp.where(lanes < 18, update_row, 1.0))

    def store(number, at, part):
        value = weights[number][at] - cell(ratios, part) * updates[number][at]
        new[number][at] = value
        if number < 4:
            copies[number][at] = value.astype(bf16)

    for which in range(6):
        store(0, which, which)
    for which in range(2):
        store(1, which, 6 + which)
    store(2, slice(None), 8)
    store(3, slice(None), 9)
    for which in range(7):
        store(4, slice(which, which + 1), 10 + which)
    store(5, slice(None), 17)
    norms_ref[0:1, :] = weight_row
    norms_ref[1:2, :] = update_row
    grad_norm_ref[...] = cell(weight_row, 18)


def same(arrays, dtype=f32):
    return tuple(jax.ShapeDtypeStruct(value.shape, dtype) for value in arrays)


def whole_call(kernel, name, out_shape, *arrays):
    return pl.pallas_call(
        kernel,
        out_shape=out_shape,
        in_specs=[VM()] * len(arrays),
        out_specs=jax.tree.map(lambda _: VM(), out_shape),
        compiler_params=pltpu.CompilerParams(vmem_limit_bytes=40 << 20),
        name=name,
    )(*arrays)


def pack_kernel(cap, starts_ref, source_ref, packed_ref, padded_ref):
    rows = source_ref.shape[0]
    padded_ref[:rows, :] = source_ref[...]
    padded_ref[rows:, :] = jnp.zeros((padded_ref.shape[0] - rows, source_ref.shape[1]), f32)

    def one(target, carry):
        packed_ref[pl.ds(target, 1)] = padded_ref[pl.ds(starts_ref[target], cap), :][None]
        return carry

    lax.fori_loop(0, packed_ref.shape[0], one, 0)


def pack_rows(source, starts, cap):
    rows, width = source.shape
    return pl.pallas_call(
        functools.partial(pack_kernel, cap),
        out_shape=jax.ShapeDtypeStruct((starts.shape[0], cap, width), f32),
        in_specs=[SM(), VM()],
        out_specs=VM(),
        scratch_shapes=[pltpu.VMEM((rows + cap, width), f32)],
        name="pack_rows",
    )(starts, source)


def unpack_kernel(slots_ref, arrived_ref, out_ref):
    def one(step, carry):
        for k in range(8):
            row = step * 8 + k
            out_ref[pl.ds(row, 1), :] = arrived_ref[pl.ds(slots_ref[row], 1), :]
        return carry

    lax.fori_loop(0, out_ref.shape[0] // 8, one, 0)


def unpack_rows(arrived, slots):
    return pl.pallas_call(
        unpack_kernel,
        out_shape=jax.ShapeDtypeStruct((slots.shape[0], arrived.shape[1]), f32),
        in_specs=[SM(), VM()],
        out_specs=VM(),
        name="unpack_rows",
    )(slots, arrived)


def place_back_kernel(slots_ref, grads_ref, out_ref):
    out_ref[...] = jnp.zeros_like(out_ref)

    def one(step, carry):
        for k in range(8):
            row = step * 8 + k
            out_ref[pl.ds(slots_ref[row], 1), :] = grads_ref[pl.ds(row, 1), :]
        return carry

    lax.fori_loop(0, grads_ref.shape[0] // 8, one, 0)


def place_back(grads_in, slots, total):
    return pl.pallas_call(
        place_back_kernel,
        out_shape=jax.ShapeDtypeStruct((total, grads_in.shape[1]), f32),
        in_specs=[SM(), VM()],
        out_specs=VM(),
        name="place_back",
    )(slots, grads_in)


def return_kernel(starts_ref, returned_ref, out_ref, padded_ref):
    cap = returned_ref.shape[1]

    def one(target, carry):
        padded_ref[pl.ds(starts_ref[target], cap), :] = returned_ref[pl.ds(target, 1)][0]
        return carry

    lax.fori_loop(0, returned_ref.shape[0], one, 0)
    out_ref[...] = padded_ref[: out_ref.shape[0], :]


def return_rows(returned, starts, rows):
    _, cap, width = returned.shape
    return pl.pallas_call(
        return_kernel,
        out_shape=jax.ShapeDtypeStruct((rows, width), f32),
        in_specs=[SM(), VM()],
        out_specs=VM(),
        scratch_shapes=[pltpu.VMEM((rows + cap, width), f32)],
        name="return_rows",
    )(starts, returned)


def cube_scatter(both):
    return [both[0]] + [flip(both[r], "dp", 2 * r) for r in range(1, both.shape[0])]


def shards(
    layer_input,
    encoder_memory,
    output_grad,
    target_lengths,
    memory_lengths,
    source_slots,
    pair_counts,
    attend_input,
    attend_output,
    expand_weight,
    reduce_weight,
    norm_vectors,
    expand_bias,
    attend_input_first,
    attend_input_second,
    attend_output_first,
    attend_output_second,
    expand_weight_first,
    expand_weight_second,
    reduce_weight_first,
    reduce_weight_second,
    norm_vectors_first,
    norm_vectors_second,
    expand_bias_first,
    expand_bias_second,
):
    data_count = lax.axis_size("dp")
    model_count = lax.axis_size("mp")
    me = lax.axis_index("dp")
    model = lax.axis_index("mp")
    tok_rows, width = layer_input.shape
    rows, columns = attend_input.shape[1:]
    units = expand_weight.shape[1]
    attend_output, attend_output_first, attend_output_second = [
        value.transpose(0, 2, 1) for value in (attend_output, attend_output_first, attend_output_second)
    ]
    reduce_weight, reduce_weight_first, reduce_weight_second = [
        value.T for value in (reduce_weight, reduce_weight_first, reduce_weight_second)
    ]
    weights = (attend_input, attend_output, expand_weight, reduce_weight, norm_vectors, expand_bias)

    extra_slots = tok_rows // 16
    slot_cap = (tok_rows - data_count // 4 * extra_slots) // data_count + extra_slots
    my_counts = lax.dynamic_index_in_dim(pair_counts, me, 0, keepdims=False)
    my_starts = jnp.cumsum(my_counts) - my_counts
    arrived = lax.all_to_all(
        pack_rows(encoder_memory, my_starts, slot_cap), "dp", split_axis=0, concat_axis=0, tiled=True
    )

    bias_rows = expand_bias.shape[0]
    vectors = jnp.concatenate(
        [
            jnp.pad(norm_vectors, ((0, 0), (0, columns - rows))),
            jnp.pad(expand_bias[None], ((0, 0), (0, columns - bias_rows))),
        ],
        axis=0,
    )
    own_self = jnp.concatenate(
        [attend_input[:3].reshape(3 * rows, columns), attend_output[0], vectors], axis=0
    )
    own_cross = jnp.concatenate(
        [attend_input[3:].reshape(3 * rows, columns), attend_output[1], vectors], axis=0
    )
    own_wide = jnp.concatenate([expand_weight, reduce_weight], axis=0)
    index = jnp.stack([me, model])
    together = lax.optimization_barrier
    memory_own = unpack_rows(arrived.reshape(data_count * slot_cap, columns), source_slots)
    self_ring, own_cross, memory_own = together((ring_gather(own_self), own_cross, memory_own))
    self_even, cross_ring = together((even_gather(jnp.stack(self_ring)), ring_gather(own_cross)))
    memory_ring = ring_gather(memory_own)
    memory_ring[1], own_wide = together((memory_ring[1], own_wide))
    all_wide = lax.all_gather(own_wide, ("dp", "mp"))
    self_pieces = odd_gather(self_even)
    cross_even = even_gather(jnp.stack(cross_ring))
    self_full, all_vectors = place(self_pieces, index, 4, rows, columns, bias_rows)
    all_wide = all_wide.reshape(data_count, model_count, 2 * rows, units)
    full_vectors = all_vectors[0]

    self_ranges = key_ranges(target_lengths[0], target_lengths[0], tok_rows)
    cross_ranges = key_ranges(target_lengths[0], memory_lengths[0], tok_rows)

    self_query = matmul(layer_input, self_full[0])
    self_key = matmul(layer_input, self_full[1])
    self_value = matmul(layer_input, self_full[2])
    self_out, self_totals = attend(self_query, self_key, self_value, self_ranges, HD)
    self_out, memory_ring, cross_even = together((self_out, memory_ring, cross_even))
    cross_full, _ = place(odd_gather(cross_even), index, 4, rows, columns, bias_rows)
    memory_target = jnp.concatenate(ring_order(memory_ring), axis=1)
    self_mix = matmul(self_out, self_full[3].T)
    first_sum = layer_input + self_mix
    first_norm = layer_norm(first_sum, full_vectors[0], full_vectors[3])
    cross_query = matmul(first_norm, cross_full[0])
    cross_key = matmul(memory_target, cross_full[1])
    cross_value = matmul(memory_target, cross_full[2])
    cross_out, cross_totals = attend(cross_query, cross_key, cross_value, cross_ranges, HD)
    cross_mix = matmul(cross_out, cross_full[3].T)
    second_sum = first_norm + cross_mix
    second_norm = layer_norm(second_sum, full_vectors[1], full_vectors[4])
    layer_output, second_grad, grad_wide, wide_sums, grad_bias = feed_forward(
        model,
        second_norm,
        output_grad,
        all_wide,
        all_vectors,
        rows,
    )

    grad_wide = lax.psum_scatter(
        grad_wide.reshape(data_count, rows, 2 * units), "dp", scatter_dimension=0, tiled=False
    )
    keep, send, resid_one_grad, memory_grad_own = cross_back(
        index,
        cross_ranges,
        second_grad,
        second_sum,
        first_sum,
        memory_target,
        cross_query,
        cross_key,
        cross_value,
        cross_out,
        cross_totals,
        cross_full,
        all_vectors,
        wide_sums,
        grad_bias,
        HD,
        columns,
        rows,
        bias_rows,
    )
    placed = place_back(memory_grad_own, source_slots, data_count * slot_cap)
    resid_one_grad, placed, both = together((resid_one_grad, placed, keep + flip(send, "dp", 1)))
    returned = lax.all_to_all(
        placed.reshape(data_count, slot_cap, columns), "dp", split_axis=0, concat_axis=0, tiled=True
    )
    grad_cross = cube_scatter(both)
    keep, send, self_query_grad, self_key_grad, self_value_grad = self_back(
        index,
        self_ranges,
        resid_one_grad,
        layer_input,
        self_query,
        self_key,
        self_value,
        self_out,
        self_totals,
        self_full,
        HD,
        columns,
        rows,
    )
    keep, send, returned, grad_cross = together((keep, send, returned, grad_cross))
    grad_self = cube_scatter(keep + flip(send, "dp", 1))
    memory_grad = return_rows(returned, my_starts, tok_rows)
    input_grad = (
        resid_one_grad
        + matmul(self_query_grad, self_full[0].T)
        + matmul(self_key_grad, self_full[1].T)
        + matmul(self_value_grad, self_full[2].T)
    )

    weights = weights[:5] + (expand_bias[None],)
    firsts = (
        attend_input_first,
        attend_output_first,
        expand_weight_first,
        reduce_weight_first,
        norm_vectors_first,
        expand_bias_first[None],
    )
    seconds = (
        attend_input_second,
        attend_output_second,
        expand_weight_second,
        reduce_weight_second,
        norm_vectors_second,
        expand_bias_second[None],
    )
    row_shape = jax.ShapeDtypeStruct((1, 128), f32)
    grad_self, grad_cross, grad_vectors, row = whole_call(
        functools.partial(squares_kernel, model_count, len(grad_self)),
        "squares",
        same(grad_self[:1] * 2) + (jax.ShapeDtypeStruct((8, rows), f32), row_shape),
        *grad_self,
        *grad_cross,
        grad_wide,
        *weights,
    )
    row, input_grad = together((small_total(row), input_grad))
    moved = whole_call(
        functools.partial(moments_kernel, model_count, columns),
        "moments",
        same(weights) * 3 + (row_shape,),
        row,
        grad_self,
        grad_cross,
        grad_wide,
        grad_vectors,
        *weights,
        *firsts,
        *seconds,
    )
    new_firsts, new_seconds, updates = moved[:6], moved[6:12], moved[12:18]
    applied = whole_call(
        apply_kernel,
        "apply",
        same(weights)
        + same(weights[:4], bf16)
        + (jax.ShapeDtypeStruct((2, 128), f32), jax.ShapeDtypeStruct((1, 1), f32)),
        row,
        small_total(moved[18]),
        *weights,
        *updates,
    )
    new_weights = applied[:5] + (applied[5][0],)
    matrix_norms = applied[10][:, :10]

    def turned(values):
        return (values[0], values[1].transpose(0, 2, 1), values[2], values[3].T) + tuple(values[4:])

    new_weights, copies = turned(new_weights), turned(applied[6:10])
    new_firsts, new_seconds = turned(new_firsts), turned(new_seconds)
    return (
        layer_output,
        input_grad,
        memory_grad,
        applied[11][0],
        *new_weights,
        *copies,
        new_firsts[0],
        new_seconds[0],
        new_firsts[1],
        new_seconds[1],
        new_firsts[2],
        new_seconds[2],
        new_firsts[3],
        new_seconds[3],
        new_firsts[4],
        new_seconds[4],
        new_firsts[5][0],
        new_seconds[5][0],
        matrix_norms,
    )


def solution(mesh):
    in_specs = (
        P("dp", None),
        P("dp", "mp"),
        P("dp", None),
        P("dp", None),
        P("dp", None),
        P("dp"),
        P(),
        P(None, "dp", "mp"),
        P(None, "mp", "dp"),
        P("dp", "mp"),
        P("mp", "dp"),
        P(None, "dp"),
        P(("mp", "dp")),
        P(None, "dp", "mp"),
        P(None, "dp", "mp"),
        P(None, "mp", "dp"),
        P(None, "mp", "dp"),
        P("dp", "mp"),
        P("dp", "mp"),
        P("mp", "dp"),
        P("mp", "dp"),
        P(None, "dp"),
        P(None, "dp"),
        P(("mp", "dp")),
        P(("mp", "dp")),
    )
    out_specs = (
        P("dp", None),
        P("dp", None),
        P("dp", "mp"),
        P(),
        P(None, "dp", "mp"),
        P(None, "mp", "dp"),
        P("dp", "mp"),
        P("mp", "dp"),
        P(None, "dp"),
        P(("mp", "dp")),
        P(None, "dp", "mp"),
        P(None, "mp", "dp"),
        P("dp", "mp"),
        P("mp", "dp"),
        P(None, "dp", "mp"),
        P(None, "dp", "mp"),
        P(None, "mp", "dp"),
        P(None, "mp", "dp"),
        P("dp", "mp"),
        P("dp", "mp"),
        P("mp", "dp"),
        P("mp", "dp"),
        P(None, "dp"),
        P(None, "dp"),
        P(("mp", "dp")),
        P(("mp", "dp")),
        P(),
    )
    return jax.shard_map(shards, mesh=mesh, in_specs=in_specs, out_specs=out_specs, check_vma=False)
```

```python
import functools

import jax
import jax.numpy as jnp
from jax import lax
from jax.experimental import pallas as pl
from jax.experimental.pallas import tpu as pltpu
from jax.sharding import PartitionSpec as P

HD = 64
STEP_NUM = 6

norm_eps = 1e-05
adam_eps = 1e-06
first_decay = 0.5
second_decay = 0.5
matrix_decay = 0.01
peak_rate = 0.6
warm_steps = 8.0
clip_norm = 1.0

bf16 = jnp.bfloat16
f32 = jnp.float32
neg_large = -1e30
q_rows = 128
key_rows = 256
pair_lanes = 128


def split_two(values):
    high = values.astype(bf16)
    return high, (values - high.astype(f32)).astype(bf16)


def dot_nn(left_side, right_side):
    return lax.dot_general(left_side, right_side, (((1,), (0,)), ((), ())), preferred_element_type=f32)


def dot_nt(left_side, right_side):
    return lax.dot_general(left_side, right_side, (((1,), (1,)), ((), ())), preferred_element_type=f32)


def dot_tn(left_side, right_side):
    return lax.dot_general(left_side, right_side, (((0,), (0,)), ((), ())), preferred_element_type=f32)


def three(dot, left_pair, right_pair):
    return (
        dot(left_pair[0], right_pair[0])
        + dot(left_pair[1], right_pair[0])
        + dot(left_pair[0], right_pair[1])
    )


def swap_halves(tile):
    return pltpu.roll(tile, pair_lanes // 2, 1)


def parts_of(tile):
    high = tile.astype(bf16).astype(f32)
    return high, tile - high


def query_packs(tile, low_half):
    high, low = parts_of(tile)
    high_swap, low_swap = swap_halves(high), swap_halves(low)
    zero = jnp.zeros_like(tile)
    first = jnp.concatenate(
        [jnp.where(low_half, high, high_swap), jnp.where(low_half, low, zero)], axis=1
    )
    second = jnp.concatenate(
        [jnp.where(low_half, high_swap, high), jnp.where(low_half, low_swap, zero)], axis=1
    )
    return first.astype(bf16), second.astype(bf16)


def key_packs(tile, low_half):
    high, low = parts_of(tile)
    high_swap, low_swap = swap_halves(high), swap_halves(low)
    zero = jnp.zeros_like(tile)
    first = jnp.concatenate(
        [jnp.where(low_half, high, low_swap), jnp.where(low_half, high, zero)], axis=1
    )
    second = jnp.concatenate(
        [jnp.where(low_half, high_swap, low), jnp.where(low_half, high_swap, zero)], axis=1
    )
    return first.astype(bf16), second.astype(bf16)


def both_parts(tile):
    high, low = split_two(tile)
    return jnp.concatenate([high, low], axis=1)


def stack_heads(tile, low_half):
    return jnp.concatenate([jnp.where(low_half, tile, 0.0), jnp.where(low_half, 0.0, tile)], axis=0)


def merge_heads(stacked, low_half):
    return jnp.where(low_half, stacked[:q_rows], stacked[q_rows:])


def folded(dot, left_pair, right_both):
    wide = dot(left_pair[0], right_both)
    return wide[:, :pair_lanes] + wide[:, pair_lanes:] + dot(left_pair[1], right_both[:, :pair_lanes])


def prepare_rows(at, source_ref, low_half, pack_ref, both_ref):
    for pair in range(source_ref.shape[1] // pair_lanes):
        tile = source_ref[at, pair * pair_lanes : (pair + 1) * pair_lanes]
        if pack_ref is not None:
            first, second = key_packs(tile, low_half)
            pack_ref[2 * pair, at, :] = first
            pack_ref[2 * pair + 1, at, :] = second
        if both_ref is not None:
            both_ref[pair, at, :] = both_parts(tile)


def clear_pad(rows, *refs):
    for ref in refs:
        ref[:, rows:, :] = jnp.zeros((ref.shape[0], ref.shape[1] - rows, ref.shape[2]), bf16)


def half_mask(rows):
    return lax.broadcasted_iota(jnp.int32, (rows, pair_lanes), 1) < pair_lanes // 2


def chunks(rows, size, body):
    def one(step, carry):
        body(pl.ds(pl.multiple_of(step * size, size), size))
        return carry

    lax.fori_loop(0, rows // size, one, 0)


def attend_kernel(
    unroll, scale, block_low, block_count,
    q_ref, k_ref, v_ref, low_ref, high_ref,
    o_ref, total_ref,
    kp_ref, vb_ref,
):
    rows, width = q_ref.shape
    lanes = lax.broadcasted_iota(jnp.int32, (q_rows, pair_lanes), 1)
    low_half = lanes < pair_lanes // 2
    clear_pad(rows, kp_ref, vb_ref)

    def before(at):
        prepare_rows(at, k_ref, low_half, kp_ref, None)
        prepare_rows(at, v_ref, low_half, None, vb_ref)

    chunks(rows, q_rows, before)
    groups = width // pair_lanes // unroll
    key_iota = lax.broadcasted_iota(jnp.int32, (q_rows, key_rows), 1)

    def block(index, carry):
        at = pl.ds(pl.multiple_of(index * q_rows, q_rows), q_rows)
        first = low_ref[at, :]
        last = high_ref[at, :]
        for group in range(groups):
            pairs = [group * unroll + u for u in range(unroll)]

            def load(u):
                lanes_of = slice(pairs[u] * pair_lanes, (pairs[u] + 1) * pair_lanes)
                return query_packs(q_ref[at, lanes_of] * scale, low_half)

            def chunk(step, state, held_packs=None):
                start = pl.multiple_of(block_low[index] + step * key_rows, 16)
                here = pl.ds(start, key_rows)
                places = key_iota + start
                bias = jnp.where(jnp.logical_and(places >= first, places < last), 0.0, neg_large)
                bias = jnp.concatenate([bias, bias], axis=0)
                out, found = [], []
                for u, p in enumerate(pairs):
                    query = load(u) if held_packs is None else held_packs[u]
                    found.append(
                        jnp.concatenate(
                            [dot_nt(query[h], kp_ref[2 * p + h, here, :]) for h in range(2)], axis=0
                        )
                    )
                for u, p in enumerate(pairs):
                    scores = bias + found[u]
                    new_top = jnp.max(scores, axis=1, keepdims=True)
                    if state is not None:
                        top, total, held = state[u]
                        new_top = jnp.maximum(top, new_top)
                        shrink = jnp.exp(top - new_top)
                    weights = jnp.exp(scores - new_top)
                    new_total = jnp.sum(weights, axis=1, keepdims=True)
                    new_held = folded(dot_nn, split_two(weights), vb_ref[p, here, :])
                    if state is not None:
                        new_total = total * shrink + new_total
                        new_held = held * shrink + new_held
                    out.append((new_top, new_total, new_held))
                return tuple(out)

            def finish(state):
                tile = total_ref[at, :] if group else jnp.zeros((q_rows, pair_lanes), f32)
                for u, p in enumerate(pairs):
                    top, total, held = state[u]
                    o_ref[at, p * pair_lanes : (p + 1) * pair_lanes] = merge_heads(held / total, low_half)
                    logs = top + jnp.log(total)
                    tile = jnp.where(lanes == 2 * p, logs[:q_rows], tile)
                    tile = jnp.where(lanes == 2 * p + 1, logs[q_rows:], tile)
                total_ref[at, :] = tile

            @pl.when(block_count[index] == 1)
            def _():
                finish(chunk(0, None))

            @pl.when(block_count[index] > 1)
            def _():
                start_state = tuple(
                    (
                        jnp.full((2 * q_rows, 1), neg_large, f32),
                        jnp.zeros((2 * q_rows, 1), f32),
                        jnp.zeros((2 * q_rows, pair_lanes), f32),
                    )
                    for _ in range(unroll)
                )
                packs = [load(u) for u in range(unroll)]
                step = lambda number, state: chunk(number, state, packs)
                finish(lax.fori_loop(0, block_count[index], step, start_state))

        return carry

    lax.fori_loop(0, rows // q_rows, block, 0)


def attend_back_blocks(
    unroll, scale, block_low, block_count,
    q_ref, o_ref, g_ref, total_ref, low_ref, high_ref,
    dq_ref, kp_ref, vp_ref, kb_ref, dk_sum, dv_sum,
):
    rows, width = q_ref.shape
    lanes = lax.broadcasted_iota(jnp.int32, (q_rows, pair_lanes), 1)
    low_half = lanes < pair_lanes // 2
    groups = width // pair_lanes // unroll
    key_iota = lax.broadcasted_iota(jnp.int32, (q_rows, key_rows), 1)

    def block(index, carry):
        at = pl.ds(pl.multiple_of(index * q_rows, q_rows), q_rows)
        first = low_ref[at, :]
        last = high_ref[at, :]
        total_tile = total_ref[at, :]
        for group in range(groups):
            pairs = [group * unroll + u for u in range(unroll)]

            def column(mask, value):
                return jnp.sum(jnp.where(mask, value, 0.0), axis=1, keepdims=True)

            def load(u):
                p = pairs[u]
                lanes_of = slice(p * pair_lanes, (p + 1) * pair_lanes)
                query = q_ref[at, lanes_of] * scale
                grad = g_ref[at, lanes_of]
                product = grad * o_ref[at, lanes_of]
                dots = [column(low_half, product), column(jnp.logical_not(low_half), product)]
                logs = [column(lanes == 2 * p, total_tile), column(lanes == 2 * p + 1, total_tile)]
                return (
                    query_packs(query, low_half),
                    query_packs(grad, low_half),
                    both_parts(stack_heads(query, low_half)),
                    both_parts(stack_heads(grad, low_half)),
                    jnp.concatenate(logs, axis=0),
                    jnp.concatenate(dots, axis=0),
                )

            def chunk(step, state, held_packs=None):
                start = pl.multiple_of(block_low[index] + step * key_rows, 16)
                here = pl.ds(start, key_rows)
                places = key_iota + start
                bias = jnp.where(jnp.logical_and(places >= first, places < last), 0.0, neg_large)
                bias = jnp.concatenate([bias, bias], axis=0)
                out, packs, found = [], [], []
                for u, p in enumerate(pairs):
                    packs.append(load(u) if held_packs is None else held_packs[u])
                    found.append(
                        [
                            jnp.concatenate(
                                [dot_nt(packs[u][k][h], ref[2 * p + h, here, :]) for h in range(2)], axis=0
                            )
                            for k, ref in enumerate((kp_ref, vp_ref))
                        ]
                    )
                for u, p in enumerate(pairs):
                    lanes_of = slice(p * pair_lanes, (p + 1) * pair_lanes)
                    _, _, query_both, grad_both, logs, dots = packs[u]
                    weights = jnp.exp(bias + found[u][0] - logs)
                    grad_scores = split_two(weights * (found[u][1] - dots))
                    new_state = folded(dot_nn, grad_scores, kb_ref[p, here, :])
                    out.append(new_state if state is None else state[u] + new_state)
                    dk_sum[here, lanes_of] += folded(dot_tn, grad_scores, query_both)
                    dv_sum[here, lanes_of] += folded(dot_tn, split_two(weights), grad_both)
                return tuple(out)

            def finish(state):
                for u, p in enumerate(pairs):
                    dq_ref[at, p * pair_lanes : (p + 1) * pair_lanes] = merge_heads(state[u], low_half) * scale

            @pl.when(block_count[index] == 1)
            def _():
                finish(chunk(0, None))

            @pl.when(block_count[index] > 1)
            def _():
                start_state = tuple(jnp.zeros((2 * q_rows, pair_lanes), f32) for _ in range(unroll))
                packs = [load(u) for u in range(unroll)]
                step = lambda number, state: chunk(number, state, packs)
                finish(lax.fori_loop(0, block_count[index], step, start_state))

        return carry

    lax.fori_loop(0, rows // q_rows, block, 0)


def own_lanes(ref, at, model, columns):
    if columns % pair_lanes == 0:
        return ref[at, pl.ds(pl.multiple_of(model * columns, pair_lanes), columns)]
    start = model * columns
    base = pl.multiple_of(start // pair_lanes * pair_lanes, pair_lanes)
    tile = ref[at, pl.ds(base, pair_lanes)]
    return pltpu.roll(tile, lax.rem(pair_lanes - lax.rem(start, pair_lanes), pair_lanes), 1)[:, :columns]


def norm_parts(values):
    centred = values - jnp.mean(values, axis=1, keepdims=True)
    scale = lax.rsqrt(jnp.mean(centred * centred, axis=1, keepdims=True) + norm_eps)
    return centred * scale, scale


def norm_back(grad, normal, scale, gain):
    inner = grad * gain
    return (
        inner
        - jnp.mean(inner, axis=1, keepdims=True)
        - normal * jnp.mean(inner * normal, axis=1, keepdims=True)
    ) * scale


def column_sum(value):
    return jnp.sum(value, axis=0, keepdims=True)


def hand_out(index_ref, grads_ref, keep_ref, send_ref, rows, extra_ref=None):
    me = index_ref[0]
    odd = lax.rem(me, 2)
    for r in range(keep_ref.shape[0]):
        pair = 2 * ((me // 2) ^ r)
        for ref, which in ((keep_ref, pair + odd), (send_ref, pair + 1 - odd)):
            ref[r, :rows, :] = grads_ref[pl.ds(pl.multiple_of(which * rows, rows), rows), :]
            if extra_ref is not None:
                ref[r, rows:, :] = extra_ref[pl.ds(which, 1)][0]


def cross_back_kernel(
    unroll, scale, columns, rows_of, bias_rows, index_ref, block_low, block_count,
    g_ref, two_ref, one_ref, mem_ref, q_ref, k_ref, v_ref, o_ref, total_ref, low_ref, high_ref,
    w_ref, vec_ref, sums_ref, bias_ref,
    keep_ref, send_ref, resid_ref, mem_grad_ref,
    kp_ref, vp_ref, kb_ref, dk_sum, dv_sum, dq_ref, go_ref, two_grad_ref, woh, wol, wqh, wql, grads, totals, parts,
):
    rows, width = q_ref.shape
    model = index_ref[1]
    mask = half_mask(256)
    clear_pad(rows, kp_ref, vp_ref, kb_ref)
    dk_sum[...] = jnp.zeros_like(dk_sum)
    dv_sum[...] = jnp.zeros_like(dv_sum)
    woh[...], wol[...] = split_two(w_ref[3])
    wqh[...], wql[...] = split_two(w_ref[0])
    totals[...] = sums_ref[...]
    grads[...] = jnp.zeros_like(grads)

    def before(at):
        normal, spread = norm_parts(two_ref[at, :])
        grad = g_ref[at, :]
        resid = norm_back(grad, normal, spread, vec_ref[0, 1:2, :])
        totals[1:2, :] += column_sum(grad * normal)
        totals[4:5, :] += column_sum(grad)
        two_grad_ref[at, :] = resid
        go_ref[at, :] = three(dot_nn, split_two(resid), (woh[...], wol[...]))
        prepare_rows(at, k_ref, mask, kp_ref, kb_ref)
        prepare_rows(at, v_ref, mask, vp_ref, None)

    chunks(rows, 256, before)
    attend_back_blocks(
        unroll, scale, block_low, block_count,
        q_ref, o_ref, go_ref, total_ref, low_ref, high_ref,
        dq_ref, kp_ref, vp_ref, kb_ref, dk_sum, dv_sum,
    )

    def after(at):
        resid = two_grad_ref[at, :]
        grad = resid + three(dot_nt, split_two(dq_ref[at, :]), (wqh[...], wql[...]))
        normal, spread = norm_parts(one_ref[at, :])
        gain = vec_ref[0, 0:1, :]
        resid_ref[at, :] = norm_back(grad, normal, spread, gain)
        totals[0:1, :] += column_sum(grad * normal)
        totals[3:4, :] += column_sum(grad)
        source = split_two(normal * gain + vec_ref[0, 3:4, :])
        memory = split_two(mem_ref[at, :])
        dk = dk_sum[at, :]
        dv = dv_sum[at, :]
        grads[:, :columns] += three(dot_tn, source, split_two(own_lanes(dq_ref, at, model, columns)))
        both = jnp.concatenate([own_lanes(ref, at, model, columns) for ref in (dk_sum, dv_sum)], axis=1)
        grads[:, columns : 3 * columns] += three(dot_tn, memory, split_two(both))
        grads[:, 3 * columns :] += three(
            dot_tn, split_two(resid), split_two(own_lanes(o_ref, at, model, columns))
        )
        slice_of = pl.ds(pl.multiple_of(model * columns, columns), columns)
        mem_grad_ref[at, :] = three(dot_nt, split_two(dk), split_two(w_ref[1, slice_of, :])) + three(
            dot_nt, split_two(dv), split_two(w_ref[2, slice_of, :])
        )

    chunks(rows, 256, after)
    parts[...] = jnp.zeros_like(parts)
    for j in range(parts.shape[0]):
        parts[j, :, :rows_of] = totals[:, j * rows_of : (j + 1) * rows_of]
        parts[j, 7:8, :bias_rows] = bias_ref[:, j * bias_rows : (j + 1) * bias_rows]
    hand_out(index_ref, grads, keep_ref, send_ref, rows_of, parts)


def self_back_kernel(
    unroll, scale, columns, rows_of, index_ref, block_low, block_count,
    g_ref, x_ref, q_ref, k_ref, v_ref, o_ref, total_ref, low_ref, high_ref, w_ref,
    keep_ref, send_ref, dq_ref, dk_ref, dv_ref,
    kp_ref, vp_ref, kb_ref, dk_sum, dv_sum, go_ref, woh, wol, grads,
):
    rows, width = q_ref.shape
    model = index_ref[1]
    mask = half_mask(256)
    clear_pad(rows, kp_ref, vp_ref, kb_ref)
    dk_sum[...] = jnp.zeros_like(dk_sum)
    dv_sum[...] = jnp.zeros_like(dv_sum)
    woh[...], wol[...] = split_two(w_ref[3])
    grads[...] = jnp.zeros_like(grads)

    def before(at):
        go_ref[at, :] = three(dot_nn, split_two(g_ref[at, :]), (woh[...], wol[...]))
        prepare_rows(at, k_ref, mask, kp_ref, kb_ref)
        prepare_rows(at, v_ref, mask, vp_ref, None)

    chunks(rows, 256, before)
    attend_back_blocks(
        unroll, scale, block_low, block_count,
        q_ref, o_ref, go_ref, total_ref, low_ref, high_ref,
        dq_ref, kp_ref, vp_ref, kb_ref, dk_sum, dv_sum,
    )

    def after(at):
        source = split_two(x_ref[at, :])
        dk_ref[at, :] = dk_sum[at, :]
        dv_ref[at, :] = dv_sum[at, :]
        every = [own_lanes(ref, at, model, columns) for ref in (dq_ref, dk_sum, dv_sum)]
        grads[:, : 3 * columns] += three(dot_tn, source, split_two(jnp.concatenate(every, axis=1)))
        grads[:, 3 * columns :] += three(
            dot_tn, split_two(g_ref[at, :]), split_two(own_lanes(o_ref, at, model, columns))
        )

    chunks(rows, 256, after)
    hand_out(index_ref, grads, keep_ref, send_ref, rows_of)


VM = functools.partial(pl.BlockSpec, memory_space=pltpu.VMEM)
SM = functools.partial(pl.BlockSpec, memory_space=pltpu.SMEM)


def attend(queries, keys_in, values_in, ranges, head_size, unroll=4):
    block_low, block_count, low, high = ranges
    rows, width = queries.shape
    pad_rows = keys_in.shape[0] + key_rows
    return pl.pallas_call(
        functools.partial(attend_kernel, unroll, head_size ** -0.5),
        out_shape=(
            jax.ShapeDtypeStruct((rows, width), f32),
            jax.ShapeDtypeStruct((rows, pair_lanes), f32),
        ),
        in_specs=[SM(), SM()] + [VM()] * 5,
        out_specs=(VM(), VM()),
        scratch_shapes=[
            pltpu.VMEM((width // 64, pad_rows, 2 * pair_lanes), bf16),
            pltpu.VMEM((width // pair_lanes, pad_rows, 2 * pair_lanes), bf16),
        ],
        compiler_params=pltpu.CompilerParams(vmem_limit_bytes=48 << 20),
        cost_estimate=pl.CostEstimate(flops=12 * rows * key_rows * width, bytes_accessed=16 * rows * width, transcendentals=rows * key_rows * 8),
        name="attend",
    )(block_low, block_count, queries, keys_in, values_in, low, high)


def back_scratch(rows, width):
    pad_rows = rows + key_rows
    return [
        pltpu.VMEM((width // 64, pad_rows, 2 * pair_lanes), bf16),
        pltpu.VMEM((width // 64, pad_rows, 2 * pair_lanes), bf16),
        pltpu.VMEM((width // pair_lanes, pad_rows, 2 * pair_lanes), bf16),
        pltpu.VMEM((pad_rows, width), f32),
        pltpu.VMEM((pad_rows, width), f32),
    ]


def cross_back(
    index, ranges, grad, two, one, memory, queries, keys_in, values_in, outputs, totals,
    matrices, vectors, sums, bias, head_size, columns, rows_of, bias_rows, unroll=4,
):
    block_low, block_count, low, high = ranges
    rows, width = queries.shape
    data = width // rows_of
    block = jax.ShapeDtypeStruct((data // 2, rows_of + 8, 4 * columns), f32)
    return pl.pallas_call(
        functools.partial(cross_back_kernel, unroll, head_size ** -0.5, columns, rows_of, bias_rows),
        out_shape=(
            block,
            block,
            jax.ShapeDtypeStruct((rows, width), f32),
            jax.ShapeDtypeStruct((rows, columns), f32),
        ),
        in_specs=[SM()] * 3 + [VM()] * 15,
        out_specs=(VM(),) * 4,
        scratch_shapes=back_scratch(rows, width)
        + [pltpu.VMEM((rows, width), f32)] * 3
        + [pltpu.VMEM((width, width), bf16)] * 4
        + [
            pltpu.VMEM((width, 4 * columns), f32),
            pltpu.VMEM((8, width), f32),
            pltpu.VMEM((data, 8, 4 * columns), f32),
        ],
        compiler_params=pltpu.CompilerParams(vmem_limit_bytes=60 << 20),
        cost_estimate=pl.CostEstimate(flops=30 << 30, bytes_accessed=30 << 20, transcendentals=rows * key_rows * 8),
        name="cross_back",
    )(
        index, block_low, block_count, grad, two, one, memory, queries, keys_in, values_in, outputs, totals,
        low, high, matrices, vectors, sums, bias,
    )


def self_back(
    index, ranges, grad, source, queries, keys_in, values_in, outputs, totals, matrices,
    head_size, columns, rows_of, unroll=4,
):
    block_low, block_count, low, high = ranges
    rows, width = queries.shape
    data = width // rows_of
    block = jax.ShapeDtypeStruct((data // 2, rows_of, 4 * columns), f32)
    return pl.pallas_call(
        functools.partial(self_back_kernel, unroll, head_size ** -0.5, columns, rows_of),
        out_shape=(block, block) + (jax.ShapeDtypeStruct((rows, width), f32),) * 3,
        in_specs=[SM()] * 3 + [VM()] * 10,
        out_specs=(VM(),) * 5,
        scratch_shapes=back_scratch(rows, width)
        + [pltpu.VMEM((rows, width), f32)]
        + [pltpu.VMEM((width, width), bf16)] * 2
        + [pltpu.VMEM((width, 4 * columns), f32)],
        compiler_params=pltpu.CompilerParams(vmem_limit_bytes=60 << 20),
        cost_estimate=pl.CostEstimate(flops=30 << 30, bytes_accessed=30 << 20, transcendentals=rows * key_rows * 8),
        name="self_back",
    )(
        index, block_low, block_count, grad, source, queries, keys_in, values_in, outputs, totals,
        low, high, matrices,
    )


def key_ranges(query_lengths, key_lengths, rows):
    query_ends = jnp.cumsum(query_lengths)
    query_starts = query_ends - query_lengths
    places = jnp.arange(rows, dtype=jnp.int32)
    low = jnp.sum(jnp.where(query_ends[None, :] <= places[:, None], key_lengths[None, :], 0), axis=1)
    high = jnp.sum(jnp.where(query_starts[None, :] <= places[:, None], key_lengths[None, :], 0), axis=1)
    block_low = low[::q_rows] // 16 * 16
    block_high = high[q_rows - 1 :: q_rows]
    block_count = (block_high - block_low + key_rows - 1) // key_rows
    return block_low, block_count, low[:, None], high[:, None]


def matmul(left_side, right_side):
    return jnp.dot(left_side, right_side, precision=lax.Precision.HIGH, preferred_element_type=f32)


def layer_norm(values, gain_row, shift_row):
    centre_mean = jnp.mean(values, axis=-1, keepdims=True)
    centred = values - centre_mean
    variance = jnp.mean(centred * centred, axis=-1, keepdims=True)
    return centred * lax.rsqrt(variance + norm_eps) * gain_row + shift_row


def flip(value, axis, distance):
    pairs = [(i, i ^ distance) for i in range(lax.axis_size(axis))]
    return lax.ppermute(value, axis, pairs)


def tree_total(pieces):
    while len(pieces) > 1:
        pieces = [pieces[i] + pieces[i + 1] for i in range(0, len(pieces), 2)]
    return pieces[0]


def small_total(value):
    value = value + flip(value, "dp", 1)
    others = lax.axis_size("dp") // 2
    value = tree_total([value] + [flip(value, "dp", 2 * r) for r in range(1, others)])
    models = lax.axis_size("mp")
    return tree_total([value] + [flip(value, "mp", r) for r in range(1, models)])


def ring_gather(own):
    count = lax.axis_size("mp")
    return [own] + [
        lax.ppermute(own, "mp", [(i, (i + step) % count) for i in range(count)])
        for step in range(1, count)
    ]


def ring_order(ring):
    count = len(ring)
    me = lax.axis_index("mp")
    found = []
    for place in range(count):
        value = ring[0]
        for step in range(1, count):
            value = jnp.where(me == (place + step) % count, ring[step], value)
        found.append(value)
    return found


def even_gather(own):
    return [own] + [flip(own, "dp", r) for r in range(2, lax.axis_size("dp"), 2)]


def odd_gather(even):
    odd = [flip(value, "dp", 1) for value in even]
    return [value for pair in zip(even, odd) for value in pair]


def place_kernel(parts, rows, columns, bias_rows, index_ref, *refs):
    pieces, (full_ref, vec_ref) = refs[:-2], refs[-2:]
    me, model = index_ref[0], index_ref[1]
    models = pieces[0].shape[0]
    width = vec_ref.shape[2]
    pad = jnp.zeros((8, width - columns), f32)
    bias_row = lax.broadcasted_iota(jnp.int32, (8, width), 0) == 7
    vec_ref[...] = jnp.zeros_like(vec_ref)
    for r, piece in enumerate(pieces):
        whose = me ^ r
        at = pl.ds(pl.multiple_of(whose * rows, rows), rows)
        for place in range(models):
            slot = lax.rem(model - place + models, models)
            for part in range(parts):
                full_ref[part, at, place * columns : (place + 1) * columns] = piece[
                    slot, part * rows : (part + 1) * rows, :
                ]
            values = jnp.concatenate([piece[slot, parts * rows :, :], pad], axis=1)
            moved = pltpu.roll(values, whose * rows, 1)
            if rows != bias_rows:
                moved = jnp.where(bias_row, pltpu.roll(values, whose * bias_rows, 1), moved)
            vec_ref[place] += moved


def place(pieces, index, parts, rows, columns, bias_rows):
    models, count = pieces[0].shape[0], len(pieces)
    return pl.pallas_call(
        functools.partial(place_kernel, parts, rows, columns, bias_rows),
        out_shape=(
            jax.ShapeDtypeStruct((parts, rows * count, columns * models), f32),
            jax.ShapeDtypeStruct((models, 8, columns * models), f32),
        ),
        in_specs=[SM()] + [VM()] * count,
        out_specs=(VM(), VM()),
        compiler_params=pltpu.CompilerParams(vmem_limit_bytes=40 << 20),
        name="place",
    )(index, *pieces)


def gelu_both(values):
    inner = 0.7978845608028654 * (values + 0.044715 * values * values * values)
    bent = jnp.tanh(inner)
    half = 0.5 * (1.0 + bent)
    slope = half + 0.5 * values * (1.0 - bent * bent) * (
        0.7978845608028654 * (1.0 + 3.0 * 0.044715 * values * values)
    )
    return values * half, slope


def wide_kernel(
    rows, model_ref, z_ref, g_ref, wide_ref, all_vec_ref,
    out_ref, second_ref, grads_ref, sums_ref, bias_grad_ref,
    eh_ref, el_ref, rh_ref, rl_ref, slope_ref, xh_ref, xl_ref, bh_ref, bl_ref,
):
    tokens, width = z_ref.shape
    data, models, _, units = wide_ref.shape
    model = model_ref[0]
    vec_ref = all_vec_ref.at[0]
    block = xh_ref.shape[0]

    def load(step, carry):
        which, part = step // models, step % models
        at = pl.ds(pl.multiple_of(which * rows, rows), rows)
        to = pl.ds(pl.multiple_of(part * units, units), units)
        eh_ref[at, to], el_ref[at, to] = split_two(wide_ref[which, part, :rows, :])
        rh_ref[at, to], rl_ref[at, to] = split_two(wide_ref[which, part, rows:, :])
        return carry

    lax.fori_loop(0, data * models, load, 0)
    sums_ref[...] = jnp.zeros_like(sums_ref)
    bias_grad_ref[...] = jnp.zeros_like(bias_grad_ref)
    grads_ref[...] = jnp.zeros_like(grads_ref)

    gain = vec_ref[2:3, :]
    half = block // 2
    halves = [slice(0, half), slice(half, block)]

    def chunk(step, carry):
        whole = pl.ds(pl.multiple_of(step * block, block), block)
        ats = [pl.ds(pl.multiple_of(step * block + h * half, half), half) for h in range(2)]
        products, resids, reduced = [None] * 2, [None] * 2, [None] * 2

        def enter(h):
            products[h] = three(dot_nn, split_two(z_ref[ats[h], :]), (eh_ref[...], el_ref[...]))

        def bend(h):
            for part in range(models):
                to = slice(part * units, (part + 1) * units)
                value, slope = gelu_both(products[h][:, to] + all_vec_ref[part, 7:8, :units])
                slope_ref[halves[h], to] = slope
                xh_ref[halves[h], to], xl_ref[halves[h], to] = split_two(value)

        def leave(h):
            reduced[h] = three(
                dot_nt, (xh_ref[halves[h], :], xl_ref[halves[h], :]), (rh_ref[...], rl_ref[...])
            )

        def turn(h):
            at = ats[h]
            normal, scale = norm_parts(z_ref[at, :] + vec_ref[6:7, :] + reduced[h])
            out_ref[at, :] = normal * gain + vec_ref[5:6, :]
            grad = g_ref[at, :]
            resids[h] = norm_back(grad, normal, scale, gain)
            sums_ref[2:3, :] += column_sum(grad * normal)
            sums_ref[5:6, :] += column_sum(grad)
            sums_ref[6:7, :] += column_sum(resids[h])

        def reenter(h):
            products[h] = three(dot_nn, split_two(resids[h]), (rh_ref[...], rl_ref[...]))

        def unbend(h):
            for part in range(models):
                to = slice(part * units, (part + 1) * units)
                back = products[h][:, to] * slope_ref[halves[h], to]
                slope_ref[halves[h], to] = back
                bh_ref[halves[h], to], bl_ref[halves[h], to] = split_two(back)

        def finish(h):
            return three(dot_nt, (bh_ref[halves[h], :], bl_ref[halves[h], :]), (eh_ref[...], el_ref[...]))

        enter(0)
        enter(1)
        bend(0)
        leave(0)
        bend(1)
        leave(1)
        turn(0)
        reenter(0)
        turn(1)
        reenter(1)
        unbend(0)
        more = finish(0)
        unbend(1)
        last = finish(1)
        second_ref[ats[0], :] = resids[0] + more
        second_ref[ats[1], :] = resids[1] + last
        to = pl.ds(pl.multiple_of(model * units, units), units)
        bias_grad_ref[...] += column_sum(slope_ref[:, to])
        grads_ref[:, :units] += three(dot_tn, split_two(z_ref[whole, :]), (bh_ref[:, to], bl_ref[:, to]))
        grads_ref[:, units:] += three(
            dot_tn, split_two(jnp.concatenate(resids, axis=0)), (xh_ref[:, to], xl_ref[:, to])
        )
        return carry

    lax.fori_loop(0, tokens // block, chunk, 0)


def feed_forward(model, source, grad, wide, vectors, rows):
    tokens, width = source.shape
    data, models, _, units = wide.shape
    block = min(512, tokens)
    return pl.pallas_call(
        functools.partial(wide_kernel, rows),
        out_shape=(
            jax.ShapeDtypeStruct((tokens, width), f32),
            jax.ShapeDtypeStruct((tokens, width), f32),
            jax.ShapeDtypeStruct((width, 2 * units), f32),
            jax.ShapeDtypeStruct((8, width), f32),
            jax.ShapeDtypeStruct((1, units), f32),
        ),
        in_specs=[SM()] + [VM()] * 4,
        out_specs=(VM(),) * 5,
        scratch_shapes=[pltpu.VMEM((width, models * units), bf16)] * 4
        + [
            pltpu.VMEM((block, models * units), f32),
        ]
        + [pltpu.VMEM((block, models * units), bf16)] * 4,
        compiler_params=pltpu.CompilerParams(vmem_limit_bytes=60 << 20),
        cost_estimate=pl.CostEstimate(
            flops=27 * tokens * width * models * units, bytes_accessed=24 << 20, transcendentals=tokens * models * units
        ),
        name="feed_forward",
    )(model[None], source, grad, wide, vectors)


def cell(row, lane):
    return jnp.sum(
        jnp.where(lax.broadcasted_iota(jnp.int32, row.shape, 1) == lane, row, 0.0), axis=1, keepdims=True
    )


def total_of(value):
    return jnp.sum(jnp.sum(value, axis=1, keepdims=True), axis=0, keepdims=True)


def put(row, lane, value):
    return jnp.where(lax.broadcasted_iota(jnp.int32, row.shape, 1) == lane, value, row)


def part_row(pieces, divisor):
    row = jnp.zeros((1, 128), f32)
    for number, value in enumerate(pieces):
        total = total_of(value * value)
        row = put(row, number, total / divisor if 10 <= number < 17 else total)
    return row


def part_list(arrays):
    return (
        [arrays[0][i] for i in range(arrays[0].shape[0])]
        + [arrays[1][i] for i in range(arrays[1].shape[0])]
        + [arrays[2][...], arrays[3][...]]
        + [arrays[4][i : i + 1, :] for i in range(arrays[4].shape[0])]
        + [arrays[5][...]]
    )


def squares_kernel(divisor, count, *refs):
    self_pieces, cross_pieces, rest = refs[:count], refs[count : 2 * count], refs[2 * count :]
    wide, weights, (self_ref, cross_ref, vector_ref, row_ref) = rest[0][...], rest[1:-4], rest[-4:]
    rows = self_ref.shape[0]
    value = tree_total([piece[...] for piece in self_pieces])
    both = tree_total([piece[...] for piece in cross_pieces])
    cross, vectors = both[:rows], both[rows:, :rows]
    self_ref[...] = value
    cross_ref[...] = cross
    vector_ref[...] = vectors
    total = total_of(value * value) + total_of(cross * cross) + total_of(wide * wide)
    norms = vectors[:7]
    last = vectors[7:8]
    total = total + total_of(norms * norms) / divisor + total_of(last * last)
    row_ref[...] = put(part_row(part_list(weights), divisor), 18, total)


def moments_kernel(divisor, columns, row_ref, *refs):
    grads, rest = refs[:4], refs[4:]
    weights, firsts, seconds = rest[:6], rest[6:12], rest[12:18]
    new_firsts, new_seconds, updates, out_row = rest[18:24], rest[24:30], rest[30:36], rest[36]
    units = rest[2].shape[1]
    bias_rows = rest[5].shape[1]
    norm = jnp.sqrt(cell(row_ref[...], 18))
    clip = jnp.minimum(1.0, clip_norm / norm)
    first_fix = 1.0 - first_decay**STEP_NUM
    second_fix = 1.0 - second_decay**STEP_NUM

    def step(grad, weight, first, second, decay):
        clipped = grad * clip
        one = first_decay * first + (1.0 - first_decay) * clipped
        two = second_decay * second + (1.0 - second_decay) * clipped * clipped
        return one, two, one / first_fix / (jnp.sqrt(two / second_fix) + adam_eps) + decay * weight

    squares = []

    def store(number, at, grad, decay):
        one, two, update = step(
            grad, weights[number][at], firsts[number][at], seconds[number][at], decay
        )
        new_firsts[number][at] = one
        new_seconds[number][at] = two
        updates[number][at] = update
        return update

    for number in range(2):
        for which in range(3):
            store(0, 3 * number + which, grads[number][:, which * columns : (which + 1) * columns], matrix_decay)
    for number in range(2):
        store(1, number, grads[number][:, 3 * columns : 4 * columns], matrix_decay)
    store(2, slice(None), grads[2][:, :units], matrix_decay)
    store(3, slice(None), grads[2][:, units:], matrix_decay)
    store(4, slice(None), grads[3][:7, :], 0.0)
    store(5, slice(None), grads[3][7:8, :bias_rows], 0.0)
    out_row[...] = part_row(part_list(updates), divisor)


def apply_kernel(weight_row_ref, update_row_ref, *refs):
    weights, updates, new, copies = refs[:6], refs[6:12], refs[12:18], refs[18:22]
    norms_ref, grad_norm_ref = refs[22:]
    rate = peak_rate * min(STEP_NUM / warm_steps, (warm_steps / STEP_NUM) ** 0.5)
    weight_row, update_row = jnp.sqrt(weight_row_ref[...]), jnp.sqrt(update_row_ref[...])
    lanes = lax.broadcasted_iota(jnp.int32, weight_row.shape, 1)
    ratios = rate * (weight_row / jnp.where(lanes < 18, update_row, 1.0))

    def store(number, at, part):
        value = weights[number][at] - cell(ratios, part) * updates[number][at]
        new[number][at] = value
        if number < 4:
            copies[number][at] = value.astype(bf16)

    for which in range(6):
        store(0, which, which)
    for which in range(2):
        store(1, which, 6 + which)
    store(2, slice(None), 8)
    store(3, slice(None), 9)
    for which in range(7):
        store(4, slice(which, which + 1), 10 + which)
    store(5, slice(None), 17)
    norms_ref[0:1, :] = weight_row
    norms_ref[1:2, :] = update_row
    grad_norm_ref[...] = cell(weight_row, 18)


def same(arrays, dtype=f32):
    return tuple(jax.ShapeDtypeStruct(value.shape, dtype) for value in arrays)


def whole_call(kernel, name, out_shape, *arrays):
    return pl.pallas_call(
        kernel,
        out_shape=out_shape,
        in_specs=[VM()] * len(arrays),
        out_specs=jax.tree.map(lambda _: VM(), out_shape),
        compiler_params=pltpu.CompilerParams(vmem_limit_bytes=40 << 20),
        name=name,
    )(*arrays)


def pack_kernel(cap, starts_ref, source_ref, packed_ref, padded_ref):
    rows = source_ref.shape[0]
    padded_ref[:rows, :] = source_ref[...]
    padded_ref[rows:, :] = jnp.zeros((padded_ref.shape[0] - rows, source_ref.shape[1]), f32)

    def one(target, carry):
        packed_ref[pl.ds(target, 1)] = padded_ref[pl.ds(starts_ref[target], cap), :][None]
        return carry

    lax.fori_loop(0, packed_ref.shape[0], one, 0)


def pack_rows(source, starts, cap):
    rows, width = source.shape
    return pl.pallas_call(
        functools.partial(pack_kernel, cap),
        out_shape=jax.ShapeDtypeStruct((starts.shape[0], cap, width), f32),
        in_specs=[SM(), VM()],
        out_specs=VM(),
        scratch_shapes=[pltpu.VMEM((rows + cap, width), f32)],
        name="pack_rows",
    )(starts, source)


def unpack_kernel(slots_ref, arrived_ref, out_ref):
    def one(step, carry):
        for k in range(8):
            row = step * 8 + k
            out_ref[pl.ds(row, 1), :] = arrived_ref[pl.ds(slots_ref[row], 1), :]
        return carry

    lax.fori_loop(0, out_ref.shape[0] // 8, one, 0)


def unpack_rows(arrived, slots):
    return pl.pallas_call(
        unpack_kernel,
        out_shape=jax.ShapeDtypeStruct((slots.shape[0], arrived.shape[1]), f32),
        in_specs=[SM(), VM()],
        out_specs=VM(),
        name="unpack_rows",
    )(slots, arrived)


def place_back_kernel(slots_ref, grads_ref, out_ref):
    out_ref[...] = jnp.zeros_like(out_ref)

    def one(step, carry):
        for k in range(8):
            row = step * 8 + k
            out_ref[pl.ds(slots_ref[row], 1), :] = grads_ref[pl.ds(row, 1), :]
        return carry

    lax.fori_loop(0, grads_ref.shape[0] // 8, one, 0)


def place_back(grads_in, slots, total):
    return pl.pallas_call(
        place_back_kernel,
        out_shape=jax.ShapeDtypeStruct((total, grads_in.shape[1]), f32),
        in_specs=[SM(), VM()],
        out_specs=VM(),
        name="place_back",
    )(slots, grads_in)


def return_kernel(starts_ref, returned_ref, out_ref, padded_ref):
    cap = returned_ref.shape[1]

    def one(target, carry):
        padded_ref[pl.ds(starts_ref[target], cap), :] = returned_ref[pl.ds(target, 1)][0]
        return carry

    lax.fori_loop(0, returned_ref.shape[0], one, 0)
    out_ref[...] = padded_ref[: out_ref.shape[0], :]


def return_rows(returned, starts, rows):
    _, cap, width = returned.shape
    return pl.pallas_call(
        return_kernel,
        out_shape=jax.ShapeDtypeStruct((rows, width), f32),
        in_specs=[SM(), VM()],
        out_specs=VM(),
        scratch_shapes=[pltpu.VMEM((rows + cap, width), f32)],
        name="return_rows",
    )(starts, returned)


def cube_scatter(both):
    return [both[0]] + [flip(both[r], "dp", 2 * r) for r in range(1, both.shape[0])]


def shards(
    layer_input,
    encoder_memory,
    output_grad,
    target_lengths,
    memory_lengths,
    source_slots,
    pair_counts,
    attend_input,
    attend_output,
    expand_weight,
    reduce_weight,
    norm_vectors,
    expand_bias,
    attend_input_first,
    attend_input_second,
    attend_output_first,
    attend_output_second,
    expand_weight_first,
    expand_weight_second,
    reduce_weight_first,
    reduce_weight_second,
    norm_vectors_first,
    norm_vectors_second,
    expand_bias_first,
    expand_bias_second,
):
    data_count = lax.axis_size("dp")
    model_count = lax.axis_size("mp")
    me = lax.axis_index("dp")
    model = lax.axis_index("mp")
    tok_rows, width = layer_input.shape
    rows, columns = attend_input.shape[1:]
    units = expand_weight.shape[1]
    attend_output, attend_output_first, attend_output_second = [
        value.transpose(0, 2, 1) for value in (attend_output, attend_output_first, attend_output_second)
    ]
    reduce_weight, reduce_weight_first, reduce_weight_second = [
        value.T for value in (reduce_weight, reduce_weight_first, reduce_weight_second)
    ]
    weights = (attend_input, attend_output, expand_weight, reduce_weight, norm_vectors, expand_bias)

    extra_slots = tok_rows // 16
    slot_cap = (tok_rows - data_count // 4 * extra_slots) // data_count + extra_slots
    my_counts = lax.dynamic_index_in_dim(pair_counts, me, 0, keepdims=False)
    my_starts = jnp.cumsum(my_counts) - my_counts
    arrived = lax.all_to_all(
        pack_rows(encoder_memory, my_starts, slot_cap), "dp", split_axis=0, concat_axis=0, tiled=True
    )

    bias_rows = expand_bias.shape[0]
    vectors = jnp.concatenate(
        [
            jnp.pad(norm_vectors, ((0, 0), (0, columns - rows))),
            jnp.pad(expand_bias[None], ((0, 0), (0, columns - bias_rows))),
        ],
        axis=0,
    )
    own_self = jnp.concatenate(
        [attend_input[:3].reshape(3 * rows, columns), attend_output[0], vectors], axis=0
    )
    own_cross = jnp.concatenate(
        [attend_input[3:].reshape(3 * rows, columns), attend_output[1], vectors], axis=0
    )
    own_wide = jnp.concatenate([expand_weight, reduce_weight], axis=0)
    index = jnp.stack([me, model])
    together = lax.optimization_barrier
    memory_own = unpack_rows(arrived.reshape(data_count * slot_cap, columns), source_slots)
    self_ring, own_cross, memory_own, own_wide = together(
        (ring_gather(own_self), own_cross, memory_own, own_wide)
    )
    all_wide = lax.all_gather(own_wide, ("dp", "mp"))
    memory_ring = ring_gather(memory_own)
    self_even, cross_ring, memory_ring[1], memory_ring[-1] = together(
        (even_gather(jnp.stack(self_ring)), ring_gather(own_cross), memory_ring[1], memory_ring[-1])
    )
    self_pieces = odd_gather(self_even)
    cross_even = even_gather(jnp.stack(cross_ring))
    self_full, all_vectors = place(self_pieces, index, 4, rows, columns, bias_rows)
    all_wide = all_wide.reshape(data_count, model_count, 2 * rows, units)
    full_vectors = all_vectors[0]

    self_ranges = key_ranges(target_lengths[0], target_lengths[0], tok_rows)
    cross_ranges = key_ranges(target_lengths[0], memory_lengths[0], tok_rows)

    self_query = matmul(layer_input, self_full[0])
    self_key = matmul(layer_input, self_full[1])
    self_value = matmul(layer_input, self_full[2])
    self_out, self_totals = attend(self_query, self_key, self_value, self_ranges, HD)
    self_out, memory_ring, cross_even = together((self_out, memory_ring, cross_even))
    cross_full, _ = place(odd_gather(cross_even), index, 4, rows, columns, bias_rows)
    memory_target = jnp.concatenate(ring_order(memory_ring), axis=1)
    self_mix = matmul(self_out, self_full[3].T)
    first_sum = layer_input + self_mix
    first_norm = layer_norm(first_sum, full_vectors[0], full_vectors[3])
    cross_query = matmul(first_norm, cross_full[0])
    cross_key = matmul(memory_target, cross_full[1])
    cross_value = matmul(memory_target, cross_full[2])
    cross_out, cross_totals = attend(cross_query, cross_key, cross_value, cross_ranges, HD)
    cross_mix = matmul(cross_out, cross_full[3].T)
    second_sum = first_norm + cross_mix
    second_norm = layer_norm(second_sum, full_vectors[1], full_vectors[4])
    layer_output, second_grad, grad_wide, wide_sums, grad_bias = feed_forward(
        model,
        second_norm,
        output_grad,
        all_wide,
        all_vectors,
        rows,
    )

    grad_wide = lax.psum_scatter(
        grad_wide.reshape(data_count, rows, 2 * units), "dp", scatter_dimension=0, tiled=False
    )
    keep, send, resid_one_grad, memory_grad_own = cross_back(
        index,
        cross_ranges,
        second_grad,
        second_sum,
        first_sum,
        memory_target,
        cross_query,
        cross_key,
        cross_value,
        cross_out,
        cross_totals,
        cross_full,
        all_vectors,
        wide_sums,
        grad_bias,
        HD,
        columns,
        rows,
        bias_rows,
    )
    placed = place_back(memory_grad_own, source_slots, data_count * slot_cap)
    resid_one_grad, placed, both = together((resid_one_grad, placed, keep + flip(send, "dp", 1)))
    returned = lax.all_to_all(
        placed.reshape(data_count, slot_cap, columns), "dp", split_axis=0, concat_axis=0, tiled=True
    )
    grad_cross = cube_scatter(both)
    keep, send, self_query_grad, self_key_grad, self_value_grad = self_back(
        index,
        self_ranges,
        resid_one_grad,
        layer_input,
        self_query,
        self_key,
        self_value,
        self_out,
        self_totals,
        self_full,
        HD,
        columns,
        rows,
    )
    keep, send, returned, grad_cross = together((keep, send, returned, grad_cross))
    grad_self = cube_scatter(keep + flip(send, "dp", 1))
    memory_grad = return_rows(returned, my_starts, tok_rows)
    input_grad = (
        resid_one_grad
        + matmul(self_query_grad, self_full[0].T)
        + matmul(self_key_grad, self_full[1].T)
        + matmul(self_value_grad, self_full[2].T)
    )

    weights = weights[:5] + (expand_bias[None],)
    firsts = (
        attend_input_first,
        attend_output_first,
        expand_weight_first,
        reduce_weight_first,
        norm_vectors_first,
        expand_bias_first[None],
    )
    seconds = (
        attend_input_second,
        attend_output_second,
        expand_weight_second,
        reduce_weight_second,
        norm_vectors_second,
        expand_bias_second[None],
    )
    row_shape = jax.ShapeDtypeStruct((1, 128), f32)
    grad_self, grad_cross, grad_vectors, row = whole_call(
        functools.partial(squares_kernel, model_count, len(grad_self)),
        "squares",
        same(grad_self[:1] * 2) + (jax.ShapeDtypeStruct((8, rows), f32), row_shape),
        *grad_self,
        *grad_cross,
        grad_wide,
        *weights,
    )
    row, input_grad = together((small_total(row), input_grad))
    moved = whole_call(
        functools.partial(moments_kernel, model_count, columns),
        "moments",
        same(weights) * 3 + (row_shape,),
        row,
        grad_self,
        grad_cross,
        grad_wide,
        grad_vectors,
        *weights,
        *firsts,
        *seconds,
    )
    new_firsts, new_seconds, updates = moved[:6], moved[6:12], moved[12:18]
    applied = whole_call(
        apply_kernel,
        "apply",
        same(weights)
        + same(weights[:4], bf16)
        + (jax.ShapeDtypeStruct((2, 128), f32), jax.ShapeDtypeStruct((1, 1), f32)),
        row,
        small_total(moved[18]),
        *weights,
        *updates,
    )
    new_weights = applied[:5] + (applied[5][0],)
    matrix_norms = applied[10][:, :10]

    def turned(values):
        return (values[0], values[1].transpose(0, 2, 1), values[2], values[3].T) + tuple(values[4:])

    new_weights, copies = turned(new_weights), turned(applied[6:10])
    new_firsts, new_seconds = turned(new_firsts), turned(new_seconds)
    return (
        layer_output,
        input_grad,
        memory_grad,
        applied[11][0],
        *new_weights,
        *copies,
        new_firsts[0],
        new_seconds[0],
        new_firsts[1],
        new_seconds[1],
        new_firsts[2],
        new_seconds[2],
        new_firsts[3],
        new_seconds[3],
        new_firsts[4],
        new_seconds[4],
        new_firsts[5][0],
        new_seconds[5][0],
        matrix_norms,
    )


def solution(mesh):
    in_specs = (
        P("dp", None),
        P("dp", "mp"),
        P("dp", None),
        P("dp", None),
        P("dp", None),
        P("dp"),
        P(),
        P(None, "dp", "mp"),
        P(None, "mp", "dp"),
        P("dp", "mp"),
        P("mp", "dp"),
        P(None, "dp"),
        P(("mp", "dp")),
        P(None, "dp", "mp"),
        P(None, "dp", "mp"),
        P(None, "mp", "dp"),
        P(None, "mp", "dp"),
        P("dp", "mp"),
        P("dp", "mp"),
        P("mp", "dp"),
        P("mp", "dp"),
        P(None, "dp"),
        P(None, "dp"),
        P(("mp", "dp")),
        P(("mp", "dp")),
    )
    out_specs = (
        P("dp", None),
        P("dp", None),
        P("dp", "mp"),
        P(),
        P(None, "dp", "mp"),
        P(None, "mp", "dp"),
        P("dp", "mp"),
        P("mp", "dp"),
        P(None, "dp"),
        P(("mp", "dp")),
        P(None, "dp", "mp"),
        P(None, "mp", "dp"),
        P("dp", "mp"),
        P("mp", "dp"),
        P(None, "dp", "mp"),
        P(None, "dp", "mp"),
        P(None, "mp", "dp"),
        P(None, "mp", "dp"),
        P("dp", "mp"),
        P("dp", "mp"),
        P("mp", "dp"),
        P("mp", "dp"),
        P(None, "dp"),
        P(None, "dp"),
        P(("mp", "dp")),
        P(("mp", "dp")),
        P(),
    )
    return jax.shard_map(shards, mesh=mesh, in_specs=in_specs, out_specs=out_specs, check_vma=False)
```

```python
import functools

import jax
import jax.numpy as jnp
from jax import lax
from jax.experimental import pallas as pl
from jax.experimental.pallas import tpu as pltpu
from jax.sharding import PartitionSpec as P

HD = 64
STEP_NUM = 6

norm_eps = 1e-05
adam_eps = 1e-06
first_decay = 0.5
second_decay = 0.5
matrix_decay = 0.01
peak_rate = 0.6
warm_steps = 8.0
clip_norm = 1.0

bf16 = jnp.bfloat16
f32 = jnp.float32
neg_large = -1e30
q_rows = 128
key_rows = 256
pair_lanes = 128


def split_two(values):
    high = values.astype(bf16)
    return high, (values - high.astype(f32)).astype(bf16)


def dot_nn(left_side, right_side):
    return lax.dot_general(left_side, right_side, (((1,), (0,)), ((), ())), preferred_element_type=f32)


def dot_nt(left_side, right_side):
    return lax.dot_general(left_side, right_side, (((1,), (1,)), ((), ())), preferred_element_type=f32)


def dot_tn(left_side, right_side):
    return lax.dot_general(left_side, right_side, (((0,), (0,)), ((), ())), preferred_element_type=f32)


def three(dot, left_pair, right_pair):
    return (
        dot(left_pair[0], right_pair[0])
        + dot(left_pair[1], right_pair[0])
        + dot(left_pair[0], right_pair[1])
    )


def swap_halves(tile):
    return pltpu.roll(tile, pair_lanes // 2, 1)


def parts_of(tile):
    high = tile.astype(bf16).astype(f32)
    return high, tile - high


def query_packs(tile, low_half):
    high, low = parts_of(tile)
    high_swap, low_swap = swap_halves(high), swap_halves(low)
    zero = jnp.zeros_like(tile)
    first = jnp.concatenate(
        [jnp.where(low_half, high, high_swap), jnp.where(low_half, low, zero)], axis=1
    )
    second = jnp.concatenate(
        [jnp.where(low_half, high_swap, high), jnp.where(low_half, low_swap, zero)], axis=1
    )
    return first.astype(bf16), second.astype(bf16)


def key_packs(tile, low_half):
    high, low = parts_of(tile)
    high_swap, low_swap = swap_halves(high), swap_halves(low)
    zero = jnp.zeros_like(tile)
    first = jnp.concatenate(
        [jnp.where(low_half, high, low_swap), jnp.where(low_half, high, zero)], axis=1
    )
    second = jnp.concatenate(
        [jnp.where(low_half, high_swap, low), jnp.where(low_half, high_swap, zero)], axis=1
    )
    return first.astype(bf16), second.astype(bf16)


def both_parts(tile):
    high, low = split_two(tile)
    return jnp.concatenate([high, low], axis=1)


def stack_heads(tile, low_half):
    return jnp.concatenate([jnp.where(low_half, tile, 0.0), jnp.where(low_half, 0.0, tile)], axis=0)


def merge_heads(stacked, low_half):
    return jnp.where(low_half, stacked[:q_rows], stacked[q_rows:])


def folded(dot, left_pair, right_both):
    wide = dot(left_pair[0], right_both)
    return wide[:, :pair_lanes] + wide[:, pair_lanes:] + dot(left_pair[1], right_both[:, :pair_lanes])


def prepare_rows(at, source_ref, low_half, pack_ref, both_ref):
    for pair in range(source_ref.shape[1] // pair_lanes):
        tile = source_ref[at, pair * pair_lanes : (pair + 1) * pair_lanes]
        if pack_ref is not None:
            first, second = key_packs(tile, low_half)
            pack_ref[2 * pair, at, :] = first
            pack_ref[2 * pair + 1, at, :] = second
        if both_ref is not None:
            both_ref[pair, at, :] = both_parts(tile)


def clear_pad(rows, *refs):
    for ref in refs:
        ref[:, rows:, :] = jnp.zeros((ref.shape[0], ref.shape[1] - rows, ref.shape[2]), bf16)


def half_mask(rows):
    return lax.broadcasted_iota(jnp.int32, (rows, pair_lanes), 1) < pair_lanes // 2


def chunks(rows, size, body):
    def one(step, carry):
        body(pl.ds(pl.multiple_of(step * size, size), size))
        return carry

    lax.fori_loop(0, rows // size, one, 0)


def attend_kernel(
    unroll, scale, block_low, block_count,
    q_ref, k_ref, v_ref, low_ref, high_ref,
    o_ref, total_ref,
    kp_ref, vb_ref,
):
    rows, width = q_ref.shape
    lanes = lax.broadcasted_iota(jnp.int32, (q_rows, pair_lanes), 1)
    low_half = lanes < pair_lanes // 2
    clear_pad(rows, kp_ref, vb_ref)

    def before(at):
        prepare_rows(at, k_ref, low_half, kp_ref, None)
        prepare_rows(at, v_ref, low_half, None, vb_ref)

    chunks(rows, q_rows, before)
    groups = width // pair_lanes // unroll
    key_iota = lax.broadcasted_iota(jnp.int32, (q_rows, key_rows), 1)

    def block(index, carry):
        at = pl.ds(pl.multiple_of(index * q_rows, q_rows), q_rows)
        first = low_ref[at, :]
        last = high_ref[at, :]
        for group in range(groups):
            pairs = [group * unroll + u for u in range(unroll)]

            def load(u):
                lanes_of = slice(pairs[u] * pair_lanes, (pairs[u] + 1) * pair_lanes)
                return query_packs(q_ref[at, lanes_of] * scale, low_half)

            def chunk(step, state, held_packs=None):
                start = pl.multiple_of(block_low[index] + step * key_rows, 16)
                here = pl.ds(start, key_rows)
                places = key_iota + start
                bias = jnp.where(jnp.logical_and(places >= first, places < last), 0.0, neg_large)
                bias = jnp.concatenate([bias, bias], axis=0)
                out, found = [], []
                for u, p in enumerate(pairs):
                    query = load(u) if held_packs is None else held_packs[u]
                    found.append(
                        jnp.concatenate(
                            [dot_nt(query[h], kp_ref[2 * p + h, here, :]) for h in range(2)], axis=0
                        )
                    )
                for u, p in enumerate(pairs):
                    scores = bias + found[u]
                    new_top = jnp.max(scores, axis=1, keepdims=True)
                    if state is not None:
                        top, total, held = state[u]
                        new_top = jnp.maximum(top, new_top)
                        shrink = jnp.exp(top - new_top)
                    weights = jnp.exp(scores - new_top)
                    new_total = jnp.sum(weights, axis=1, keepdims=True)
                    new_held = folded(dot_nn, split_two(weights), vb_ref[p, here, :])
                    if state is not None:
                        new_total = total * shrink + new_total
                        new_held = held * shrink + new_held
                    out.append((new_top, new_total, new_held))
                return tuple(out)

            def finish(state):
                tile = total_ref[at, :] if group else jnp.zeros((q_rows, pair_lanes), f32)
                for u, p in enumerate(pairs):
                    top, total, held = state[u]
                    o_ref[at, p * pair_lanes : (p + 1) * pair_lanes] = merge_heads(held / total, low_half)
                    logs = top + jnp.log(total)
                    tile = jnp.where(lanes == 2 * p, logs[:q_rows], tile)
                    tile = jnp.where(lanes == 2 * p + 1, logs[q_rows:], tile)
                total_ref[at, :] = tile

            @pl.when(block_count[index] == 1)
            def _():
                finish(chunk(0, None))

            @pl.when(block_count[index] > 1)
            def _():
                start_state = tuple(
                    (
                        jnp.full((2 * q_rows, 1), neg_large, f32),
                        jnp.zeros((2 * q_rows, 1), f32),
                        jnp.zeros((2 * q_rows, pair_lanes), f32),
                    )
                    for _ in range(unroll)
                )
                packs = [load(u) for u in range(unroll)]
                step = lambda number, state: chunk(number, state, packs)
                finish(lax.fori_loop(0, block_count[index], step, start_state))

        return carry

    lax.fori_loop(0, rows // q_rows, block, 0)


def attend_back_blocks(
    unroll, scale, block_low, block_count,
    q_ref, o_ref, g_ref, total_ref, low_ref, high_ref,
    dq_ref, kp_ref, vp_ref, kb_ref, dk_sum, dv_sum,
):
    rows, width = q_ref.shape
    lanes = lax.broadcasted_iota(jnp.int32, (q_rows, pair_lanes), 1)
    low_half = lanes < pair_lanes // 2
    groups = width // pair_lanes // unroll
    key_iota = lax.broadcasted_iota(jnp.int32, (q_rows, key_rows), 1)

    def block(index, carry):
        at = pl.ds(pl.multiple_of(index * q_rows, q_rows), q_rows)
        first = low_ref[at, :]
        last = high_ref[at, :]
        total_tile = total_ref[at, :]
        for group in range(groups):
            pairs = [group * unroll + u for u in range(unroll)]

            def column(mask, value):
                return jnp.sum(jnp.where(mask, value, 0.0), axis=1, keepdims=True)

            def load(u):
                p = pairs[u]
                lanes_of = slice(p * pair_lanes, (p + 1) * pair_lanes)
                query = q_ref[at, lanes_of] * scale
                grad = g_ref[at, lanes_of]
                product = grad * o_ref[at, lanes_of]
                dots = [column(low_half, product), column(jnp.logical_not(low_half), product)]
                logs = [column(lanes == 2 * p, total_tile), column(lanes == 2 * p + 1, total_tile)]
                return (
                    query_packs(query, low_half),
                    query_packs(grad, low_half),
                    both_parts(stack_heads(query, low_half)),
                    both_parts(stack_heads(grad, low_half)),
                    jnp.concatenate(logs, axis=0),
                    jnp.concatenate(dots, axis=0),
                )

            def chunk(step, state, held_packs=None):
                start = pl.multiple_of(block_low[index] + step * key_rows, 16)
                here = pl.ds(start, key_rows)
                places = key_iota + start
                bias = jnp.where(jnp.logical_and(places >= first, places < last), 0.0, neg_large)
                bias = jnp.concatenate([bias, bias], axis=0)
                out, packs, found = [], [], []
                for u, p in enumerate(pairs):
                    packs.append(load(u) if held_packs is None else held_packs[u])
                    found.append(
                        [
                            jnp.concatenate(
                                [dot_nt(packs[u][k][h], ref[2 * p + h, here, :]) for h in range(2)], axis=0
                            )
                            for k, ref in enumerate((kp_ref, vp_ref))
                        ]
                    )
                for u, p in enumerate(pairs):
                    lanes_of = slice(p * pair_lanes, (p + 1) * pair_lanes)
                    _, _, query_both, grad_both, logs, dots = packs[u]
                    weights = jnp.exp(bias + found[u][0] - logs)
                    grad_scores = split_two(weights * (found[u][1] - dots))
                    new_state = folded(dot_nn, grad_scores, kb_ref[p, here, :])
                    out.append(new_state if state is None else state[u] + new_state)
                    dk_sum[here, lanes_of] += folded(dot_tn, grad_scores, query_both)
                    dv_sum[here, lanes_of] += folded(dot_tn, split_two(weights), grad_both)
                return tuple(out)

            def finish(state):
                for u, p in enumerate(pairs):
                    dq_ref[at, p * pair_lanes : (p + 1) * pair_lanes] = merge_heads(state[u], low_half) * scale

            @pl.when(block_count[index] == 1)
            def _():
                finish(chunk(0, None))

            @pl.when(block_count[index] > 1)
            def _():
                start_state = tuple(jnp.zeros((2 * q_rows, pair_lanes), f32) for _ in range(unroll))
                packs = [load(u) for u in range(unroll)]
                step = lambda number, state: chunk(number, state, packs)
                finish(lax.fori_loop(0, block_count[index], step, start_state))

        return carry

    lax.fori_loop(0, rows // q_rows, block, 0)


def own_lanes(ref, at, model, columns):
    if columns % pair_lanes == 0:
        return ref[at, pl.ds(pl.multiple_of(model * columns, pair_lanes), columns)]
    start = model * columns
    base = pl.multiple_of(start // pair_lanes * pair_lanes, pair_lanes)
    tile = ref[at, pl.ds(base, pair_lanes)]
    return pltpu.roll(tile, lax.rem(pair_lanes - lax.rem(start, pair_lanes), pair_lanes), 1)[:, :columns]


def norm_parts(values):
    centred = values - jnp.mean(values, axis=1, keepdims=True)
    scale = lax.rsqrt(jnp.mean(centred * centred, axis=1, keepdims=True) + norm_eps)
    return centred * scale, scale


def norm_back(grad, normal, scale, gain):
    inner = grad * gain
    return (
        inner
        - jnp.mean(inner, axis=1, keepdims=True)
        - normal * jnp.mean(inner * normal, axis=1, keepdims=True)
    ) * scale


def column_sum(value):
    return jnp.sum(value, axis=0, keepdims=True)


def hand_out(index_ref, grads_ref, keep_ref, send_ref, rows, extra_ref=None):
    me = index_ref[0]
    odd = lax.rem(me, 2)
    for r in range(keep_ref.shape[0]):
        pair = 2 * ((me // 2) ^ r)
        for ref, which in ((keep_ref, pair + odd), (send_ref, pair + 1 - odd)):
            ref[r, :rows, :] = grads_ref[pl.ds(pl.multiple_of(which * rows, rows), rows), :]
            if extra_ref is not None:
                ref[r, rows:, :] = extra_ref[pl.ds(which, 1)][0]


def cross_back_kernel(
    unroll, scale, columns, rows_of, bias_rows, index_ref, block_low, block_count,
    g_ref, two_ref, one_ref, mem_ref, q_ref, k_ref, v_ref, o_ref, total_ref, low_ref, high_ref,
    w_ref, vec_ref, sums_ref, bias_ref,
    keep_ref, send_ref, resid_ref, mem_grad_ref,
    kp_ref, vp_ref, kb_ref, dk_sum, dv_sum, dq_ref, go_ref, two_grad_ref, woh, wol, wqh, wql, grads, totals, parts,
):
    rows, width = q_ref.shape
    model = index_ref[1]
    mask = half_mask(256)
    clear_pad(rows, kp_ref, vp_ref, kb_ref)
    dk_sum[...] = jnp.zeros_like(dk_sum)
    dv_sum[...] = jnp.zeros_like(dv_sum)
    woh[...], wol[...] = split_two(w_ref[3])
    wqh[...], wql[...] = split_two(w_ref[0])
    totals[...] = sums_ref[...]
    grads[...] = jnp.zeros_like(grads)

    def before(at):
        normal, spread = norm_parts(two_ref[at, :])
        grad = g_ref[at, :]
        resid = norm_back(grad, normal, spread, vec_ref[0, 1:2, :])
        totals[1:2, :] += column_sum(grad * normal)
        totals[4:5, :] += column_sum(grad)
        two_grad_ref[at, :] = resid
        go_ref[at, :] = three(dot_nn, split_two(resid), (woh[...], wol[...]))
        prepare_rows(at, k_ref, mask, kp_ref, kb_ref)
        prepare_rows(at, v_ref, mask, vp_ref, None)

    chunks(rows, 256, before)
    attend_back_blocks(
        unroll, scale, block_low, block_count,
        q_ref, o_ref, go_ref, total_ref, low_ref, high_ref,
        dq_ref, kp_ref, vp_ref, kb_ref, dk_sum, dv_sum,
    )

    def after(at):
        resid = two_grad_ref[at, :]
        grad = resid + three(dot_nt, split_two(dq_ref[at, :]), (wqh[...], wql[...]))
        normal, spread = norm_parts(one_ref[at, :])
        gain = vec_ref[0, 0:1, :]
        resid_ref[at, :] = norm_back(grad, normal, spread, gain)
        totals[0:1, :] += column_sum(grad * normal)
        totals[3:4, :] += column_sum(grad)
        source = split_two(normal * gain + vec_ref[0, 3:4, :])
        memory = split_two(mem_ref[at, :])
        dk = dk_sum[at, :]
        dv = dv_sum[at, :]
        grads[:, :columns] += three(dot_tn, source, split_two(own_lanes(dq_ref, at, model, columns)))
        both = jnp.concatenate([own_lanes(ref, at, model, columns) for ref in (dk_sum, dv_sum)], axis=1)
        grads[:, columns : 3 * columns] += three(dot_tn, memory, split_two(both))
        grads[:, 3 * columns :] += three(
            dot_tn, split_two(resid), split_two(own_lanes(o_ref, at, model, columns))
        )
        slice_of = pl.ds(pl.multiple_of(model * columns, columns), columns)
        mem_grad_ref[at, :] = three(dot_nt, split_two(dk), split_two(w_ref[1, slice_of, :])) + three(
            dot_nt, split_two(dv), split_two(w_ref[2, slice_of, :])
        )

    chunks(rows, 256, after)
    parts[...] = jnp.zeros_like(parts)
    for j in range(parts.shape[0]):
        parts[j, :, :rows_of] = totals[:, j * rows_of : (j + 1) * rows_of]
        parts[j, 7:8, :bias_rows] = bias_ref[:, j * bias_rows : (j + 1) * bias_rows]
    hand_out(index_ref, grads, keep_ref, send_ref, rows_of, parts)


def self_back_kernel(
    unroll, scale, columns, rows_of, index_ref, block_low, block_count,
    g_ref, x_ref, q_ref, k_ref, v_ref, o_ref, total_ref, low_ref, high_ref, w_ref,
    keep_ref, send_ref, dq_ref, dk_ref, dv_ref,
    kp_ref, vp_ref, kb_ref, dk_sum, dv_sum, go_ref, woh, wol, grads,
):
    rows, width = q_ref.shape
    model = index_ref[1]
    mask = half_mask(256)
    clear_pad(rows, kp_ref, vp_ref, kb_ref)
    dk_sum[...] = jnp.zeros_like(dk_sum)
    dv_sum[...] = jnp.zeros_like(dv_sum)
    woh[...], wol[...] = split_two(w_ref[3])
    grads[...] = jnp.zeros_like(grads)

    def before(at):
        go_ref[at, :] = three(dot_nn, split_two(g_ref[at, :]), (woh[...], wol[...]))
        prepare_rows(at, k_ref, mask, kp_ref, kb_ref)
        prepare_rows(at, v_ref, mask, vp_ref, None)

    chunks(rows, 256, before)
    attend_back_blocks(
        unroll, scale, block_low, block_count,
        q_ref, o_ref, go_ref, total_ref, low_ref, high_ref,
        dq_ref, kp_ref, vp_ref, kb_ref, dk_sum, dv_sum,
    )

    def after(at):
        source = split_two(x_ref[at, :])
        dk_ref[at, :] = dk_sum[at, :]
        dv_ref[at, :] = dv_sum[at, :]
        every = [own_lanes(ref, at, model, columns) for ref in (dq_ref, dk_sum, dv_sum)]
        grads[:, : 3 * columns] += three(dot_tn, source, split_two(jnp.concatenate(every, axis=1)))
        grads[:, 3 * columns :] += three(
            dot_tn, split_two(g_ref[at, :]), split_two(own_lanes(o_ref, at, model, columns))
        )

    chunks(rows, 256, after)
    hand_out(index_ref, grads, keep_ref, send_ref, rows_of)


VM = functools.partial(pl.BlockSpec, memory_space=pltpu.VMEM)
SM = functools.partial(pl.BlockSpec, memory_space=pltpu.SMEM)


def attend(queries, keys_in, values_in, ranges, head_size, unroll=4):
    block_low, block_count, low, high = ranges
    rows, width = queries.shape
    pad_rows = keys_in.shape[0] + key_rows
    return pl.pallas_call(
        functools.partial(attend_kernel, unroll, head_size ** -0.5),
        out_shape=(
            jax.ShapeDtypeStruct((rows, width), f32),
            jax.ShapeDtypeStruct((rows, pair_lanes), f32),
        ),
        in_specs=[SM(), SM()] + [VM()] * 5,
        out_specs=(VM(), VM()),
        scratch_shapes=[
            pltpu.VMEM((width // 64, pad_rows, 2 * pair_lanes), bf16),
            pltpu.VMEM((width // pair_lanes, pad_rows, 2 * pair_lanes), bf16),
        ],
        compiler_params=pltpu.CompilerParams(vmem_limit_bytes=48 << 20),
        cost_estimate=pl.CostEstimate(flops=12 * rows * key_rows * width, bytes_accessed=16 * rows * width, transcendentals=rows * key_rows * 8),
        name="attend",
    )(block_low, block_count, queries, keys_in, values_in, low, high)


def back_scratch(rows, width):
    pad_rows = rows + key_rows
    return [
        pltpu.VMEM((width // 64, pad_rows, 2 * pair_lanes), bf16),
        pltpu.VMEM((width // 64, pad_rows, 2 * pair_lanes), bf16),
        pltpu.VMEM((width // pair_lanes, pad_rows, 2 * pair_lanes), bf16),
        pltpu.VMEM((pad_rows, width), f32),
        pltpu.VMEM((pad_rows, width), f32),
    ]


def cross_back(
    index, ranges, grad, two, one, memory, queries, keys_in, values_in, outputs, totals,
    matrices, vectors, sums, bias, head_size, columns, rows_of, bias_rows, unroll=4,
):
    block_low, block_count, low, high = ranges
    rows, width = queries.shape
    data = width // rows_of
    block = jax.ShapeDtypeStruct((data // 2, rows_of + 8, 4 * columns), f32)
    return pl.pallas_call(
        functools.partial(cross_back_kernel, unroll, head_size ** -0.5, columns, rows_of, bias_rows),
        out_shape=(
            block,
            block,
            jax.ShapeDtypeStruct((rows, width), f32),
            jax.ShapeDtypeStruct((rows, columns), f32),
        ),
        in_specs=[SM()] * 3 + [VM()] * 15,
        out_specs=(VM(),) * 4,
        scratch_shapes=back_scratch(rows, width)
        + [pltpu.VMEM((rows, width), f32)] * 3
        + [pltpu.VMEM((width, width), bf16)] * 4
        + [
            pltpu.VMEM((width, 4 * columns), f32),
            pltpu.VMEM((8, width), f32),
            pltpu.VMEM((data, 8, 4 * columns), f32),
        ],
        compiler_params=pltpu.CompilerParams(vmem_limit_bytes=60 << 20),
        cost_estimate=pl.CostEstimate(flops=30 << 30, bytes_accessed=30 << 20, transcendentals=rows * key_rows * 8),
        name="cross_back",
    )(
        index, block_low, block_count, grad, two, one, memory, queries, keys_in, values_in, outputs, totals,
        low, high, matrices, vectors, sums, bias,
    )


def self_back(
    index, ranges, grad, source, queries, keys_in, values_in, outputs, totals, matrices,
    head_size, columns, rows_of, unroll=4,
):
    block_low, block_count, low, high = ranges
    rows, width = queries.shape
    data = width // rows_of
    block = jax.ShapeDtypeStruct((data // 2, rows_of, 4 * columns), f32)
    return pl.pallas_call(
        functools.partial(self_back_kernel, unroll, head_size ** -0.5, columns, rows_of),
        out_shape=(block, block) + (jax.ShapeDtypeStruct((rows, width), f32),) * 3,
        in_specs=[SM()] * 3 + [VM()] * 10,
        out_specs=(VM(),) * 5,
        scratch_shapes=back_scratch(rows, width)
        + [pltpu.VMEM((rows, width), f32)]
        + [pltpu.VMEM((width, width), bf16)] * 2
        + [pltpu.VMEM((width, 4 * columns), f32)],
        compiler_params=pltpu.CompilerParams(vmem_limit_bytes=60 << 20),
        cost_estimate=pl.CostEstimate(flops=30 << 30, bytes_accessed=30 << 20, transcendentals=rows * key_rows * 8),
        name="self_back",
    )(
        index, block_low, block_count, grad, source, queries, keys_in, values_in, outputs, totals,
        low, high, matrices,
    )


def key_ranges(query_lengths, key_lengths, rows):
    query_ends = jnp.cumsum(query_lengths)
    query_starts = query_ends - query_lengths
    places = jnp.arange(rows, dtype=jnp.int32)
    low = jnp.sum(jnp.where(query_ends[None, :] <= places[:, None], key_lengths[None, :], 0), axis=1)
    high = jnp.sum(jnp.where(query_starts[None, :] <= places[:, None], key_lengths[None, :], 0), axis=1)
    block_low = low[::q_rows] // 16 * 16
    block_high = high[q_rows - 1 :: q_rows]
    block_count = (block_high - block_low + key_rows - 1) // key_rows
    return block_low, block_count, low[:, None], high[:, None]


def matmul(left_side, right_side):
    return jnp.dot(left_side, right_side, precision=lax.Precision.HIGH, preferred_element_type=f32)


def layer_norm(values, gain_row, shift_row):
    centre_mean = jnp.mean(values, axis=-1, keepdims=True)
    centred = values - centre_mean
    variance = jnp.mean(centred * centred, axis=-1, keepdims=True)
    return centred * lax.rsqrt(variance + norm_eps) * gain_row + shift_row


def flip(value, axis, distance):
    pairs = [(i, i ^ distance) for i in range(lax.axis_size(axis))]
    return lax.ppermute(value, axis, pairs)


def tree_total(pieces):
    while len(pieces) > 1:
        pieces = [pieces[i] + pieces[i + 1] for i in range(0, len(pieces), 2)]
    return pieces[0]


def small_total(value):
    value = value + flip(value, "dp", 1)
    others = lax.axis_size("dp") // 2
    value = tree_total([value] + [flip(value, "dp", 2 * r) for r in range(1, others)])
    models = lax.axis_size("mp")
    return tree_total([value] + [flip(value, "mp", r) for r in range(1, models)])


def ring_gather(own):
    count = lax.axis_size("mp")
    return [own] + [
        lax.ppermute(own, "mp", [(i, (i + step) % count) for i in range(count)])
        for step in range(1, count)
    ]


def ring_order(ring):
    count = len(ring)
    me = lax.axis_index("mp")
    found = []
    for place in range(count):
        value = ring[0]
        for step in range(1, count):
            value = jnp.where(me == (place + step) % count, ring[step], value)
        found.append(value)
    return found


def even_gather(own):
    return [own] + [flip(own, "dp", r) for r in range(2, lax.axis_size("dp"), 2)]


def odd_gather(even):
    odd = [flip(value, "dp", 1) for value in even]
    return [value for pair in zip(even, odd) for value in pair]


def place_kernel(parts, rows, columns, bias_rows, index_ref, *refs):
    pieces, (full_ref, vec_ref) = refs[:-2], refs[-2:]
    me, model = index_ref[0], index_ref[1]
    models = pieces[0].shape[0]
    width = vec_ref.shape[2]
    pad = jnp.zeros((8, width - columns), f32)
    bias_row = lax.broadcasted_iota(jnp.int32, (8, width), 0) == 7
    vec_ref[...] = jnp.zeros_like(vec_ref)
    for r, piece in enumerate(pieces):
        whose = me ^ r
        at = pl.ds(pl.multiple_of(whose * rows, rows), rows)
        for place in range(models):
            slot = lax.rem(model - place + models, models)
            for part in range(parts):
                full_ref[part, at, place * columns : (place + 1) * columns] = piece[
                    slot, part * rows : (part + 1) * rows, :
                ]
            values = jnp.concatenate([piece[slot, parts * rows :, :], pad], axis=1)
            moved = pltpu.roll(values, whose * rows, 1)
            if rows != bias_rows:
                moved = jnp.where(bias_row, pltpu.roll(values, whose * bias_rows, 1), moved)
            vec_ref[place] += moved


def place(pieces, index, parts, rows, columns, bias_rows):
    models, count = pieces[0].shape[0], len(pieces)
    return pl.pallas_call(
        functools.partial(place_kernel, parts, rows, columns, bias_rows),
        out_shape=(
            jax.ShapeDtypeStruct((parts, rows * count, columns * models), f32),
            jax.ShapeDtypeStruct((models, 8, columns * models), f32),
        ),
        in_specs=[SM()] + [VM()] * count,
        out_specs=(VM(), VM()),
        compiler_params=pltpu.CompilerParams(vmem_limit_bytes=40 << 20),
        name="place",
    )(index, *pieces)


def gelu_both(values):
    inner = 0.7978845608028654 * (values + 0.044715 * values * values * values)
    bent = jnp.tanh(inner)
    half = 0.5 * (1.0 + bent)
    slope = half + 0.5 * values * (1.0 - bent * bent) * (
        0.7978845608028654 * (1.0 + 3.0 * 0.044715 * values * values)
    )
    return values * half, slope


def wide_kernel(
    rows, model_ref, z_ref, g_ref, wide_ref, all_vec_ref,
    out_ref, second_ref, grads_ref, sums_ref, bias_grad_ref,
    eh_ref, el_ref, rh_ref, rl_ref, slope_ref, xh_ref, xl_ref, bh_ref, bl_ref,
):
    tokens, width = z_ref.shape
    data, models, _, units = wide_ref.shape
    model = model_ref[0]
    vec_ref = all_vec_ref.at[0]
    block = xh_ref.shape[0]

    def load(step, carry):
        which, part = step // models, step % models
        at = pl.ds(pl.multiple_of(which * rows, rows), rows)
        to = pl.ds(pl.multiple_of(part * units, units), units)
        eh_ref[at, to], el_ref[at, to] = split_two(wide_ref[which, part, :rows, :])
        rh_ref[at, to], rl_ref[at, to] = split_two(wide_ref[which, part, rows:, :])
        return carry

    lax.fori_loop(0, data * models, load, 0)
    sums_ref[...] = jnp.zeros_like(sums_ref)
    bias_grad_ref[...] = jnp.zeros_like(bias_grad_ref)
    grads_ref[...] = jnp.zeros_like(grads_ref)

    gain = vec_ref[2:3, :]
    half = block // 2
    halves = [slice(0, half), slice(half, block)]

    def chunk(step, carry):
        whole = pl.ds(pl.multiple_of(step * block, block), block)
        ats = [pl.ds(pl.multiple_of(step * block + h * half, half), half) for h in range(2)]
        products, resids, reduced = [None] * 2, [None] * 2, [None] * 2

        def enter(h):
            products[h] = three(dot_nn, split_two(z_ref[ats[h], :]), (eh_ref[...], el_ref[...]))

        def bend(h):
            for part in range(models):
                to = slice(part * units, (part + 1) * units)
                value, slope = gelu_both(products[h][:, to] + all_vec_ref[part, 7:8, :units])
                slope_ref[halves[h], to] = slope
                xh_ref[halves[h], to], xl_ref[halves[h], to] = split_two(value)

        def leave(h):
            reduced[h] = three(
                dot_nt, (xh_ref[halves[h], :], xl_ref[halves[h], :]), (rh_ref[...], rl_ref[...])
            )

        def turn(h):
            at = ats[h]
            normal, scale = norm_parts(z_ref[at, :] + vec_ref[6:7, :] + reduced[h])
            out_ref[at, :] = normal * gain + vec_ref[5:6, :]
            grad = g_ref[at, :]
            resids[h] = norm_back(grad, normal, scale, gain)
            sums_ref[2:3, :] += column_sum(grad * normal)
            sums_ref[5:6, :] += column_sum(grad)
            sums_ref[6:7, :] += column_sum(resids[h])

        def reenter(h):
            products[h] = three(dot_nn, split_two(resids[h]), (rh_ref[...], rl_ref[...]))

        def unbend(h):
            for part in range(models):
                to = slice(part * units, (part + 1) * units)
                back = products[h][:, to] * slope_ref[halves[h], to]
                slope_ref[halves[h], to] = back
                bh_ref[halves[h], to], bl_ref[halves[h], to] = split_two(back)

        def finish(h):
            return three(dot_nt, (bh_ref[halves[h], :], bl_ref[halves[h], :]), (eh_ref[...], el_ref[...]))

        enter(0)
        enter(1)
        bend(0)
        leave(0)
        bend(1)
        leave(1)
        turn(0)
        reenter(0)
        turn(1)
        reenter(1)
        unbend(0)
        more = finish(0)
        unbend(1)
        last = finish(1)
        second_ref[ats[0], :] = resids[0] + more
        second_ref[ats[1], :] = resids[1] + last
        to = pl.ds(pl.multiple_of(model * units, units), units)
        bias_grad_ref[...] += column_sum(slope_ref[:, to])
        grads_ref[:, :units] += three(dot_tn, split_two(z_ref[whole, :]), (bh_ref[:, to], bl_ref[:, to]))
        grads_ref[:, units:] += three(
            dot_tn, split_two(jnp.concatenate(resids, axis=0)), (xh_ref[:, to], xl_ref[:, to])
        )
        return carry

    lax.fori_loop(0, tokens // block, chunk, 0)


def feed_forward(model, source, grad, wide, vectors, rows):
    tokens, width = source.shape
    data, models, _, units = wide.shape
    block = min(512, tokens)
    return pl.pallas_call(
        functools.partial(wide_kernel, rows),
        out_shape=(
            jax.ShapeDtypeStruct((tokens, width), f32),
            jax.ShapeDtypeStruct((tokens, width), f32),
            jax.ShapeDtypeStruct((width, 2 * units), f32),
            jax.ShapeDtypeStruct((8, width), f32),
            jax.ShapeDtypeStruct((1, units), f32),
        ),
        in_specs=[SM()] + [VM()] * 4,
        out_specs=(VM(),) * 5,
        scratch_shapes=[pltpu.VMEM((width, models * units), bf16)] * 4
        + [
            pltpu.VMEM((block, models * units), f32),
        ]
        + [pltpu.VMEM((block, models * units), bf16)] * 4,
        compiler_params=pltpu.CompilerParams(vmem_limit_bytes=60 << 20),
        cost_estimate=pl.CostEstimate(
            flops=27 * tokens * width * models * units, bytes_accessed=24 << 20, transcendentals=tokens * models * units
        ),
        name="feed_forward",
    )(model[None], source, grad, wide, vectors)


def cell(row, lane):
    return jnp.sum(
        jnp.where(lax.broadcasted_iota(jnp.int32, row.shape, 1) == lane, row, 0.0), axis=1, keepdims=True
    )


def total_of(value):
    return jnp.sum(jnp.sum(value, axis=1, keepdims=True), axis=0, keepdims=True)


def put(row, lane, value):
    return jnp.where(lax.broadcasted_iota(jnp.int32, row.shape, 1) == lane, value, row)


def part_row(pieces, divisor):
    row = jnp.zeros((1, 128), f32)
    for number, value in enumerate(pieces):
        total = total_of(value * value)
        row = put(row, number, total / divisor if 10 <= number < 17 else total)
    return row


def part_list(arrays):
    return (
        [arrays[0][i] for i in range(arrays[0].shape[0])]
        + [arrays[1][i] for i in range(arrays[1].shape[0])]
        + [arrays[2][...], arrays[3][...]]
        + [arrays[4][i : i + 1, :] for i in range(arrays[4].shape[0])]
        + [arrays[5][...]]
    )


def squares_kernel(divisor, count, *refs):
    self_pieces, cross_pieces, rest = refs[:count], refs[count : 2 * count], refs[2 * count :]
    wide, weights, (self_ref, cross_ref, vector_ref, row_ref) = rest[0][...], rest[1:-4], rest[-4:]
    rows = self_ref.shape[0]
    value = tree_total([piece[...] for piece in self_pieces])
    both = tree_total([piece[...] for piece in cross_pieces])
    cross, vectors = both[:rows], both[rows:, :rows]
    self_ref[...] = value
    cross_ref[...] = cross
    vector_ref[...] = vectors
    total = total_of(value * value) + total_of(cross * cross) + total_of(wide * wide)
    norms = vectors[:7]
    last = vectors[7:8]
    total = total + total_of(norms * norms) / divisor + total_of(last * last)
    row_ref[...] = put(part_row(part_list(weights), divisor), 18, total)


def moments_kernel(divisor, columns, row_ref, *refs):
    grads, rest = refs[:4], refs[4:]
    weights, firsts, seconds = rest[:6], rest[6:12], rest[12:18]
    new_firsts, new_seconds, updates, out_row = rest[18:24], rest[24:30], rest[30:36], rest[36]
    units = rest[2].shape[1]
    bias_rows = rest[5].shape[1]
    norm = jnp.sqrt(cell(row_ref[...], 18))
    clip = jnp.minimum(1.0, clip_norm / norm)
    first_fix = 1.0 - first_decay**STEP_NUM
    second_fix = 1.0 - second_decay**STEP_NUM

    def step(grad, weight, first, second, decay):
        clipped = grad * clip
        one = first_decay * first + (1.0 - first_decay) * clipped
        two = second_decay * second + (1.0 - second_decay) * clipped * clipped
        return one, two, one / first_fix / (jnp.sqrt(two / second_fix) + adam_eps) + decay * weight

    squares = []

    def store(number, at, grad, decay):
        one, two, update = step(
            grad, weights[number][at], firsts[number][at], seconds[number][at], decay
        )
        new_firsts[number][at] = one
        new_seconds[number][at] = two
        updates[number][at] = update
        return update

    for number in range(2):
        for which in range(3):
            store(0, 3 * number + which, grads[number][:, which * columns : (which + 1) * columns], matrix_decay)
    for number in range(2):
        store(1, number, grads[number][:, 3 * columns : 4 * columns], matrix_decay)
    store(2, slice(None), grads[2][:, :units], matrix_decay)
    store(3, slice(None), grads[2][:, units:], matrix_decay)
    store(4, slice(None), grads[3][:7, :], 0.0)
    store(5, slice(None), grads[3][7:8, :bias_rows], 0.0)
    out_row[...] = part_row(part_list(updates), divisor)


def apply_kernel(weight_row_ref, update_row_ref, *refs):
    weights, updates, new, copies = refs[:6], refs[6:12], refs[12:18], refs[18:22]
    norms_ref, grad_norm_ref = refs[22:]
    rate = peak_rate * min(STEP_NUM / warm_steps, (warm_steps / STEP_NUM) ** 0.5)
    weight_row, update_row = jnp.sqrt(weight_row_ref[...]), jnp.sqrt(update_row_ref[...])
    lanes = lax.broadcasted_iota(jnp.int32, weight_row.shape, 1)
    ratios = rate * (weight_row / jnp.where(lanes < 18, update_row, 1.0))

    def store(number, at, part):
        value = weights[number][at] - cell(ratios, part) * updates[number][at]
        new[number][at] = value
        if number < 4:
            copies[number][at] = value.astype(bf16)

    for which in range(6):
        store(0, which, which)
    for which in range(2):
        store(1, which, 6 + which)
    store(2, slice(None), 8)
    store(3, slice(None), 9)
    for which in range(7):
        store(4, slice(which, which + 1), 10 + which)
    store(5, slice(None), 17)
    norms_ref[0:1, :] = weight_row
    norms_ref[1:2, :] = update_row
    grad_norm_ref[...] = cell(weight_row, 18)


def same(arrays, dtype=f32):
    return tuple(jax.ShapeDtypeStruct(value.shape, dtype) for value in arrays)


def whole_call(kernel, name, out_shape, *arrays):
    return pl.pallas_call(
        kernel,
        out_shape=out_shape,
        in_specs=[VM()] * len(arrays),
        out_specs=jax.tree.map(lambda _: VM(), out_shape),
        compiler_params=pltpu.CompilerParams(vmem_limit_bytes=40 << 20),
        name=name,
    )(*arrays)


def pack_kernel(cap, starts_ref, source_ref, packed_ref, padded_ref):
    rows = source_ref.shape[0]
    padded_ref[:rows, :] = source_ref[...]
    padded_ref[rows:, :] = jnp.zeros((padded_ref.shape[0] - rows, source_ref.shape[1]), f32)

    def one(target, carry):
        packed_ref[pl.ds(target, 1)] = padded_ref[pl.ds(starts_ref[target], cap), :][None]
        return carry

    lax.fori_loop(0, packed_ref.shape[0], one, 0)


def pack_rows(source, starts, cap):
    rows, width = source.shape
    return pl.pallas_call(
        functools.partial(pack_kernel, cap),
        out_shape=jax.ShapeDtypeStruct((starts.shape[0], cap, width), f32),
        in_specs=[SM(), VM()],
        out_specs=VM(),
        scratch_shapes=[pltpu.VMEM((rows + cap, width), f32)],
        name="pack_rows",
    )(starts, source)


def unpack_kernel(slots_ref, arrived_ref, out_ref):
    def one(step, carry):
        lines = [step * 16 + k for k in range(16)]
        found = [arrived_ref[pl.ds(slots_ref[row], 1), :] for row in lines]
        for row, value in zip(lines, found):
            out_ref[pl.ds(row, 1), :] = value
        return carry

    lax.fori_loop(0, out_ref.shape[0] // 16, one, 0)


def unpack_rows(arrived, slots):
    return pl.pallas_call(
        unpack_kernel,
        out_shape=jax.ShapeDtypeStruct((slots.shape[0], arrived.shape[1]), f32),
        in_specs=[SM(), VM()],
        out_specs=VM(),
        name="unpack_rows",
    )(slots, arrived)


def place_back_kernel(slots_ref, grads_ref, out_ref):
    out_ref[...] = jnp.zeros_like(out_ref)

    def one(step, carry):
        lines = [step * 16 + k for k in range(16)]
        found = [grads_ref[pl.ds(row, 1), :] for row in lines]
        for row, value in zip(lines, found):
            out_ref[pl.ds(slots_ref[row], 1), :] = value
        return carry

    lax.fori_loop(0, grads_ref.shape[0] // 16, one, 0)


def place_back(grads_in, slots, total):
    return pl.pallas_call(
        place_back_kernel,
        out_shape=jax.ShapeDtypeStruct((total, grads_in.shape[1]), f32),
        in_specs=[SM(), VM()],
        out_specs=VM(),
        name="place_back",
    )(slots, grads_in)


def return_kernel(starts_ref, returned_ref, out_ref, padded_ref):
    cap = returned_ref.shape[1]

    def one(target, carry):
        padded_ref[pl.ds(starts_ref[target], cap), :] = returned_ref[pl.ds(target, 1)][0]
        return carry

    lax.fori_loop(0, returned_ref.shape[0], one, 0)
    out_ref[...] = padded_ref[: out_ref.shape[0], :]


def return_rows(returned, starts, rows):
    _, cap, width = returned.shape
    return pl.pallas_call(
        return_kernel,
        out_shape=jax.ShapeDtypeStruct((rows, width), f32),
        in_specs=[SM(), VM()],
        out_specs=VM(),
        scratch_shapes=[pltpu.VMEM((rows + cap, width), f32)],
        name="return_rows",
    )(starts, returned)


def cube_scatter(both):
    return [both[0]] + [flip(both[r], "dp", 2 * r) for r in range(1, both.shape[0])]


def shards(
    layer_input,
    encoder_memory,
    output_grad,
    target_lengths,
    memory_lengths,
    source_slots,
    pair_counts,
    attend_input,
    attend_output,
    expand_weight,
    reduce_weight,
    norm_vectors,
    expand_bias,
    attend_input_first,
    attend_input_second,
    attend_output_first,
    attend_output_second,
    expand_weight_first,
    expand_weight_second,
    reduce_weight_first,
    reduce_weight_second,
    norm_vectors_first,
    norm_vectors_second,
    expand_bias_first,
    expand_bias_second,
):
    data_count = lax.axis_size("dp")
    model_count = lax.axis_size("mp")
    me = lax.axis_index("dp")
    model = lax.axis_index("mp")
    tok_rows, width = layer_input.shape
    rows, columns = attend_input.shape[1:]
    units = expand_weight.shape[1]
    attend_output, attend_output_first, attend_output_second = [
        value.transpose(0, 2, 1) for value in (attend_output, attend_output_first, attend_output_second)
    ]
    reduce_weight, reduce_weight_first, reduce_weight_second = [
        value.T for value in (reduce_weight, reduce_weight_first, reduce_weight_second)
    ]
    weights = (attend_input, attend_output, expand_weight, reduce_weight, norm_vectors, expand_bias)

    extra_slots = tok_rows // 16
    slot_cap = (tok_rows - data_count // 4 * extra_slots) // data_count + extra_slots
    my_counts = lax.dynamic_index_in_dim(pair_counts, me, 0, keepdims=False)
    my_starts = jnp.cumsum(my_counts) - my_counts
    arrived = lax.all_to_all(
        pack_rows(encoder_memory, my_starts, slot_cap), "dp", split_axis=0, concat_axis=0, tiled=True
    )

    bias_rows = expand_bias.shape[0]
    vectors = jnp.concatenate(
        [
            jnp.pad(norm_vectors, ((0, 0), (0, columns - rows))),
            jnp.pad(expand_bias[None], ((0, 0), (0, columns - bias_rows))),
        ],
        axis=0,
    )
    own_self = jnp.concatenate(
        [attend_input[:3].reshape(3 * rows, columns), attend_output[0], vectors], axis=0
    )
    own_cross = jnp.concatenate(
        [attend_input[3:].reshape(3 * rows, columns), attend_output[1], vectors], axis=0
    )
    own_wide = jnp.concatenate([expand_weight, reduce_weight], axis=0)
    index = jnp.stack([me, model])
    together = lax.optimization_barrier
    memory_own = unpack_rows(arrived.reshape(data_count * slot_cap, columns), source_slots)
    self_ring, own_cross, memory_own, own_wide = together(
        (ring_gather(own_self), own_cross, memory_own, own_wide)
    )
    all_wide = lax.all_gather(own_wide, ("dp", "mp"))
    memory_ring = ring_gather(memory_own)
    self_even, cross_ring, memory_ring[1], memory_ring[-1] = together(
        (even_gather(jnp.stack(self_ring)), ring_gather(own_cross), memory_ring[1], memory_ring[-1])
    )
    self_pieces = odd_gather(self_even)
    cross_even = even_gather(jnp.stack(cross_ring))
    self_full, all_vectors = place(self_pieces, index, 4, rows, columns, bias_rows)
    all_wide = all_wide.reshape(data_count, model_count, 2 * rows, units)
    full_vectors = all_vectors[0]

    self_ranges = key_ranges(target_lengths[0], target_lengths[0], tok_rows)
    cross_ranges = key_ranges(target_lengths[0], memory_lengths[0], tok_rows)

    self_query = matmul(layer_input, self_full[0])
    self_key = matmul(layer_input, self_full[1])
    self_value = matmul(layer_input, self_full[2])
    self_out, self_totals = attend(self_query, self_key, self_value, self_ranges, HD)
    self_out, memory_ring, cross_even = together((self_out, memory_ring, cross_even))
    cross_full, _ = place(odd_gather(cross_even), index, 4, rows, columns, bias_rows)
    memory_target = jnp.concatenate(ring_order(memory_ring), axis=1)
    self_mix = matmul(self_out, self_full[3].T)
    first_sum = layer_input + self_mix
    first_norm = layer_norm(first_sum, full_vectors[0], full_vectors[3])
    cross_query = matmul(first_norm, cross_full[0])
    cross_key = matmul(memory_target, cross_full[1])
    cross_value = matmul(memory_target, cross_full[2])
    cross_out, cross_totals = attend(cross_query, cross_key, cross_value, cross_ranges, HD)
    cross_mix = matmul(cross_out, cross_full[3].T)
    second_sum = first_norm + cross_mix
    second_norm = layer_norm(second_sum, full_vectors[1], full_vectors[4])
    layer_output, second_grad, grad_wide, wide_sums, grad_bias = feed_forward(
        model,
        second_norm,
        output_grad,
        all_wide,
        all_vectors,
        rows,
    )

    grad_wide = lax.psum_scatter(
        grad_wide.reshape(data_count, rows, 2 * units), "dp", scatter_dimension=0, tiled=False
    )
    keep, send, resid_one_grad, memory_grad_own = cross_back(
        index,
        cross_ranges,
        second_grad,
        second_sum,
        first_sum,
        memory_target,
        cross_query,
        cross_key,
        cross_value,
        cross_out,
        cross_totals,
        cross_full,
        all_vectors,
        wide_sums,
        grad_bias,
        HD,
        columns,
        rows,
        bias_rows,
    )
    placed = place_back(memory_grad_own, source_slots, data_count * slot_cap)
    resid_one_grad, placed, both = together((resid_one_grad, placed, keep + flip(send, "dp", 1)))
    returned = lax.all_to_all(
        placed.reshape(data_count, slot_cap, columns), "dp", split_axis=0, concat_axis=0, tiled=True
    )
    grad_cross = cube_scatter(both)
    keep, send, self_query_grad, self_key_grad, self_value_grad = self_back(
        index,
        self_ranges,
        resid_one_grad,
        layer_input,
        self_query,
        self_key,
        self_value,
        self_out,
        self_totals,
        self_full,
        HD,
        columns,
        rows,
    )
    keep, send, returned, grad_cross = together((keep, send, returned, grad_cross))
    grad_self = cube_scatter(keep + flip(send, "dp", 1))
    memory_grad = return_rows(returned, my_starts, tok_rows)
    input_grad = (
        resid_one_grad
        + matmul(self_query_grad, self_full[0].T)
        + matmul(self_key_grad, self_full[1].T)
        + matmul(self_value_grad, self_full[2].T)
    )

    weights = weights[:5] + (expand_bias[None],)
    firsts = (
        attend_input_first,
        attend_output_first,
        expand_weight_first,
        reduce_weight_first,
        norm_vectors_first,
        expand_bias_first[None],
    )
    seconds = (
        attend_input_second,
        attend_output_second,
        expand_weight_second,
        reduce_weight_second,
        norm_vectors_second,
        expand_bias_second[None],
    )
    row_shape = jax.ShapeDtypeStruct((1, 128), f32)
    grad_self, grad_cross, grad_vectors, row = whole_call(
        functools.partial(squares_kernel, model_count, len(grad_self)),
        "squares",
        same(grad_self[:1] * 2) + (jax.ShapeDtypeStruct((8, rows), f32), row_shape),
        *grad_self,
        *grad_cross,
        grad_wide,
        *weights,
    )
    row, input_grad = together((small_total(row), input_grad))
    moved = whole_call(
        functools.partial(moments_kernel, model_count, columns),
        "moments",
        same(weights) * 3 + (row_shape,),
        row,
        grad_self,
        grad_cross,
        grad_wide,
        grad_vectors,
        *weights,
        *firsts,
        *seconds,
    )
    new_firsts, new_seconds, updates = moved[:6], moved[6:12], moved[12:18]
    applied = whole_call(
        apply_kernel,
        "apply",
        same(weights)
        + same(weights[:4], bf16)
        + (jax.ShapeDtypeStruct((2, 128), f32), jax.ShapeDtypeStruct((1, 1), f32)),
        row,
        small_total(moved[18]),
        *weights,
        *updates,
    )
    new_weights = applied[:5] + (applied[5][0],)
    matrix_norms = applied[10][:, :10]

    def turned(values):
        return (values[0], values[1].transpose(0, 2, 1), values[2], values[3].T) + tuple(values[4:])

    new_weights, copies = turned(new_weights), turned(applied[6:10])
    new_firsts, new_seconds = turned(new_firsts), turned(new_seconds)
    return (
        layer_output,
        input_grad,
        memory_grad,
        applied[11][0],
        *new_weights,
        *copies,
        new_firsts[0],
        new_seconds[0],
        new_firsts[1],
        new_seconds[1],
        new_firsts[2],
        new_seconds[2],
        new_firsts[3],
        new_seconds[3],
        new_firsts[4],
        new_seconds[4],
        new_firsts[5][0],
        new_seconds[5][0],
        matrix_norms,
    )


def solution(mesh):
    in_specs = (
        P("dp", None),
        P("dp", "mp"),
        P("dp", None),
        P("dp", None),
        P("dp", None),
        P("dp"),
        P(),
        P(None, "dp", "mp"),
        P(None, "mp", "dp"),
        P("dp", "mp"),
        P("mp", "dp"),
        P(None, "dp"),
        P(("mp", "dp")),
        P(None, "dp", "mp"),
        P(None, "dp", "mp"),
        P(None, "mp", "dp"),
        P(None, "mp", "dp"),
        P("dp", "mp"),
        P("dp", "mp"),
        P("mp", "dp"),
        P("mp", "dp"),
        P(None, "dp"),
        P(None, "dp"),
        P(("mp", "dp")),
        P(("mp", "dp")),
    )
    out_specs = (
        P("dp", None),
        P("dp", None),
        P("dp", "mp"),
        P(),
        P(None, "dp", "mp"),
        P(None, "mp", "dp"),
        P("dp", "mp"),
        P("mp", "dp"),
        P(None, "dp"),
        P(("mp", "dp")),
        P(None, "dp", "mp"),
        P(None, "mp", "dp"),
        P("dp", "mp"),
        P("mp", "dp"),
        P(None, "dp", "mp"),
        P(None, "dp", "mp"),
        P(None, "mp", "dp"),
        P(None, "mp", "dp"),
        P("dp", "mp"),
        P("dp", "mp"),
        P("mp", "dp"),
        P("mp", "dp"),
        P(None, "dp"),
        P(None, "dp"),
        P(("mp", "dp")),
        P(("mp", "dp")),
        P(),
    )
    return jax.shard_map(shards, mesh=mesh, in_specs=in_specs, out_specs=out_specs, check_vma=False)
```
